32 devices in a mesh: head: 2 (over x), blk: 16 (over z, y, core).
Axes of the slice: x: 2, y: 2, z: 4, core: 2. Of those that a mesh axis runs over, the one named last changes fastest.
Arguments:
- tokens: bfloat16 [4, 2048, 1536], P('head', 'blk'), may hold values from -6 to 6
- gain_attn: bfloat16 [1536], P(('head', 'blk')), may hold values from 0.5 to 1.5
- w_query: bfloat16 [1536, 1536], P(('head', 'blk')), may hold values from -0.15625 to 0.15625
- w_key: bfloat16 [1536, 512], P(('head', 'blk')), may hold values from -0.15625 to 0.15625
- w_value: bfloat16 [1536, 512], P(('head', 'blk')), may hold values from -0.15625 to 0.15625
- w_out: bfloat16 [1536, 1536], P(('head', 'blk')), may hold values from -6 to 6
- gain_moe: bfloat16 [1536], P(('head', 'blk')), may hold values from 0.5 to 1.5
- w_router: bfloat16 [1536, 16], P(('head', 'blk')), may hold values from -0.15625 to 0.15625
- w_gate: bfloat16 [16, 1536, 512], P('blk'), may hold values from -0.15625 to 0.15625
- w_up: bfloat16 [16, 1536, 512], P('blk'), may hold values from -0.15625 to 0.15625
- w_down: bfloat16 [16, 512, 1536], P('blk'), may hold values from -0.75 to 0.75
- routes: int32 [4, 2048, 8], P('head', 'blk'), may hold values from 0 to 15, all different within a row; in each aligned block of 128 rows (0 to 127, 128 to 255, ..., all dimensions but the last counted through in order) at most 96 rows name the same one
- grad_out: float32 [4, 2048, 1536], P('head', 'blk'), may hold values from -6 to 6
Outputs:
- out: float32 [4, 2048, 1536], P('head', 'blk')
- grad_tokens: float32 [4, 2048, 1536], P('head', 'blk')
- grad_gain_attn: float32 [1536], P(('head', 'blk'))
- grad_w_query: float32 [1536, 1536], P(('head', 'blk'))
- grad_w_key: float32 [1536, 512], P(('head', 'blk'))
- grad_w_value: float32 [1536, 512], P(('head', 'blk'))
- grad_w_out: float32 [1536, 1536], P(('head', 'blk'))
- grad_gain_moe: float32 [1536], P(('head', 'blk'))
- grad_w_router: float32 [1536, 16], P(('head', 'blk'))
- grad_w_gate: float32 [16, 1536, 512], P('blk')
- grad_w_up: float32 [16, 1536, 512], P('blk')
- grad_w_down: float32 [16, 512, 1536], P('blk')
The draws below stay inside these ranges and needn't reach their ends.
Inputs may be any that keep to these rules, and one draw needn't show every extreme that they name: `routes`: each token names 8 different experts. In each aligned block of 128 rows (the positions of one sequence on one device), no expert is named by more than 96 rows, and in some block one expert is named by exactly 96 rows.
All inputs are finite; a program needn't handle non-finite values.
Results may differ from the reference program's by a relative error of at most 0.02.
Values may be sent and summed in bfloat16 or wider, within the bound.
No kernel may reach another device: no remote copies, remote signals or barrier semaphores. Data moves between devices by JAX's collectives and lax.ppermute only.
A program may use at most 320 MiB of HBM per device.

```python
import math
from functools import partial
import jax
import jax.numpy as jnp
import numpy as np
from jax import lax

D = 1536
HEADS = 24
KVH = 8
HDIM = 64
EFF = 512
TOP = 8
BLOCK = 256
SHARD = 128
SEQS = 4
SEQ = 2048
EXPERTS = 16
MOST = 96


def levels(rng, extent, cuts, low, top_value):
    level = 1.0
    for dim, blocks in cuts:
        heights = jax.random.uniform(jax.random.fold_in(jax.random.fold_in(rng, 6), dim), (blocks,), jnp.float32, low / len(cuts), top_value / len(cuts))
        level = level * jnp.repeat(jnp.exp(heights), extent[dim] // blocks).reshape((-1,) + (1,) * (len(extent) - 1 - dim))
    return level


def assign_block(rng, own, number, rows, amount, top, most, skew):
    sequence = jax.random.permutation(rng, amount)
    crowded, usual = shares(amount, rows * top, most, skew, True), shares(amount, rows * top, most, skew, False)
    places = jnp.arange(amount)

    def named(tallies, rotation):
        used = int((tallies > 0).sum())
        fixed = max(1, used // 4)
        shifted = fixed + (places - fixed + rotation * (used - fixed)) % max(1, amount - fixed)
        return jnp.zeros((amount,), jnp.int32).at[sequence[jnp.where(places < fixed, places, shifted)]].set(jnp.asarray(tallies, jnp.int32))

    tallies = jnp.where(number % 4 == 0, named(crowded, number // 4), named(usual, number - number // 4 - 1))
    mixed = jax.random.permutation(jax.random.fold_in(own, 3), amount)
    giver, sink = mixed[0:amount // 2 * 2:2], mixed[1:amount // 2 * 2:2]
    room = jnp.minimum(tallies[giver] - 1, most - tallies[sink]) // 2
    room = jnp.where((giver == sequence[0]) | (sink == sequence[0]) | (tallies[sink] == 0), 0, jnp.maximum(room, 0))
    shifted = jax.random.randint(jax.random.fold_in(own, 4), (amount // 2,), 0, 1 << 20) % (room + 1)
    tallies = tallies.at[giver].add(-shifted).at[sink].add(shifted)
    labels = jnp.searchsorted(jnp.cumsum(tallies), jnp.arange(rows * top), side="right").astype(jnp.int32)
    listing = labels.reshape(top, rows).T
    listing = listing[jax.random.permutation(jax.random.fold_in(own, 1), rows)]
    rotation = jax.random.randint(jax.random.fold_in(own, 2), (rows, 1), 0, top)
    return jnp.take_along_axis(listing, (jnp.arange(top)[None, :] + rotation) % top, axis=1)


def shares(number_of, total, reach, lean, full):
    loads = [(1 << 20) // math.isqrt(rank ** lean) + 1 for rank in range(1, number_of + 1)]
    largest = reach if full else min(reach, max(-(-total // number_of), total * loads[0] // sum(loads)))
    least = 1 if total - largest >= number_of - 1 else 0
    given, spare = [largest] + [least] * (number_of - 1), total - largest - least * (number_of - 1)
    while spare > 0:
        movable = [i for i in range(1, number_of) if given[i] < largest] or [i for i in range(1, number_of) if given[i] < reach]
        mass, left = sum([loads[i] for i in movable]), spare
        for i in movable:
            more = min(reach - given[i], max(1, left * loads[i] // mass), spare)
            given[i] = given[i] + more
            spare = spare - more
    return np.array(given)


def centred(rng, dims, scale, most, split=(), kind=jnp.bfloat16):
    loudness = levels(rng, dims, split, -0.22, 0.18) if split else 1.0
    entries = jax.random.normal(rng, dims, jnp.float32) * scale * loudness
    return jnp.minimum(jnp.maximum(entries, -most), most).astype(kind)


def setup_inputs(seed: int = 0) -> dict:
    seeds = jax.random.split(jax.random.key(seed), 14)
    tokens = centred(seeds[0], (SEQS, SEQ, D), 1.0, 6.0, ((0, 2), (1, 16)))
    gain_attn = jnp.clip(1.0 + 0.1 * jax.random.normal(seeds[1], (D,), jnp.float32), 0.5, 1.5).astype(jnp.bfloat16)
    w_query = centred(seeds[2], (D, HEADS * HDIM), D ** -0.5, 0.15625, ((0, 32),))
    w_key = centred(seeds[3], (D, KVH * HDIM), D ** -0.5, 0.15625, ((0, 32),))
    w_value = centred(seeds[4], (D, KVH * HDIM), D ** -0.5, 0.15625, ((0, 32),))
    w_out = centred(seeds[5], (HEADS * HDIM, D), ((SEQ // 8) ** 0.5 * (HEADS * HDIM) ** -0.5), 6.0, ((0, 32),))
    gain_moe = jnp.clip(1.0 + 0.1 * jax.random.normal(seeds[6], (D,), jnp.float32), 0.5, 1.5).astype(jnp.bfloat16)
    w_router = centred(seeds[7], (D, EXPERTS), D ** -0.5, 0.15625, ((0, 32),))
    w_gate = centred(seeds[8], (EXPERTS, D, EFF), D ** -0.5, 0.15625, ((0, 16),))
    w_up = centred(seeds[9], (EXPERTS, D, EFF), D ** -0.5, 0.15625, ((0, 16),))
    w_down = centred(seeds[10], (EXPERTS, EFF, D), (EFF // 8) ** -0.5, 0.75, ((0, 16),))
    routes_keys = jax.random.split(jax.random.fold_in(seeds[11], 1), SEQS * SEQ // SHARD)
    routes_turns = jax.random.permutation(jax.random.fold_in(seeds[11], 3), SEQS * SEQ // SHARD)
    routes = jax.vmap(lambda own, number: assign_block(jax.random.fold_in(seeds[11], 2), own, number, SHARD, EXPERTS, TOP, MOST, 1))(routes_keys, routes_turns).reshape((SEQS, SEQ, TOP))
    grad_out = centred(seeds[12], (SEQS, SEQ, D), 1.0, 6.0, ((0, 2), (1, 16)), jnp.float32)
    return dict(tokens=tokens, gain_attn=gain_attn, w_query=w_query, w_key=w_key, w_value=w_value, w_out=w_out, gain_moe=gain_moe, w_router=w_router, w_gate=w_gate, w_up=w_up, w_down=w_down, routes=routes, grad_out=grad_out)


@jax.custom_vjp
def low(v):
    return lax.optimization_barrier(v.astype(jnp.bfloat16)).astype(jnp.float32)

@jax.custom_vjp
def low_back(v):
    return v

def low_keep(v):
    return (low(v), None)

def low_pass(kept, grad):
    return (grad,)

def back_keep(v):
    return (v, None)

def back_low(kept, grad):
    return (low(grad),)
low.defvjp(low_keep, low_pass)
low_back.defvjp(back_keep, back_low)
highest = lax.Precision.HIGHEST
theta_base = 10000.0
norm_eps = 1e-06
masked_score = -1e+30

def rope_tables(positions, half_width):
    index_float = jnp.arange(half_width, dtype=jnp.float32)
    frequency = theta_base ** (-2.0 * index_float / (2 * half_width))
    angles = positions.astype(jnp.float32)[:, None] * frequency[None, :]
    return (jnp.cos(angles), jnp.sin(angles))

def rotate(values, cosine, sine):
    half_width = values.shape[-1] // 2
    first_half = values[..., :half_width]
    second_half = values[..., half_width:]
    cosine = cosine[:, None, :]
    sine = sine[:, None, :]
    return jnp.concatenate([first_half * cosine - second_half * sine, second_half * cosine + first_half * sine], axis=-1)

def rms_norm(values, gain):
    return values * lax.rsqrt(lax.optimization_barrier(jnp.mean(values * values, axis=-1, keepdims=True)) + norm_eps) * gain

def attend_pair(queries, keys, values, allowed):
    scores = jnp.einsum('igd,kd->gik', queries, keys, precision=highest) * HDIM ** (-0.5)
    scores = jnp.where(allowed[None], low_back(scores), masked_score)
    weights = low(jax.nn.softmax(scores, axis=-1))
    return jnp.einsum('gik,kd->igd', weights, values, precision=highest)

def expert_rows(table_row, gate_row, weight_gate, weight_up, weight_down, padded):
    dispatched = low_back(padded[table_row])
    gate_lin = low_back(jnp.dot(dispatched, weight_gate, precision=highest))
    up_lin = low_back(jnp.dot(dispatched, weight_up, precision=highest))
    hidden = low(jax.nn.silu(gate_lin) * up_lin)
    produced = low_back(low(jnp.dot(hidden, weight_down, precision=highest)))
    return produced * gate_row[:, None]

def route_tables(flat_routes):
    count_all = flat_routes.shape[0]
    blocks = count_all // SHARD
    member = (flat_routes.reshape(blocks, SHARD * TOP)[:, :, None] == jnp.arange(EXPERTS, dtype=jnp.int32)[None, None, :]).astype(jnp.int32)
    ranks = lax.optimization_barrier(jnp.sum(member * (jnp.cumsum(member, axis=1) - 1), axis=-1)).astype(jnp.int32)
    slot_index = (jnp.arange(blocks, dtype=jnp.int32)[:, None] * MOST + ranks).reshape(-1)
    target = (flat_routes.reshape(-1) * (blocks * MOST) + slot_index).astype(jnp.int32)
    assign_ids = jnp.arange(count_all * TOP, dtype=jnp.int32)
    assign_table = jnp.full((EXPERTS * blocks * MOST,), count_all * TOP, jnp.int32).at[target].set(assign_ids)
    token_table = (assign_table // TOP).astype(jnp.int32)
    return (token_table.reshape(EXPERTS, blocks * MOST), assign_table.reshape(EXPERTS, blocks * MOST))

def layer(tokens, gain_attn, w_query, w_key, w_value, w_out, gain_moe, w_router, w_gate, w_up, w_down, routes):
    count_all = SEQS * SEQ
    group_size = HEADS // KVH
    normed = low(rms_norm(tokens, gain_attn)).reshape(count_all, D)
    cosine, sine = rope_tables(jnp.arange(SEQ, dtype=jnp.int32), HDIM // 2)
    lin_query = low_back(jnp.dot(normed, w_query, precision=highest)).reshape(SEQS, SEQ, HEADS, HDIM)
    lin_key = low_back(jnp.dot(normed, w_key, precision=highest)).reshape(SEQS, SEQ, KVH, HDIM)
    queries = low(rotate(lin_query, cosine, sine))
    keys = low(rotate(lin_key, cosine, sine))
    values = low(low_back(jnp.dot(normed, w_value, precision=highest))).reshape(SEQS, SEQ, KVH, HDIM)
    pair_query = queries.reshape(SEQS, SEQ, KVH, group_size, HDIM).transpose(0, 2, 1, 3, 4).reshape(SEQS * KVH, SEQ, group_size, HDIM)
    pair_key = keys.transpose(0, 2, 1, 3).reshape(SEQS * KVH, SEQ, HDIM)
    pair_value = values.transpose(0, 2, 1, 3).reshape(SEQS * KVH, SEQ, HDIM)
    block_of = jnp.arange(SEQ, dtype=jnp.int32) // BLOCK
    allowed = block_of[None, :] <= block_of[:, None]
    checked = jax.checkpoint(partial(attend_pair, allowed=allowed))

    def per_pair(grouped):
        return checked(grouped[0], grouped[1], grouped[2])
    attended = lax.map(per_pair, (pair_query, pair_key, pair_value))
    attended = attended.reshape(SEQS, KVH, SEQ, group_size, HDIM).transpose(0, 2, 1, 3, 4).reshape(count_all, HEADS * HDIM)
    attended = low_back(low(attended))
    branch = low_back(jnp.dot(attended, w_out, precision=highest))
    middle = tokens.reshape(count_all, D) + branch
    normed_two = low(rms_norm(middle, gain_moe))
    logits = jnp.dot(normed_two, w_router, precision=highest)
    flat_routes = routes.reshape(count_all, TOP)
    gates = jax.nn.softmax(jnp.take_along_axis(logits, flat_routes, axis=1), axis=-1)
    token_table, assign_table = route_tables(flat_routes)
    gate_pad = jnp.concatenate([gates.reshape(-1), jnp.zeros((1,), jnp.float32)])
    gate_slots = gate_pad[assign_table]
    padded = jnp.concatenate([normed_two, jnp.zeros((1, D), jnp.float32)], axis=0)
    checked_expert = jax.checkpoint(expert_rows)

    def per_expert(grouped):
        return checked_expert(grouped[0], grouped[1], grouped[2], grouped[3], grouped[4], padded)
    produced = lax.map(per_expert, (token_table, gate_slots, w_gate, w_up, w_down))
    mixed = jnp.zeros((count_all + 1, D), jnp.float32).at[token_table.reshape(-1)].add(produced.reshape(-1, D))[:count_all]
    return (middle + mixed).reshape(SEQS, SEQ, D)

def reference(tokens, gain_attn, w_query, w_key, w_value, w_out, gain_moe, w_router, w_gate, w_up, w_down, routes, grad_out):
    floats = tuple((array_in.astype(jnp.float32) for array_in in (tokens, gain_attn, w_query, w_key, w_value, w_out, gain_moe, w_router, w_gate, w_up, w_down)))

    def closed(*params):
        return layer(*params, routes)
    result, pull = jax.vjp(closed, *floats)
    grads = pull(grad_out.astype(jnp.float32))
    return (result, grads[0], grads[1], grads[2], grads[3], grads[4], grads[5], grads[6], grads[7], grads[8], grads[9], grads[10])
```

```python
import functools

import jax
import jax.numpy as jnp
from jax import lax
from jax.experimental import pallas as pl
from jax.experimental.pallas import tpu as pltpu
from jax.sharding import PartitionSpec as P

HDIM = 64
TOP = 8
BLOCK = 256
LANES = 128

highest = lax.Precision.HIGHEST
theta_base = 10000.0
norm_eps = 1e-06


def rope_tables(positions, half_width):
    index_float = jnp.arange(half_width, dtype=jnp.float32)
    frequency = theta_base ** (-2.0 * index_float / (2 * half_width))
    angles = positions.astype(jnp.float32)[:, None] * frequency[None, :]
    return (jnp.cos(angles), jnp.sin(angles))


def rms_scale(values):
    return lax.rsqrt(jnp.mean(values * values, axis=-1, keepdims=True) + norm_eps)


def norm_back(values, inverse, gain, d_normed):
    unit_values = values * inverse
    scaled = d_normed * gain
    d_gain = jnp.sum(d_normed * unit_values, axis=0)
    d_values = inverse * (
        scaled - unit_values * jnp.mean(scaled * unit_values, axis=-1, keepdims=True)
    )
    return (d_values, d_gain)


def matmul(left, right):
    return jnp.dot(left, right, preferred_element_type=jnp.float32)


def matmul_nt(left, right):
    return lax.dot_general(left, right, (((1,), (1,)), ((), ())), preferred_element_type=jnp.float32)


def matmul_tn(left, right):
    return lax.dot_general(left, right, (((0,), (0,)), ((), ())), preferred_element_type=jnp.float32)


def wide(block, group):
    flipped = block.T
    return jnp.concatenate([flipped[h*HDIM:(h+1)*HDIM] for h in range(group)], axis=1)

def tall(block, group):
    return jnp.concatenate([block[:, h*HDIM:(h+1)*HDIM] for h in range(group)], axis=0)

def narrow(values, group, rows):
    return jnp.concatenate([values[:, h*rows:(h+1)*rows] for h in range(group)], axis=0).T

def forward_kernel(group, qkv_ref, att_ref, flat_ref, lse_ref, key_sc, val_sc, acc_sc):
    i = pl.program_id(0)
    lanes = group*HDIM
    @pl.when(i == 0)
    def _():
        key_sc[...] = qkv_ref[:, lanes:lanes+HDIM]
        val_sc[...] = qkv_ref[:, lanes+HDIM:lanes+2*HDIM].T
    rows = pl.ds(pl.multiple_of(i*BLOCK, BLOCK), BLOCK)
    query = wide(qkv_ref[rows, :lanes], group) * jnp.bfloat16(HDIM**-0.5)
    acc_sc[...] = jnp.zeros_like(acc_sc)
    def step(j, carry):
        top, total = carry
        here = pl.ds(pl.multiple_of(j*BLOCK, BLOCK), BLOCK)
        scores = jnp.dot(key_sc[here, :], query, preferred_element_type=jnp.float32)
        new_top = jnp.maximum(top, jnp.max(scores, axis=0, keepdims=True))
        probs = jnp.exp(scores - new_top)
        fade = jnp.exp(top - new_top)
        acc_sc[...] = acc_sc[...]*fade + jnp.dot(val_sc[:, here], probs.astype(jnp.bfloat16), preferred_element_type=jnp.float32)
        return new_top, total*fade + jnp.sum(probs, axis=0, keepdims=True)
    width = group*BLOCK
    top, total = lax.fori_loop(0, i+1, step, (jnp.full((1,width), -1e30, jnp.float32), jnp.zeros((1,width), jnp.float32)))
    result = acc_sc[...] / total
    flat_ref[0] = result
    att_ref[...] = narrow(result.astype(jnp.bfloat16), group, BLOCK)
    lse_ref[0] = top + jnp.log(total)

def attend_forward(qkv, group):
    total = qkv.shape[0]; steps = total//BLOCK; lanes = group*HDIM; width = group*BLOCK
    return pl.pallas_call(
        functools.partial(forward_kernel, group),
        grid=(steps,),
        in_specs=[pl.BlockSpec((total, lanes+2*HDIM), lambda i: (0,0))],
        out_specs=[pl.BlockSpec((BLOCK, lanes), lambda i: (i,0)),
                   pl.BlockSpec((1, HDIM, width), lambda i: (i,0,0)),
                   pl.BlockSpec((1,1,width), lambda i: (i,0,0))],
        out_shape=[jax.ShapeDtypeStruct((total, lanes), jnp.bfloat16),
                   jax.ShapeDtypeStruct((steps,HDIM,width), jnp.float32),
                   jax.ShapeDtypeStruct((steps,1,width), jnp.float32)],
        scratch_shapes=[pltpu.VMEM((total,HDIM), jnp.bfloat16), pltpu.VMEM((HDIM,total), jnp.bfloat16), pltpu.VMEM((HDIM,width), jnp.float32)],
        compiler_params=pltpu.CompilerParams(dimension_semantics=("arbitrary",)),
        name="attend_forward",
    )(qkv)

def unrotate(values, cosine, sine):
    a, b = values[:HDIM//2], values[HDIM//2:]
    return jnp.concatenate([a*cosine + b*sine, b*cosine - a*sine], axis=0)

def backward_kernel(group, steps, qkv_ref, grad_ref, flat_ref, lse_ref, cos_ref, sin_ref, out_ref, key_sc, keyt_sc, val_sc, dq_sc, dk_sc, dv_sc):
    i = pl.program_id(0)
    lanes = group*HDIM
    scale = HDIM**-0.5
    @pl.when(i == 0)
    def _():
        key = qkv_ref[:, lanes:lanes+HDIM]
        key_sc[...] = key
        keyt_sc[...] = key.T
        val_sc[...] = qkv_ref[:, lanes+HDIM:lanes+2*HDIM]
        dk_sc[...] = jnp.zeros_like(dk_sc)
        dv_sc[...] = jnp.zeros_like(dv_sc)
    rows = pl.ds(pl.multiple_of(i*BLOCK, BLOCK), BLOCK)
    block = qkv_ref[rows, :lanes] * jnp.bfloat16(scale)
    query_w, query_t = wide(block, group), tall(block, group)
    grad = grad_ref[...]
    grad_w, grad_t = wide(grad, group), tall(grad, group)
    lse = lse_ref[0]
    delta = jnp.sum(grad_w.astype(jnp.float32)*flat_ref[0], axis=0, keepdims=True)
    dq_sc[...] = jnp.zeros_like(dq_sc)
    def step(j, carry):
        here = pl.ds(pl.multiple_of(j*BLOCK, BLOCK), BLOCK)
        scores = jnp.dot(key_sc[here,:], query_w, preferred_element_type=jnp.float32)
        probs = jnp.exp(scores - lse)
        dprobs = jnp.dot(val_sc[here,:], grad_w, preferred_element_type=jnp.float32)
        dv_sc[here,:] += jnp.dot(probs.astype(jnp.bfloat16), grad_t, preferred_element_type=jnp.float32)
        dscores = (probs*(dprobs-delta)).astype(jnp.bfloat16)
        dk_sc[here,:] += jnp.dot(dscores, query_t, preferred_element_type=jnp.float32)
        dq_sc[...] += jnp.dot(keyt_sc[:,here], dscores, preferred_element_type=jnp.float32)
        return carry
    lax.fori_loop(0, i+1, step, 0)
    cosine, sine = cos_ref[:, rows], sin_ref[:, rows]
    pieces = [unrotate(dq_sc[:, h*BLOCK:(h+1)*BLOCK]*scale, cosine, sine).astype(jnp.bfloat16) for h in range(group)]
    out_ref[rows, :lanes] = jnp.concatenate(pieces, axis=0).T
    @pl.when(i == steps-1)
    def _():
        def finish(j, carry):
            here = pl.ds(pl.multiple_of(j*BLOCK, BLOCK), BLOCK)
            turned = unrotate(dk_sc[here,:].T, cos_ref[:,here], sin_ref[:,here]).astype(jnp.bfloat16)
            both = jnp.concatenate([turned, dv_sc[here,:].astype(jnp.bfloat16).T], axis=0).T
            out_ref[here, lanes:lanes+2*HDIM] = both
            return carry
        lax.fori_loop(0, steps, finish, 0)

def attend_backward(qkv, grad, flat, lse, cosine, sine, group):
    total = qkv.shape[0]; steps = total//BLOCK; lanes = group*HDIM; width = group*BLOCK
    return pl.pallas_call(
        functools.partial(backward_kernel, group, steps),
        grid=(steps,),
        in_specs=[pl.BlockSpec((total, lanes+2*HDIM), lambda i: (0,0)),
                  pl.BlockSpec((BLOCK, lanes), lambda i: (i,0)),
                  pl.BlockSpec((1, HDIM, width), lambda i: (i,0,0)),
                  pl.BlockSpec((1,1,width), lambda i: (i,0,0)),
                  pl.BlockSpec((HDIM//2, total), lambda i: (0,0)),
                  pl.BlockSpec((HDIM//2, total), lambda i: (0,0))],
        out_specs=pl.BlockSpec((total, lanes+2*HDIM), lambda i: (0,0)),
        out_shape=jax.ShapeDtypeStruct((total, lanes+2*HDIM), jnp.bfloat16),
        scratch_shapes=[pltpu.VMEM((total,HDIM), jnp.bfloat16), pltpu.VMEM((HDIM,total), jnp.bfloat16), pltpu.VMEM((total,HDIM), jnp.bfloat16),
                        pltpu.VMEM((HDIM,width), jnp.float32), pltpu.VMEM((total,HDIM), jnp.float32), pltpu.VMEM((total,HDIM), jnp.float32)],
        compiler_params=pltpu.CompilerParams(dimension_semantics=("arbitrary",)),
        name="attend_backward",
    )(qkv, grad, flat, lse, cosine, sine)

def expert_kernel(
    parts, rows, width, experts, steps, chained, index_ref, *refs
):
    blocks = refs[:parts]
    grads = refs[parts : 2 * parts]
    router_ref, gate_ref, up_ref, down_ref = refs[2 * parts : 2 * parts + 4]
    refs = refs[2 * parts + 4 + (5 if chained else 0) :]
    mixed_ref, back_ref, rows_ref, grads_ref, d_gate_ref, d_up_ref, hidden_ref = refs[:7]
    gates_sc, d_gates_sc, mixed_sc, back_sc = refs[7:]
    step = pl.program_id(0)
    lane = lax.broadcasted_iota(jnp.int32, (rows, LANES), 1)

    @pl.when(step == 0)
    def _():
        part = rows // parts
        for k in range(parts):
            here = pl.ds(k * part, part)
            rows_ref[here, :] = blocks[k][...]
            grads_ref[here, :] = grads[k][:, :width]
            logits = jnp.dot(blocks[k][...], router_ref[...], preferred_element_type=jnp.float32)
            logits = jnp.where(grads[k][:, width:].astype(jnp.float32) > 0.5, logits, -1e30)
            weight = jnp.exp(logits - jnp.max(logits, axis=1, keepdims=True))
            gates_sc[here, :] = weight / jnp.sum(weight, axis=1, keepdims=True)
        d_gates_sc[...] = jnp.zeros_like(d_gates_sc)

    expert = index_ref[step * 2 // steps]
    own = lane == expert
    gate = jnp.sum(jnp.where(own, gates_sc[...], 0.0), axis=1, keepdims=True)
    block = rows_ref[...]
    gate_lin = jnp.dot(block, gate_ref[0], preferred_element_type=jnp.float32)
    up_lin = jnp.dot(block, up_ref[0], preferred_element_type=jnp.float32)
    d_hidden = matmul_nt(grads_ref[...], down_ref[0])
    sigma = 1.0 / (1.0 + jnp.exp(-gate_lin))
    active = gate_lin * sigma
    hidden = active * up_lin
    d_gates_sc[...] += jnp.where(own, jnp.sum(hidden * d_hidden, axis=1, keepdims=True), 0.0)
    hidden = (gate * hidden).astype(jnp.bfloat16)
    d_hidden = gate * d_hidden
    d_gate = (d_hidden * up_lin * sigma * (1.0 + gate_lin * (1.0 - sigma))).astype(jnp.bfloat16)
    d_up = (d_hidden * active).astype(jnp.bfloat16)
    hidden_ref[...] = hidden
    d_gate_ref[...] = d_gate
    d_up_ref[...] = d_up
    mixed = jnp.dot(hidden, down_ref[0], preferred_element_type=jnp.float32)
    back = matmul_nt(d_gate, gate_ref[0]) + matmul_nt(d_up, up_ref[0])

    @pl.when(step == 0)
    def _():
        mixed_sc[...] = mixed
        back_sc[...] = back

    @pl.when(step > 0)
    def _():
        mixed_sc[...] += mixed
        back_sc[...] += back

    @pl.when(step == steps - 1)
    def _():
        mixed_ref[...] = mixed_sc[...].astype(jnp.bfloat16)
        back_ref[:, :width] = back_sc[...].astype(jnp.bfloat16)
        d_gates = d_gates_sc[...]
        high = d_gates.astype(jnp.bfloat16).astype(jnp.float32)
        low = pltpu.roll(d_gates - high, experts, 1)
        back_ref[:, width:] = jnp.where(lane < experts, high, low).astype(jnp.bfloat16)


def expert_rows(index, experts, blocks, grads, router, gate, up, down, slot, total, buffers):
    parts = len(blocks)
    part, width = blocks[0].shape
    rows = parts * part
    units = gate.shape[2]
    tile = 256
    tiles = units // tile
    steps = 2 * tiles
    whole = lambda *shape: pl.BlockSpec(shape, lambda i, ids: (0,) * len(shape))
    activation = pl.BlockSpec((rows, tile), lambda i, ids: (slot, i))
    kept = pl.BlockSpec((rows, width), lambda i, ids: (slot, 0))
    chained = buffers is not None
    shapes = [
        jax.ShapeDtypeStruct((rows, width), jnp.bfloat16),
        jax.ShapeDtypeStruct((rows, width + LANES), jnp.bfloat16),
        jax.ShapeDtypeStruct((total, width), jnp.bfloat16),
        jax.ShapeDtypeStruct((total, width), jnp.bfloat16),
    ] + [jax.ShapeDtypeStruct((total, 2 * units), jnp.bfloat16)] * 3
    inputs = [index, *blocks, *grads, router, gate, up, down] + (list(buffers) if chained else [])
    first = 1 + 2 * parts + 4
    return pl.pallas_call(
        functools.partial(expert_kernel, parts, rows, width, experts, steps, chained),
        grid_spec=pltpu.PrefetchScalarGridSpec(
            num_scalar_prefetch=1,
            grid=(steps,),
            in_specs=[whole(part, width)] * parts
            + [whole(part, width + LANES)] * parts
            + [
                whole(width, LANES),
                pl.BlockSpec((1, width, tile), lambda i, ids: (i // tiles, 0, i % tiles)),
                pl.BlockSpec((1, width, tile), lambda i, ids: (i // tiles, 0, i % tiles)),
                pl.BlockSpec((1, tile, width), lambda i, ids: (i // tiles, i % tiles, 0)),
            ]
            + ([pl.BlockSpec(memory_space=pl.ANY)] * 5 if chained else []),
            out_specs=[
                whole(rows, width),
                whole(rows, width + LANES),
                kept,
                kept,
                activation,
                activation,
                activation,
            ],
            scratch_shapes=[
                pltpu.VMEM((rows, LANES), jnp.float32),
                pltpu.VMEM((rows, LANES), jnp.float32),
                pltpu.VMEM((rows, width), jnp.float32),
                pltpu.VMEM((rows, width), jnp.float32),
            ],
        ),
        out_shape=shapes,
        input_output_aliases={first + k: 2 + k for k in range(5)} if chained else {},
        compiler_params=pltpu.CompilerParams(dimension_semantics=("arbitrary",)),
        cost_estimate=pl.CostEstimate(
            flops=rows * width * units * 24,
            bytes_accessed=12 * width * units + 20 * rows * width,
            transcendentals=rows * units * 2,
        ),
        name="expert_rows",
    )(*inputs)


def gather_dense(values):
    return lax.all_gather(values, ("head", "blk"), axis=0, tiled=True)


def scatter_dense(values):
    return lax.psum_scatter(
        values.astype(jnp.bfloat16), ("head", "blk"), scatter_dimension=0, tiled=True
    ).astype(jnp.float32)


def exchange(values):
    return lax.all_to_all(values, "blk", split_axis=0, concat_axis=0, tiled=True)


def sum_heads(values):
    if lax.axis_size("head") == 2:
        other = lax.ppermute(values, "head", [(0, 1), (1, 0)])
        return values.astype(jnp.float32) + other.astype(jnp.float32)
    return lax.psum(values, "head").astype(jnp.float32)


def partner(values):
    count = lax.axis_size("blk")
    return lax.ppermute(values, "blk", [(k, k ^ 1) for k in range(count)])


def ring_steps():
    count = lax.axis_size("blk")
    half = count // 4
    order = [2 * k for k in range(half)] + [2 * k + 1 for k in reversed(range(half))]
    onward, back = [], []
    for place, chip in enumerate(order):
        following = order[(place + 1) % len(order)]
        for core in range(2):
            onward.append((2 * chip + core, 2 * following + core))
            back.append((2 * following + core, 2 * chip + core))
    send_on = lambda values: lax.ppermute(values, "blk", onward)
    send_back = lambda values: lax.ppermute(values, "blk", back)
    return len(order), send_on, send_back


def ring_gather(values):
    length, send_on, send_back = ring_steps()
    half = values.shape[0] // 2
    behind = ahead = values
    pairs = []
    for _ in range(length // 2 - 1):
        behind, ahead = send_on(behind), send_back(ahead)
        pairs.append((behind, ahead))
    return pairs, (send_on(behind[:half]), send_back(ahead[half:]))


def ring_scatter(own, pairs, opposite):
    length, send_on, send_back = ring_steps()
    half = own.shape[0] // 2
    onward, back = send_on(opposite[:half]), send_back(opposite[half:])
    onward = jnp.pad(onward, ((0, half), (0, 0)))
    back = jnp.pad(back, ((half, 0), (0, 0)))
    for behind, ahead in reversed(pairs):
        onward = send_on(onward + ahead)
        back = send_back(back + behind)
    wide = own.astype(jnp.float32)
    return wide + onward.astype(jnp.float32) + back.astype(jnp.float32)


def with_lanes(values, extra):
    rows = values.shape[0]
    spare = jnp.zeros((rows, LANES - extra.shape[1]), values.dtype)
    return jnp.concatenate([values, extra.astype(values.dtype), spare], axis=1)


def add_lanes(padded, extra):
    rows, columns = padded.shape
    spread = ((0, 0), (columns - LANES, LANES - extra.shape[1]))
    return padded + jnp.pad(extra, spread)


def local(
    tokens,
    gain_attn,
    w_query,
    w_key,
    w_value,
    w_out,
    gain_moe,
    w_router,
    w_gate,
    w_up,
    w_down,
    routes,
    grad_out,
):
    seq_local, shard, width = tokens.shape
    token_rows = seq_local * shard
    blk_index = lax.axis_index("blk")
    blk_count = lax.axis_size("blk")
    seq_total = blk_count * shard
    part_rows = w_query.shape[0]
    groups = w_key.shape[1] // HDIM
    group = w_query.shape[1] // w_key.shape[1]
    lanes = group * HDIM
    span = lanes + 2 * HDIM
    pairs = seq_local * groups
    copies = blk_count // pairs
    experts = w_router.shape[1]
    units = w_gate.shape[2]

    mixed_weights = jnp.concatenate(
        [
            w_query.reshape(part_rows, groups, lanes),
            w_key.reshape(part_rows, groups, HDIM),
            w_value.reshape(part_rows, groups, HDIM),
        ],
        axis=2,
    ).reshape(part_rows, groups * span)
    full_mixed = gather_dense(with_lanes(mixed_weights, gain_attn[:, None]))
    full_out = gather_dense(
        with_lanes(w_out, jnp.concatenate([w_router, gain_moe[:, None]], axis=1))
    )
    router = full_out[:, width:]
    full_router = router[:, :experts]
    router = jnp.where(jnp.arange(LANES)[None, :] < experts, router, jnp.bfloat16(0.0))
    gain_first = full_mixed[:, groups * span].astype(jnp.float32)
    gain_second = full_out[:, width + experts].astype(jnp.float32)

    expert_ids = jnp.arange(experts, dtype=jnp.int32)
    routes_tok = routes.reshape(token_rows, TOP)
    chosen = jnp.any(routes_tok[:, :, None] == expert_ids[None, None, :], axis=1)
    d_out = grad_out.reshape(token_rows, width)
    grads_own = with_lanes(d_out.astype(jnp.bfloat16), chosen)
    grads_pairs, grads_opposite = ring_gather(grads_own)
    both_gate = jnp.concatenate([w_gate, partner(w_gate)], axis=0)
    both_up = jnp.concatenate([w_up, partner(w_up)], axis=0)
    both_down = jnp.concatenate([w_down, partner(w_down)], axis=0)

    residual = tokens.astype(jnp.float32).reshape(token_rows, width)
    inverse_one = rms_scale(residual)
    normed = (residual * inverse_one * gain_first).astype(jnp.bfloat16)
    positions = blk_index * shard + jnp.arange(shard, dtype=jnp.int32)
    cosine, sine = rope_tables(positions, HDIM // 2)
    turned = (jnp.arange(groups * (group + 2)) % (group + 2) < group + 1)[None, None, :, None]
    cosine = jnp.where(turned, cosine[None, :, None, :], 1.0)
    sine = jnp.where(turned, sine[None, :, None, :], 0.0)
    linear = matmul(normed, full_mixed)[:, : groups * span].reshape(seq_local, shard, -1, HDIM)
    first, second = linear[..., : HDIM // 2], linear[..., HDIM // 2 :]
    packed = jnp.concatenate(
        [first * cosine - second * sine, second * cosine + first * sine], axis=-1
    ).astype(jnp.bfloat16)

    def to_pairs(values, columns):
        values = values.reshape(seq_local, shard, groups, columns)
        values = values.transpose(0, 2, 1, 3).reshape(pairs, 1, shard, columns)
        values = jnp.broadcast_to(values, (pairs, copies, shard, columns))
        return exchange(values.reshape(blk_count, shard, columns)).reshape(seq_total, columns)

    def to_tokens(values, columns):
        values = exchange(values.reshape(blk_count, shard, columns))
        values = values.reshape(pairs, copies, shard, columns)[:, 0]
        values = values.reshape(seq_local, groups, shard, columns).transpose(0, 2, 1, 3)
        return values.reshape(token_rows, groups * columns)

    pair_qkv = to_pairs(packed, span)
    pair_attended, flat, log_total = attend_forward(pair_qkv, group)
    attended = to_tokens(pair_attended, lanes)
    middle = residual + matmul(attended, full_out)[:, :width]
    inverse_two = rms_scale(middle)
    normed_two = (middle * inverse_two * gain_second).astype(jnp.bfloat16)
    logits = matmul(normed_two, full_router)
    gates = jax.nn.softmax(jnp.where(chosen, logits, -jnp.inf), axis=-1)

    blocks_pairs, blocks_opposite = ring_gather(normed_two)
    total = blk_count // 2 * token_rows
    ids = jnp.stack([blk_index, blk_index ^ 1]).astype(jnp.int32)

    def apply_experts(blocks, grads, slot, buffers):
        return expert_rows(
            ids, experts, blocks, grads, router, both_gate, both_up, both_down, slot, total, buffers
        )

    ring_pairs = len(blocks_pairs)
    mixed_own, back_own, *buffers = apply_experts(
        [normed_two], [grads_own], 2 * ring_pairs, None
    )
    mixed_pairs, back_pairs = [], []
    for k in range(ring_pairs):
        mixed, back, *buffers = apply_experts(blocks_pairs[k], grads_pairs[k], k, buffers)
        mixed_pairs.append((mixed[:token_rows], mixed[token_rows:]))
        back_pairs.append((back[:token_rows], back[token_rows:]))
    mixed_opposite, back_opposite, *buffers = apply_experts(
        blocks_opposite, grads_opposite, 2 * ring_pairs + 1, buffers
    )
    rows_all, grads_all, d_gate_all, d_up_all, hidden_all = buffers
    back_sum = ring_scatter(back_own, back_pairs, back_opposite)
    mixed_sum = ring_scatter(mixed_own, mixed_pairs, mixed_opposite)
    out = (middle + mixed_sum).reshape(seq_local, shard, width)

    def expert_sum(left, right, swap):
        other = matmul_tn(*((left[:, units:], right) if swap else (left, right[:, units:])))
        mine = matmul_tn(*((left[:, :units], right) if swap else (left, right[:, :units])))
        mine = mine + partner(other.astype(jnp.bfloat16)).astype(jnp.float32)
        return sum_heads(mine.astype(jnp.bfloat16))

    grad_gate_sum = expert_sum(rows_all, d_gate_all, False)
    grad_up_sum = expert_sum(rows_all, d_up_all, False)
    grad_down_sum = expert_sum(hidden_all, grads_all, True)

    d_gates = back_sum[:, width : width + experts] + back_sum[:, width + experts : width + 2 * experts]
    d_logits = gates * (d_gates - jnp.sum(gates * d_gates, axis=-1, keepdims=True))
    grad_router = jnp.dot(normed_two.astype(jnp.float32).T, d_logits, precision=highest)
    d_normed_two = back_sum[:, :width] + jnp.dot(
        d_logits, full_router.astype(jnp.float32).T, precision=highest
    )
    d_mid_norm, grad_gain_second = norm_back(middle, inverse_two, gain_second, d_normed_two)
    d_mid = d_out + d_mid_norm
    d_branch = jnp.pad(d_mid.astype(jnp.bfloat16), ((0, 0), (0, LANES)))
    d_attended = matmul_nt(d_branch, full_out).astype(jnp.bfloat16)
    pair_grad = to_pairs(d_attended, lanes)
    pair_cosine, pair_sine = rope_tables(jnp.arange(seq_total, dtype=jnp.int32), HDIM // 2)
    pair_d = attend_backward(
        pair_qkv, pair_grad, flat, log_total, pair_cosine.T, pair_sine.T, group
    )
    early = scatter_dense(
        add_lanes(
            matmul_tn(attended, d_branch),
            jnp.concatenate([grad_router, grad_gain_second[:, None]], axis=1),
        )
    )
    d_linear = jnp.pad(to_tokens(pair_d, span), ((0, 0), (0, LANES)))
    d_normed = matmul_nt(d_linear, full_mixed)
    d_tok_norm, grad_gain_first = norm_back(residual, inverse_one, gain_first, d_normed)
    grad_tokens = (d_mid + d_tok_norm).reshape(seq_local, shard, width)
    late = scatter_dense(add_lanes(matmul_tn(normed, d_linear), grad_gain_first[:, None]))
    late_mixed = late[:, : groups * span].reshape(part_rows, groups, span)
    return (
        out,
        grad_tokens,
        late[:, groups * span],
        late_mixed[:, :, :lanes].reshape(part_rows, -1),
        late_mixed[:, :, lanes : lanes + HDIM].reshape(part_rows, -1),
        late_mixed[:, :, lanes + HDIM :].reshape(part_rows, -1),
        early[:, :width],
        early[:, width + experts],
        early[:, width : width + experts],
        grad_gate_sum[None],
        grad_up_sum[None],
        grad_down_sum[None],
    )


def solution(mesh):
    placed = (
        P("head", "blk", None),
        P(("head", "blk")),
        P(("head", "blk"), None),
        P(("head", "blk"), None),
        P(("head", "blk"), None),
        P(("head", "blk"), None),
        P(("head", "blk")),
        P(("head", "blk"), None),
        P("blk", None, None),
        P("blk", None, None),
        P("blk", None, None),
        P("head", "blk", None),
        P("head", "blk", None),
    )
    return jax.shard_map(
        local,
        mesh=mesh,
        in_specs=placed,
        out_specs=(
            P("head", "blk", None),
            P("head", "blk", None),
            P(("head", "blk")),
            P(("head", "blk"), None),
            P(("head", "blk"), None),
            P(("head", "blk"), None),
            P(("head", "blk"), None),
            P(("head", "blk")),
            P(("head", "blk"), None),
            P("blk", None, None),
            P("blk", None, None),
            P("blk", None, None),
        ),
        check_vma=False,
    )
```

```python
import functools

import jax
import jax.numpy as jnp
from jax import lax
from jax.experimental import pallas as pl
from jax.experimental.pallas import tpu as pltpu
from jax.sharding import PartitionSpec as P

HDIM = 64
TOP = 8
BLOCK = 256
LANES = 128

highest = lax.Precision.HIGHEST
theta_base = 10000.0
norm_eps = 1e-06


def rope_tables(positions, half_width):
    index_float = jnp.arange(half_width, dtype=jnp.float32)
    frequency = theta_base ** (-2.0 * index_float / (2 * half_width))
    angles = positions.astype(jnp.float32)[:, None] * frequency[None, :]
    return (jnp.cos(angles), jnp.sin(angles))


def rms_scale(values):
    return lax.rsqrt(jnp.mean(values * values, axis=-1, keepdims=True) + norm_eps)


def norm_back(values, inverse, gain, d_normed):
    unit_values = values * inverse
    scaled = d_normed * gain
    d_gain = jnp.sum(d_normed * unit_values, axis=0)
    d_values = inverse * (
        scaled - unit_values * jnp.mean(scaled * unit_values, axis=-1, keepdims=True)
    )
    return (d_values, d_gain)


def matmul(left, right):
    return jnp.dot(left, right, preferred_element_type=jnp.float32)


def matmul_nt(left, right):
    return lax.dot_general(left, right, (((1,), (1,)), ((), ())), preferred_element_type=jnp.float32)


def matmul_tn(left, right):
    return lax.dot_general(left, right, (((0,), (0,)), ((), ())), preferred_element_type=jnp.float32)


def wide(block, group):
    flipped = block.T
    return jnp.concatenate([flipped[h*HDIM:(h+1)*HDIM] for h in range(group)], axis=1)

def tall(block, group):
    return jnp.concatenate([block[:, h*HDIM:(h+1)*HDIM] for h in range(group)], axis=0)

def narrow(values, group, rows):
    return jnp.concatenate([values[:, h*rows:(h+1)*rows] for h in range(group)], axis=0).T

def forward_kernel(group, qkv_ref, att_ref, flat_ref, lse_ref, key_sc, val_sc, acc_sc):
    i = pl.program_id(0)
    lanes = group*HDIM
    @pl.when(i == 0)
    def _():
        key_sc[...] = qkv_ref[:, lanes:lanes+HDIM]
        val_sc[...] = qkv_ref[:, lanes+HDIM:lanes+2*HDIM].T
    rows = pl.ds(pl.multiple_of(i*BLOCK, BLOCK), BLOCK)
    query = wide(qkv_ref[rows, :lanes], group) * jnp.bfloat16(HDIM**-0.5)
    acc_sc[...] = jnp.zeros_like(acc_sc)
    def step(j, carry):
        top, total = carry
        here = pl.ds(pl.multiple_of(j*BLOCK, BLOCK), BLOCK)
        scores = jnp.dot(key_sc[here, :], query, preferred_element_type=jnp.float32)
        new_top = jnp.maximum(top, jnp.max(scores, axis=0, keepdims=True))
        probs = jnp.exp(scores - new_top)
        fade = jnp.exp(top - new_top)
        acc_sc[...] = acc_sc[...]*fade + jnp.dot(val_sc[:, here], probs.astype(jnp.bfloat16), preferred_element_type=jnp.float32)
        return new_top, total*fade + jnp.sum(probs, axis=0, keepdims=True)
    width = group*BLOCK
    top, total = lax.fori_loop(0, i+1, step, (jnp.full((1,width), -1e30, jnp.float32), jnp.zeros((1,width), jnp.float32)))
    result = acc_sc[...] / total
    flat_ref[0] = result
    att_ref[...] = narrow(result.astype(jnp.bfloat16), group, BLOCK)
    lse_ref[0] = top + jnp.log(total)

def attend_forward(qkv, group):
    total = qkv.shape[0]; steps = total//BLOCK; lanes = group*HDIM; width = group*BLOCK
    return pl.pallas_call(
        functools.partial(forward_kernel, group),
        grid=(steps,),
        in_specs=[pl.BlockSpec((total, lanes+2*HDIM), lambda i: (0,0))],
        out_specs=[pl.BlockSpec((BLOCK, lanes), lambda i: (i,0)),
                   pl.BlockSpec((1, HDIM, width), lambda i: (i,0,0)),
                   pl.BlockSpec((1,1,width), lambda i: (i,0,0))],
        out_shape=[jax.ShapeDtypeStruct((total, lanes), jnp.bfloat16),
                   jax.ShapeDtypeStruct((steps,HDIM,width), jnp.float32),
                   jax.ShapeDtypeStruct((steps,1,width), jnp.float32)],
        scratch_shapes=[pltpu.VMEM((total,HDIM), jnp.bfloat16), pltpu.VMEM((HDIM,total), jnp.bfloat16), pltpu.VMEM((HDIM,width), jnp.float32)],
        compiler_params=pltpu.CompilerParams(dimension_semantics=("arbitrary",)),
        name="attend_forward",
    )(qkv)

def unrotate(values, cosine, sine):
    a, b = values[:HDIM//2], values[HDIM//2:]
    return jnp.concatenate([a*cosine + b*sine, b*cosine - a*sine], axis=0)

def backward_kernel(group, steps, qkv_ref, grad_ref, flat_ref, lse_ref, cos_ref, sin_ref, out_ref, key_sc, keyt_sc, val_sc, dq_sc, dk_sc, dv_sc):
    i = pl.program_id(0)
    lanes = group*HDIM
    scale = HDIM**-0.5
    @pl.when(i == 0)
    def _():
        key = qkv_ref[:, lanes:lanes+HDIM]
        key_sc[...] = key
        keyt_sc[...] = key.T
        val_sc[...] = qkv_ref[:, lanes+HDIM:lanes+2*HDIM]
        dk_sc[...] = jnp.zeros_like(dk_sc)
        dv_sc[...] = jnp.zeros_like(dv_sc)
    rows = pl.ds(pl.multiple_of(i*BLOCK, BLOCK), BLOCK)
    block = qkv_ref[rows, :lanes] * jnp.bfloat16(scale)
    query_w, query_t = wide(block, group), tall(block, group)
    grad = grad_ref[...]
    grad_w, grad_t = wide(grad, group), tall(grad, group)
    lse = lse_ref[0]
    delta = jnp.sum(grad_w.astype(jnp.float32)*flat_ref[0], axis=0, keepdims=True)
    dq_sc[...] = jnp.zeros_like(dq_sc)
    def step(j, carry):
        here = pl.ds(pl.multiple_of(j*BLOCK, BLOCK), BLOCK)
        scores = jnp.dot(key_sc[here,:], query_w, preferred_element_type=jnp.float32)
        probs = jnp.exp(scores - lse)
        dprobs = jnp.dot(val_sc[here,:], grad_w, preferred_element_type=jnp.float32)
        dv_sc[here,:] += jnp.dot(probs.astype(jnp.bfloat16), grad_t, preferred_element_type=jnp.float32)
        dscores = (probs*(dprobs-delta)).astype(jnp.bfloat16)
        dk_sc[here,:] += jnp.dot(dscores, query_t, preferred_element_type=jnp.float32)
        dq_sc[...] += jnp.dot(keyt_sc[:,here], dscores, preferred_element_type=jnp.float32)
        return carry
    lax.fori_loop(0, i+1, step, 0)
    cosine, sine = cos_ref[:, rows], sin_ref[:, rows]
    pieces = [unrotate(dq_sc[:, h*BLOCK:(h+1)*BLOCK]*scale, cosine, sine).astype(jnp.bfloat16) for h in range(group)]
    out_ref[rows, :lanes] = jnp.concatenate(pieces, axis=0).T
    @pl.when(i == steps-1)
    def _():
        def finish(j, carry):
            here = pl.ds(pl.multiple_of(j*BLOCK, BLOCK), BLOCK)
            turned = unrotate(dk_sc[here,:].T, cos_ref[:,here], sin_ref[:,here]).astype(jnp.bfloat16)
            both = jnp.concatenate([turned, dv_sc[here,:].astype(jnp.bfloat16).T], axis=0).T
            out_ref[here, lanes:lanes+2*HDIM] = both
            return carry
        lax.fori_loop(0, steps, finish, 0)

def attend_backward(qkv, grad, flat, lse, cosine, sine, group):
    total = qkv.shape[0]; steps = total//BLOCK; lanes = group*HDIM; width = group*BLOCK
    return pl.pallas_call(
        functools.partial(backward_kernel, group, steps),
        grid=(steps,),
        in_specs=[pl.BlockSpec((total, lanes+2*HDIM), lambda i: (0,0)),
                  pl.BlockSpec((BLOCK, lanes), lambda i: (i,0)),
                  pl.BlockSpec((1, HDIM, width), lambda i: (i,0,0)),
                  pl.BlockSpec((1,1,width), lambda i: (i,0,0)),
                  pl.BlockSpec((HDIM//2, total), lambda i: (0,0)),
                  pl.BlockSpec((HDIM//2, total), lambda i: (0,0))],
        out_specs=pl.BlockSpec((total, lanes+2*HDIM), lambda i: (0,0)),
        out_shape=jax.ShapeDtypeStruct((total, lanes+2*HDIM), jnp.bfloat16),
        scratch_shapes=[pltpu.VMEM((total,HDIM), jnp.bfloat16), pltpu.VMEM((HDIM,total), jnp.bfloat16), pltpu.VMEM((total,HDIM), jnp.bfloat16),
                        pltpu.VMEM((HDIM,width), jnp.float32), pltpu.VMEM((total,HDIM), jnp.float32), pltpu.VMEM((total,HDIM), jnp.float32)],
        compiler_params=pltpu.CompilerParams(dimension_semantics=("arbitrary",)),
        name="attend_backward",
    )(qkv, grad, flat, lse, cosine, sine)

def expert_kernel(
    parts, rows, width, experts, steps, chained, index_ref, *refs
):
    blocks = refs[:parts]
    grads = refs[parts : 2 * parts]
    router_ref, lin_ref, down_ref = refs[2 * parts : 2 * parts + 3]
    refs = refs[2 * parts + 3 + (4 if chained else 0) :]
    mixed_ref, back_ref, rows_ref, grads_ref, d_lin_ref, hidden_ref = refs[:6]
    gates_sc, d_gates_sc, mixed_sc, back_sc = refs[6:]
    units = down_ref.shape[1]
    step = pl.program_id(0)
    lane = lax.broadcasted_iota(jnp.int32, (rows, LANES), 1)

    @pl.when(step == 0)
    def _():
        part = rows // parts
        for k in range(parts):
            here = pl.ds(k * part, part)
            rows_ref[here, :] = blocks[k][...]
            grads_ref[here, :] = grads[k][:, :width]
            logits = jnp.dot(blocks[k][...], router_ref[...], preferred_element_type=jnp.float32)
            logits = jnp.where(grads[k][:, width:].astype(jnp.float32) > 0.5, logits, -1e30)
            weight = jnp.exp(logits - jnp.max(logits, axis=1, keepdims=True))
            gates_sc[here, :] = weight / jnp.sum(weight, axis=1, keepdims=True)
        d_gates_sc[...] = jnp.zeros_like(d_gates_sc)

    expert = index_ref[step]
    own = lane == expert
    gate = jnp.sum(jnp.where(own, gates_sc[...], 0.0), axis=1, keepdims=True)
    block = rows_ref[...]
    lin = jnp.dot(block, lin_ref[0], preferred_element_type=jnp.float32)
    gate_lin, up_lin = lin[:, :units], lin[:, units:]
    d_hidden = matmul_nt(grads_ref[...], down_ref[0])
    sigma = 1.0 / (1.0 + jnp.exp(-gate_lin))
    active = gate_lin * sigma
    hidden = active * up_lin
    d_gates_sc[...] += jnp.where(own, jnp.sum(hidden * d_hidden, axis=1, keepdims=True), 0.0)
    hidden = (gate * hidden).astype(jnp.bfloat16)
    d_hidden = gate * d_hidden
    d_gate = (d_hidden * up_lin * sigma * (1.0 + gate_lin * (1.0 - sigma))).astype(jnp.bfloat16)
    d_up = (d_hidden * active).astype(jnp.bfloat16)
    hidden_ref[...] = hidden
    d_lin = jnp.concatenate([d_gate, d_up], axis=1)
    d_lin_ref[...] = d_lin
    mixed = jnp.dot(hidden, down_ref[0], preferred_element_type=jnp.float32)
    back = matmul_nt(d_lin, lin_ref[0])

    @pl.when(step == 0)
    def _():
        mixed_sc[...] = mixed
        back_sc[...] = back

    @pl.when(step > 0)
    def _():
        mixed_sc[...] += mixed
        back_sc[...] += back

    @pl.when(step == steps - 1)
    def _():
        mixed_ref[...] = mixed_sc[...].astype(jnp.bfloat16)
        back_ref[:, :width] = back_sc[...].astype(jnp.bfloat16)
        d_gates = d_gates_sc[...]
        high = d_gates.astype(jnp.bfloat16).astype(jnp.float32)
        low = pltpu.roll(d_gates - high, experts, 1)
        back_ref[:, width:] = jnp.where(lane < experts, high, low).astype(jnp.bfloat16)


def expert_rows(index, experts, blocks, grads, router, lin, down, slot, total, buffers):
    parts = len(blocks)
    part, width = blocks[0].shape
    rows = parts * part
    units = down.shape[1]
    steps = 2
    whole = lambda *shape: pl.BlockSpec(shape, lambda i, ids: (0,) * len(shape))
    columns = lambda count: pl.BlockSpec((rows, count), lambda i, ids: (slot, i))
    kept = pl.BlockSpec((rows, width), lambda i, ids: (slot, 0))
    chained = buffers is not None
    shapes = [
        jax.ShapeDtypeStruct((rows, width), jnp.bfloat16),
        jax.ShapeDtypeStruct((rows, width + LANES), jnp.bfloat16),
        jax.ShapeDtypeStruct((total, width), jnp.bfloat16),
        jax.ShapeDtypeStruct((total, width), jnp.bfloat16),
        jax.ShapeDtypeStruct((total, 4 * units), jnp.bfloat16),
        jax.ShapeDtypeStruct((total, 2 * units), jnp.bfloat16),
    ]
    inputs = [index, *blocks, *grads, router, lin, down] + (list(buffers) if chained else [])
    first = 1 + 2 * parts + 3
    return pl.pallas_call(
        functools.partial(expert_kernel, parts, rows, width, experts, steps, chained),
        grid_spec=pltpu.PrefetchScalarGridSpec(
            num_scalar_prefetch=1,
            grid=(steps,),
            in_specs=[whole(part, width)] * parts
            + [whole(part, width + LANES)] * parts
            + [
                whole(width, LANES),
                pl.BlockSpec((1, width, 2 * units), lambda i, ids: (i, 0, 0)),
                pl.BlockSpec((1, units, width), lambda i, ids: (i, 0, 0)),
            ]
            + ([pl.BlockSpec(memory_space=pl.ANY)] * 4 if chained else []),
            out_specs=[
                whole(rows, width),
                whole(rows, width + LANES),
                kept,
                kept,
                columns(2 * units),
                columns(units),
            ],
            scratch_shapes=[
                pltpu.VMEM((rows, LANES), jnp.float32),
                pltpu.VMEM((rows, LANES), jnp.float32),
                pltpu.VMEM((rows, width), jnp.float32),
                pltpu.VMEM((rows, width), jnp.float32),
            ],
        ),
        out_shape=shapes,
        input_output_aliases={first + k: 2 + k for k in range(4)} if chained else {},
        compiler_params=pltpu.CompilerParams(dimension_semantics=("arbitrary",)),
        cost_estimate=pl.CostEstimate(
            flops=rows * width * units * 24,
            bytes_accessed=12 * width * units + 20 * rows * width,
            transcendentals=rows * units * 2,
        ),
        name="expert_rows",
    )(*inputs)


def gather_dense(values):
    return lax.all_gather(values, ("head", "blk"), axis=0, tiled=True)


def exchange(values):
    return lax.all_to_all(values, "blk", split_axis=0, concat_axis=0, tiled=True)


def sum_heads(values):
    if lax.axis_size("head") == 2:
        other = lax.ppermute(values, "head", [(0, 1), (1, 0)])
        return values.astype(jnp.float32) + other.astype(jnp.float32)
    return lax.psum(values, "head").astype(jnp.float32)


def partner(values):
    count = lax.axis_size("blk")
    return lax.ppermute(values, "blk", [(k, k ^ 1) for k in range(count)])


def after(values, *earlier):
    return lax.optimization_barrier((values, earlier))[0]


def ring_order():
    half = lax.axis_size("blk") // 4
    return [2 * k for k in range(half)] + [2 * k + 1 for k in reversed(range(half))]


def ring_steps():
    order = ring_order()
    onward, back = [], []
    for place, chip in enumerate(order):
        following = order[(place + 1) % len(order)]
        for core in range(2):
            onward.append((2 * chip + core, 2 * following + core))
            back.append((2 * following + core, 2 * chip + core))
    send_on = lambda values: lax.ppermute(values, "blk", onward)
    send_back = lambda values: lax.ppermute(values, "blk", back)
    return len(order), send_on, send_back


def ring_gather(values):
    length, send_on, send_back = ring_steps()
    half = values.shape[0] // 2
    behind = ahead = values
    pairs = []
    for _ in range(length // 2 - 1):
        behind, ahead = send_on(behind), send_back(ahead)
        pairs.append((behind, ahead))
    return pairs, (send_on(behind[:half]), send_back(ahead[half:]))


class RingSum:
    def __init__(self, own, pairs, opposite, axis=0):
        _, self.send_on, self.send_back = ring_steps()
        self.own, self.pairs, self.axis = own, list(reversed(pairs)), axis
        self.half = own.shape[axis] // 2
        self.onward = lax.slice_in_dim(opposite, 0, self.half, axis=axis)
        self.back = lax.slice_in_dim(opposite, self.half, 2 * self.half, axis=axis)
        self.hop = 0

    def send(self, *hold):
        if self.hop > 0:
            behind, ahead = self.pairs[self.hop - 1]
            self.onward, self.back = self.onward + ahead, self.back + behind
        if hold:
            self.onward, self.back = after((self.onward, self.back), hold)
        self.onward, self.back = self.send_on(self.onward), self.send_back(self.back)
        return self

    def land(self, *filler):
        if filler:
            self.onward, self.back = after((self.onward, self.back), filler)
        if self.hop == 0:
            spread = [(0, 0), (0, 0)]
            spread[self.axis] = (0, self.half)
            self.onward = jnp.pad(self.onward, spread)
            spread[self.axis] = (self.half, 0)
            self.back = jnp.pad(self.back, spread)
        self.hop += 1
        return self

    def total(self):
        while self.hop <= len(self.pairs):
            self.send().land()
        wide = self.own.astype(jnp.float32)
        return wide + self.onward.astype(jnp.float32) + self.back.astype(jnp.float32)


def scatter_dense(values):
    return lax.psum_scatter(
        values, ("head", "blk"), scatter_dimension=0, tiled=True
    ).astype(jnp.float32)


def dense_scatter(values):
    heads = lax.axis_size("head")
    chips = lax.axis_size("blk") // 2
    rows = values.shape[0] // (2 * heads * chips)
    columns = values.shape[1]
    grid = values.reshape(heads, chips, 2, rows, columns)
    index = lax.axis_index("blk")
    head = lax.axis_index("head")
    chip, turns = index // 2, chips // 2
    place = jnp.where(chip % 2 == 0, chip // 2, chips - 1 - chip // 2)
    parts = grid[:, :, 0], grid[:, :, 1]
    even = index % 2 == 0
    away = jnp.where(even, parts[1], parts[0])
    mine = jnp.where(even, parts[0], parts[1]) + partner(away)

    def block(offset):
        target = (place + offset) % chips
        chip = jnp.where(target < turns, 2 * target, 2 * (chips - 1 - target) + 1)
        piece = lax.dynamic_slice(mine, (0, chip, 0, 0), (heads, 1, rows, columns))
        return piece.reshape(heads * rows, columns)

    pairs = [(block(-k), block(k)) for k in range(1, chips // 2)]
    total = RingSum(block(0), pairs, block(chips // 2)).total().astype(jnp.bfloat16)
    share = lambda turn: lax.dynamic_slice(
        total, ((head + turn) % heads * rows, 0), (rows, columns)
    )
    result = share(0).astype(jnp.float32)
    for turn in range(1, heads):
        moved = [(k, (k + turn) % heads) for k in range(heads)]
        result = result + lax.ppermute(share(turn), "head", moved).astype(jnp.float32)
    return result


def with_lanes(values, extra):
    rows = values.shape[0]
    spare = jnp.zeros((rows, LANES - extra.shape[1]), values.dtype)
    return jnp.concatenate([values, extra.astype(values.dtype), spare], axis=1)


def add_lanes(padded, extra):
    rows, columns = padded.shape
    spread = ((0, 0), (columns - LANES, LANES - extra.shape[1]))
    return padded + jnp.pad(extra, spread)


def local(
    tokens,
    gain_attn,
    w_query,
    w_key,
    w_value,
    w_out,
    gain_moe,
    w_router,
    w_gate,
    w_up,
    w_down,
    routes,
    grad_out,
):
    seq_local, shard, width = tokens.shape
    token_rows = seq_local * shard
    blk_index = lax.axis_index("blk")
    blk_count = lax.axis_size("blk")
    seq_total = blk_count * shard
    part_rows = w_query.shape[0]
    groups = w_key.shape[1] // HDIM
    group = w_query.shape[1] // w_key.shape[1]
    lanes = group * HDIM
    span = lanes + 2 * HDIM
    pairs = seq_local * groups
    copies = blk_count // pairs
    experts = w_router.shape[1]
    units = w_gate.shape[2]

    mixed_weights = jnp.concatenate(
        [
            w_query.reshape(part_rows, groups, lanes),
            w_key.reshape(part_rows, groups, HDIM),
            w_value.reshape(part_rows, groups, HDIM),
        ],
        axis=2,
    ).reshape(part_rows, groups * span)
    full_mixed = gather_dense(with_lanes(mixed_weights, gain_attn[:, None]))
    full_out = gather_dense(
        with_lanes(w_out, jnp.concatenate([w_router, gain_moe[:, None]], axis=1))
    )
    router = full_out[:, width:]
    full_router = router[:, :experts]
    router = jnp.where(jnp.arange(LANES)[None, :] < experts, router, jnp.bfloat16(0.0))
    gain_first = full_mixed[:, groups * span].astype(jnp.float32)
    gain_second = full_out[:, width + experts].astype(jnp.float32)

    expert_ids = jnp.arange(experts, dtype=jnp.int32)
    routes_tok = routes.reshape(token_rows, TOP)
    chosen = jnp.any(routes_tok[:, :, None] == expert_ids[None, None, :], axis=1)
    d_out = grad_out.reshape(token_rows, width)
    grads_own = with_lanes(d_out.astype(jnp.bfloat16), chosen)
    grads_pairs, grads_opposite = ring_gather(grads_own)
    full_mixed = after(full_mixed, grads_pairs[:2])
    w_lin = jnp.concatenate([w_gate, w_up], axis=2)
    both_lin = jnp.concatenate([w_lin, partner(w_lin)], axis=0)
    both_down = jnp.concatenate([w_down, partner(w_down)], axis=0)

    residual = tokens.astype(jnp.float32).reshape(token_rows, width)
    inverse_one = rms_scale(residual)
    normed = (residual * inverse_one * gain_first).astype(jnp.bfloat16)
    positions = blk_index * shard + jnp.arange(shard, dtype=jnp.int32)
    cosine, sine = rope_tables(positions, HDIM // 2)
    turned = (jnp.arange(groups * (group + 2)) % (group + 2) < group + 1)[None, None, :, None]
    cosine = jnp.where(turned, cosine[None, :, None, :], 1.0)
    sine = jnp.where(turned, sine[None, :, None, :], 0.0)
    linear = matmul(normed, full_mixed)[:, : groups * span].reshape(seq_local, shard, -1, HDIM)
    first, second = linear[..., : HDIM // 2], linear[..., HDIM // 2 :]
    packed = jnp.concatenate(
        [first * cosine - second * sine, second * cosine + first * sine], axis=-1
    ).astype(jnp.bfloat16)

    def to_pairs(values, columns):
        values = values.reshape(seq_local, shard, groups, columns)
        values = values.transpose(0, 2, 1, 3).reshape(pairs, 1, shard, columns)
        values = jnp.broadcast_to(values, (pairs, copies, shard, columns))
        return exchange(values.reshape(blk_count, shard, columns)).reshape(seq_total, columns)

    def to_tokens(values, columns):
        values = exchange(values.reshape(blk_count, shard, columns))
        values = values.reshape(pairs, copies, shard, columns)[:, 0]
        values = values.reshape(seq_local, groups, shard, columns).transpose(0, 2, 1, 3)
        return values.reshape(token_rows, groups * columns)

    pair_qkv = to_pairs(packed, span)
    pair_attended, flat, log_total = attend_forward(pair_qkv, group)
    attended = to_tokens(pair_attended, lanes)
    middle = residual + matmul(attended, full_out)[:, :width]
    inverse_two = rms_scale(middle)
    normed_two = (middle * inverse_two * gain_second).astype(jnp.bfloat16)
    logits = matmul(normed_two, full_router)
    gates = jax.nn.softmax(jnp.where(chosen, logits, -jnp.inf), axis=-1)

    blocks_pairs, blocks_opposite = ring_gather(normed_two)
    total = blk_count // 2 * token_rows
    ids = jnp.stack([blk_index, blk_index ^ 1]).astype(jnp.int32)

    def apply_experts(blocks, grads, slot, buffers):
        return expert_rows(
            ids, experts, blocks, grads, router, both_lin, both_down, slot, total, buffers
        )

    ring_pairs = len(blocks_pairs)
    mixed_own, back_own, *buffers = apply_experts(
        [normed_two], [grads_own], 2 * ring_pairs, None
    )
    mixed_pairs, back_pairs = [], []
    for k in range(ring_pairs):
        mixed, back, *buffers = apply_experts(blocks_pairs[k], grads_pairs[k], k, buffers)
        mixed_pairs.append((mixed[:token_rows], mixed[token_rows:]))
        back_pairs.append((back[:token_rows], back[token_rows:]))
    mixed_opposite, back_opposite, *buffers = apply_experts(
        blocks_opposite, grads_opposite, 2 * ring_pairs + 1, buffers
    )
    rows_all, grads_all, d_lin_all, hidden_all = buffers
    others = [
        matmul_tn(rows_all, d_lin_all[:, 2 * units :]).astype(jnp.bfloat16),
        matmul_tn(hidden_all[:, units:], grads_all).astype(jnp.bfloat16),
    ]
    mine = [
        matmul_tn(rows_all, d_lin_all[:, : 2 * units]),
        matmul_tn(hidden_all[:, :units], grads_all),
    ]
    mine = [
        (part + partner(other).astype(jnp.float32)).astype(jnp.bfloat16)
        for part, other in zip(mine, others)
    ]
    back_ring = RingSum(back_own, back_pairs, back_opposite)
    back_ring.send().land(others).send().land(mine)
    back_sum = back_ring.total()
    grad_lin_sum, grad_down_sum = [sum_heads(part) for part in mine]
    grad_gate_sum, grad_up_sum = grad_lin_sum[:, :units], grad_lin_sum[:, units:]
    mixed_ring = RingSum(mixed_own, mixed_pairs, mixed_opposite)
    mixed_ring.send(back_sum)

    d_gates = back_sum[:, width : width + experts] + back_sum[:, width + experts : width + 2 * experts]
    d_logits = gates * (d_gates - jnp.sum(gates * d_gates, axis=-1, keepdims=True))
    grad_router = jnp.dot(normed_two.astype(jnp.float32).T, d_logits, precision=highest)
    d_normed_two = back_sum[:, :width] + jnp.dot(
        d_logits, full_router.astype(jnp.float32).T, precision=highest
    )
    d_mid_norm, grad_gain_second = norm_back(middle, inverse_two, gain_second, d_normed_two)
    d_mid = d_out + d_mid_norm
    d_branch = jnp.pad(d_mid.astype(jnp.bfloat16), ((0, 0), (0, LANES)))
    d_attended = matmul_nt(d_branch, full_out).astype(jnp.bfloat16)
    early = add_lanes(
        matmul_tn(attended, d_branch),
        jnp.concatenate([grad_router, grad_gain_second[:, None]], axis=1),
    ).astype(jnp.bfloat16)
    d_attended = after(d_attended, early)
    mixed_ring.land(d_attended)
    pair_grad = to_pairs(d_attended, lanes)
    mixed_ring.send(pair_grad)
    pair_cosine, pair_sine = rope_tables(jnp.arange(seq_total, dtype=jnp.int32), HDIM // 2)
    pair_d = attend_backward(
        pair_qkv, pair_grad, flat, log_total, pair_cosine.T, pair_sine.T, group
    )
    early = scatter_dense(early)
    mixed_ring.land(pair_d).send(pair_d)
    d_linear = to_tokens(pair_d, span)
    mixed_ring.land(d_linear)
    out = (middle + mixed_ring.total()).reshape(seq_local, shard, width)
    grad_mixed = matmul_tn(normed, d_linear).astype(jnp.bfloat16)
    late_mixed = dense_scatter(grad_mixed).reshape(part_rows, groups, span)
    d_normed = matmul_nt(jnp.pad(d_linear, ((0, 0), (0, LANES))), full_mixed)
    d_tok_norm, grad_gain_first = norm_back(residual, inverse_one, gain_first, d_normed)
    grad_tokens = (d_mid + d_tok_norm).reshape(seq_local, shard, width)
    late_gain = dense_scatter(
        jnp.pad(grad_gain_first[:, None].astype(jnp.bfloat16), ((0, 0), (0, LANES - 1)))
    )
    return (
        out,
        grad_tokens,
        late_gain[:, 0],
        late_mixed[:, :, :lanes].reshape(part_rows, -1),
        late_mixed[:, :, lanes : lanes + HDIM].reshape(part_rows, -1),
        late_mixed[:, :, lanes + HDIM :].reshape(part_rows, -1),
        early[:, :width],
        early[:, width + experts],
        early[:, width : width + experts],
        grad_gate_sum[None],
        grad_up_sum[None],
        grad_down_sum[None],
    )


def solution(mesh):
    placed = (
        P("head", "blk", None),
        P(("head", "blk")),
        P(("head", "blk"), None),
        P(("head", "blk"), None),
        P(("head", "blk"), None),
        P(("head", "blk"), None),
        P(("head", "blk")),
        P(("head", "blk"), None),
        P("blk", None, None),
        P("blk", None, None),
        P("blk", None, None),
        P("head", "blk", None),
        P("head", "blk", None),
    )
    return jax.shard_map(
        local,
        mesh=mesh,
        in_specs=placed,
        out_specs=(
            P("head", "blk", None),
            P("head", "blk", None),
            P(("head", "blk")),
            P(("head", "blk"), None),
            P(("head", "blk"), None),
            P(("head", "blk"), None),
            P(("head", "blk"), None),
            P(("head", "blk")),
            P(("head", "blk"), None),
            P("blk", None, None),
            P("blk", None, None),
            P("blk", None, None),
        ),
        check_vma=False,
    )
```

```python
import functools

import jax
import jax.numpy as jnp
from jax import lax
from jax.experimental import pallas as pl
from jax.experimental.pallas import tpu as pltpu
from jax.sharding import PartitionSpec as P


HDIM = 64
TOP = 8
BLOCK = 256
LANES = 128

highest = lax.Precision.HIGHEST
theta_base = 10000.0
norm_eps = 1e-06


def rope_tables(positions, half_width):
    index_float = jnp.arange(half_width, dtype=jnp.float32)
    frequency = theta_base ** (-2.0 * index_float / (2 * half_width))
    angles = positions.astype(jnp.float32)[:, None] * frequency[None, :]
    return (jnp.cos(angles), jnp.sin(angles))


def rms_scale(values):
    return lax.rsqrt(jnp.mean(values * values, axis=-1, keepdims=True) + norm_eps)


def norm_back(values, inverse, gain, d_normed):
    unit_values = values * inverse
    scaled = d_normed * gain
    d_gain = jnp.sum(d_normed * unit_values, axis=0)
    d_values = inverse * (
        scaled - unit_values * jnp.mean(scaled * unit_values, axis=-1, keepdims=True)
    )
    return (d_values, d_gain)


def matmul(left, right):
    return jnp.dot(left, right, preferred_element_type=jnp.float32)


def matmul_nt(left, right):
    return lax.dot_general(left, right, (((1,), (1,)), ((), ())), preferred_element_type=jnp.float32)


def matmul_tn(left, right):
    return lax.dot_general(left, right, (((0,), (0,)), ((), ())), preferred_element_type=jnp.float32)


def wide(block, group):
    flipped = block.T
    return jnp.concatenate([flipped[h*HDIM:(h+1)*HDIM] for h in range(group)], axis=1)


def tall(block, group):
    return jnp.concatenate([block[:, h*HDIM:(h+1)*HDIM] for h in range(group)], axis=0)


def narrow(values, group, rows):
    return jnp.concatenate([values[:, h*rows:(h+1)*rows] for h in range(group)], axis=0).T


def forward_kernel(group, qkv_ref, att_ref, flat_ref, lse_ref, key_sc, val_sc, acc_sc):
    i = pl.program_id(0)
    lanes = group*HDIM

    @pl.when(i == 0)
    def _():
        key_sc[...] = qkv_ref[:, lanes:lanes+HDIM]
        val_sc[...] = qkv_ref[:, lanes+HDIM:lanes+2*HDIM].T

    rows = pl.ds(pl.multiple_of(i*BLOCK, BLOCK), BLOCK)
    query = wide(qkv_ref[rows, :lanes], group) * jnp.bfloat16(HDIM**-0.5)
    acc_sc[...] = jnp.zeros_like(acc_sc)

    def step(j, carry):
        top, total = carry
        here = pl.ds(pl.multiple_of(j*BLOCK, BLOCK), BLOCK)
        scores = jnp.dot(key_sc[here, :], query, preferred_element_type=jnp.float32)
        new_top = jnp.maximum(top, jnp.max(scores, axis=0, keepdims=True))
        probs = jnp.exp(scores - new_top)
        fade = jnp.exp(top - new_top)
        acc_sc[...] = acc_sc[...]*fade + jnp.dot(val_sc[:, here], probs.astype(jnp.bfloat16), preferred_element_type=jnp.float32)
        return new_top, total*fade + jnp.sum(probs, axis=0, keepdims=True)

    width = group*BLOCK
    top, total = lax.fori_loop(0, i+1, step, (jnp.full((1,width), -1e30, jnp.float32), jnp.zeros((1,width), jnp.float32)))
    result = acc_sc[...] / total
    flat_ref[0] = result
    att_ref[...] = narrow(result.astype(jnp.bfloat16), group, BLOCK)
    lse_ref[0] = top + jnp.log(total)


def attend_forward(qkv, group):
    total = qkv.shape[0]; steps = total//BLOCK; lanes = group*HDIM; width = group*BLOCK
    return pl.pallas_call(
        functools.partial(forward_kernel, group),
        grid=(steps,),
        in_specs=[pl.BlockSpec((total, lanes+2*HDIM), lambda i: (0,0))],
        out_specs=[pl.BlockSpec((BLOCK, lanes), lambda i: (i,0)),
                   pl.BlockSpec((1, HDIM, width), lambda i: (i,0,0)),
                   pl.BlockSpec((1,1,width), lambda i: (i,0,0))],
        out_shape=[jax.ShapeDtypeStruct((total, lanes), jnp.bfloat16),
                   jax.ShapeDtypeStruct((steps,HDIM,width), jnp.float32),
                   jax.ShapeDtypeStruct((steps,1,width), jnp.float32)],
        scratch_shapes=[pltpu.VMEM((total,HDIM), jnp.bfloat16), pltpu.VMEM((HDIM,total), jnp.bfloat16), pltpu.VMEM((HDIM,width), jnp.float32)],
        compiler_params=pltpu.CompilerParams(dimension_semantics=("arbitrary",)),
        name="attend_forward",
    )(qkv)


def unrotate(values, cosine, sine):
    a, b = values[:HDIM//2], values[HDIM//2:]
    return jnp.concatenate([a*cosine + b*sine, b*cosine - a*sine], axis=0)


def backward_kernel(group, steps, qkv_ref, grad_ref, flat_ref, lse_ref, cos_ref, sin_ref, out_ref, key_sc, keyt_sc, val_sc, dq_sc, dk_sc, dv_sc):
    i = pl.program_id(0)
    lanes = group*HDIM
    scale = HDIM**-0.5

    @pl.when(i == 0)
    def _():
        key = qkv_ref[:, lanes:lanes+HDIM]
        key_sc[...] = key
        keyt_sc[...] = key.T
        val_sc[...] = qkv_ref[:, lanes+HDIM:lanes+2*HDIM]
        dk_sc[...] = jnp.zeros_like(dk_sc)
        dv_sc[...] = jnp.zeros_like(dv_sc)

    rows = pl.ds(pl.multiple_of(i*BLOCK, BLOCK), BLOCK)
    block = qkv_ref[rows, :lanes] * jnp.bfloat16(scale)
    query_w, query_t = wide(block, group), tall(block, group)
    grad = grad_ref[...]
    grad_w, grad_t = wide(grad, group), tall(grad, group)
    lse = lse_ref[0]
    delta = jnp.sum(grad_w.astype(jnp.float32)*flat_ref[0], axis=0, keepdims=True)
    dq_sc[...] = jnp.zeros_like(dq_sc)

    def step(j, carry):
        here = pl.ds(pl.multiple_of(j*BLOCK, BLOCK), BLOCK)
        scores = jnp.dot(key_sc[here,:], query_w, preferred_element_type=jnp.float32)
        probs = jnp.exp(scores - lse)
        dprobs = jnp.dot(val_sc[here,:], grad_w, preferred_element_type=jnp.float32)
        dv_sc[here,:] += jnp.dot(probs.astype(jnp.bfloat16), grad_t, preferred_element_type=jnp.float32)
        dscores = (probs*(dprobs-delta)).astype(jnp.bfloat16)
        dk_sc[here,:] += jnp.dot(dscores, query_t, preferred_element_type=jnp.float32)
        dq_sc[...] += jnp.dot(keyt_sc[:,here], dscores, preferred_element_type=jnp.float32)
        return carry

    lax.fori_loop(0, i+1, step, 0)
    cosine, sine = cos_ref[:, rows], sin_ref[:, rows]
    pieces = [unrotate(dq_sc[:, h*BLOCK:(h+1)*BLOCK]*scale, cosine, sine).astype(jnp.bfloat16) for h in range(group)]
    out_ref[rows, :lanes] = jnp.concatenate(pieces, axis=0).T

    @pl.when(i == steps-1)
    def _():
        def finish(j, carry):
            here = pl.ds(pl.multiple_of(j*BLOCK, BLOCK), BLOCK)
            turned = unrotate(dk_sc[here,:].T, cos_ref[:,here], sin_ref[:,here]).astype(jnp.bfloat16)
            both = jnp.concatenate([turned, dv_sc[here,:].astype(jnp.bfloat16).T], axis=0).T
            out_ref[here, lanes:lanes+2*HDIM] = both
            return carry

        lax.fori_loop(0, steps, finish, 0)


def attend_backward(qkv, grad, flat, lse, cosine, sine, group):
    total = qkv.shape[0]; steps = total//BLOCK; lanes = group*HDIM; width = group*BLOCK
    return pl.pallas_call(
        functools.partial(backward_kernel, group, steps),
        grid=(steps,),
        in_specs=[pl.BlockSpec((total, lanes+2*HDIM), lambda i: (0,0)),
                  pl.BlockSpec((BLOCK, lanes), lambda i: (i,0)),
                  pl.BlockSpec((1, HDIM, width), lambda i: (i,0,0)),
                  pl.BlockSpec((1,1,width), lambda i: (i,0,0)),
                  pl.BlockSpec((HDIM//2, total), lambda i: (0,0)),
                  pl.BlockSpec((HDIM//2, total), lambda i: (0,0))],
        out_specs=pl.BlockSpec((total, lanes+2*HDIM), lambda i: (0,0)),
        out_shape=jax.ShapeDtypeStruct((total, lanes+2*HDIM), jnp.bfloat16),
        scratch_shapes=[pltpu.VMEM((total,HDIM), jnp.bfloat16), pltpu.VMEM((HDIM,total), jnp.bfloat16), pltpu.VMEM((total,HDIM), jnp.bfloat16),
                        pltpu.VMEM((HDIM,width), jnp.float32), pltpu.VMEM((total,HDIM), jnp.float32), pltpu.VMEM((total,HDIM), jnp.float32)],
        compiler_params=pltpu.CompilerParams(dimension_semantics=("arbitrary",)),
        name="attend_backward",
    )(qkv, grad, flat, lse, cosine, sine)


def expert_kernel(
    parts, rows, width, experts, steps, chained, index_ref, *refs
):
    blocks = refs[:parts]
    grads = refs[parts : 2 * parts]
    router_ref, lin_ref, down_ref = refs[2 * parts : 2 * parts + 3]
    refs = refs[2 * parts + 3 + (4 if chained else 0) :]
    mixed_refs, back_refs, refs = refs[:parts], refs[parts : 2 * parts], refs[2 * parts :]
    rows_ref, grads_ref, d_lin_ref, hidden_ref = refs[:4]
    gates_sc, d_gates_sc, mixed_sc, back_sc = refs[4:]
    part = rows // parts
    units = down_ref.shape[1]
    step = pl.program_id(0)
    lane = lax.broadcasted_iota(jnp.int32, (rows, LANES), 1)

    @pl.when(step == 0)
    def _():
        for k in range(parts):
            here = pl.ds(k * part, part)
            rows_ref[here, :] = blocks[k][...]
            grads_ref[here, :] = grads[k][:, :width]
            logits = jnp.dot(blocks[k][...], router_ref[...], preferred_element_type=jnp.float32)
            logits = jnp.where(grads[k][:, width:].astype(jnp.float32) > 0.5, logits, -1e30)
            weight = jnp.exp(logits - jnp.max(logits, axis=1, keepdims=True))
            gates_sc[here, :] = weight / jnp.sum(weight, axis=1, keepdims=True)
        d_gates_sc[...] = jnp.zeros_like(d_gates_sc)

    expert = index_ref[step]
    own = lane == expert
    gate = jnp.sum(jnp.where(own, gates_sc[...], 0.0), axis=1, keepdims=True)
    block = rows_ref[...]
    lin = jnp.dot(block, lin_ref[0], preferred_element_type=jnp.float32)
    gate_lin, up_lin = lin[:, :units], lin[:, units:]
    d_hidden = matmul_nt(grads_ref[...], down_ref[0])
    sigma = 1.0 / (1.0 + jnp.exp(-gate_lin))
    active = gate_lin * sigma
    hidden = active * up_lin
    d_gates_sc[...] += jnp.where(own, jnp.sum(hidden * d_hidden, axis=1, keepdims=True), 0.0)
    hidden = (gate * hidden).astype(jnp.bfloat16)
    d_hidden = gate * d_hidden
    slope = sigma + active - active * sigma
    d_gate = (d_hidden * up_lin * slope).astype(jnp.bfloat16)
    d_up = (d_hidden * active).astype(jnp.bfloat16)
    hidden_ref[...] = hidden
    d_lin = jnp.concatenate([d_gate, d_up], axis=1)
    d_lin_ref[...] = d_lin
    mixed = jnp.dot(hidden, down_ref[0], preferred_element_type=jnp.float32)
    back = matmul_nt(d_lin, lin_ref[0])

    @pl.when(step == 0)
    def _():
        mixed_sc[...] = mixed
        back_sc[...] = back

    @pl.when(step > 0)
    def _():
        mixed_sc[...] += mixed
        back_sc[...] += back

    @pl.when(step == steps - 1)
    def _():
        d_gates = d_gates_sc[...]
        high = d_gates.astype(jnp.bfloat16).astype(jnp.float32)
        low = pltpu.roll(d_gates - high, experts, 1)
        d_gates = jnp.where(lane < experts, high, low).astype(jnp.bfloat16)
        for k in range(parts):
            here = slice(k * part, (k + 1) * part)
            mixed_refs[k][...] = mixed_sc[here, :].astype(jnp.bfloat16)
            back_refs[k][:, :width] = back_sc[here, :].astype(jnp.bfloat16)
            back_refs[k][:, width:] = d_gates[here]


def expert_rows(index, experts, blocks, grads, router, lin, down, slot, total, buffers):
    parts = len(blocks)
    part, width = blocks[0].shape
    rows = parts * part
    units = down.shape[1]
    steps = 2
    whole = lambda *shape: pl.BlockSpec(shape, lambda i, ids: (0,) * len(shape))
    columns = lambda count: pl.BlockSpec((rows, count), lambda i, ids: (slot, i))
    kept = pl.BlockSpec((rows, width), lambda i, ids: (slot, 0))
    chained = buffers is not None
    shapes = [
        *[jax.ShapeDtypeStruct((part, width), jnp.bfloat16)] * parts,
        *[jax.ShapeDtypeStruct((part, width + LANES), jnp.bfloat16)] * parts,
        jax.ShapeDtypeStruct((total, width), jnp.bfloat16),
        jax.ShapeDtypeStruct((total, width), jnp.bfloat16),
        jax.ShapeDtypeStruct((total, 4 * units), jnp.bfloat16),
        jax.ShapeDtypeStruct((total, 2 * units), jnp.bfloat16),
    ]
    inputs = [index, *blocks, *grads, router, lin, down] + (list(buffers) if chained else [])
    first = 1 + 2 * parts + 3
    results = pl.pallas_call(
        functools.partial(expert_kernel, parts, rows, width, experts, steps, chained),
        grid_spec=pltpu.PrefetchScalarGridSpec(
            num_scalar_prefetch=1,
            grid=(steps,),
            in_specs=[whole(part, width)] * parts
            + [whole(part, width + LANES)] * parts
            + [
                whole(width, LANES),
                pl.BlockSpec((1, width, 2 * units), lambda i, ids: (i, 0, 0)),
                pl.BlockSpec((1, units, width), lambda i, ids: (i, 0, 0)),
            ]
            + ([pl.BlockSpec(memory_space=pl.ANY)] * 4 if chained else []),
            out_specs=[
                *[whole(part, width)] * parts,
                *[whole(part, width + LANES)] * parts,
                kept,
                kept,
                columns(2 * units),
                columns(units),
            ],
            scratch_shapes=[
                pltpu.VMEM((rows, LANES), jnp.float32),
                pltpu.VMEM((rows, LANES), jnp.float32),
                pltpu.VMEM((rows, width), jnp.float32),
                pltpu.VMEM((rows, width), jnp.float32),
            ],
        ),
        out_shape=shapes,
        input_output_aliases={first + k: 2 * parts + k for k in range(4)} if chained else {},
        compiler_params=pltpu.CompilerParams(dimension_semantics=("arbitrary",)),
        cost_estimate=pl.CostEstimate(
            flops=rows * width * units * 24,
            bytes_accessed=12 * width * units + 20 * rows * width,
            transcendentals=rows * units * 2,
        ),
        name="expert_rows",
    )(*inputs)
    return results[:parts], results[parts : 2 * parts], results[2 * parts :]


def gather_dense(values):
    return lax.all_gather(values, ("head", "blk"), axis=0, tiled=True)


def exchange(values):
    return lax.all_to_all(values, "blk", split_axis=0, concat_axis=0, tiled=True)


def from_heads(values):
    heads = lax.axis_size("head")
    return [
        lax.ppermute(values, "head", [(k, (k + turn) % heads) for k in range(heads)])
        for turn in range(1, heads)
    ]


def partner(values):
    count = lax.axis_size("blk")
    return lax.ppermute(values, "blk", [(k, k ^ 1) for k in range(count)])


def after(values, *earlier):
    return lax.optimization_barrier((values, earlier))[0]


def ring_order():
    half = lax.axis_size("blk") // 4
    return [2 * k for k in range(half)] + [2 * k + 1 for k in reversed(range(half))]


def ring_steps():
    order = ring_order()
    onward, back = [], []
    for place, chip in enumerate(order):
        following = order[(place + 1) % len(order)]
        for core in range(2):
            onward.append((2 * chip + core, 2 * following + core))
            back.append((2 * following + core, 2 * chip + core))
    send_on = lambda values: lax.ppermute(values, "blk", onward)
    send_back = lambda values: lax.ppermute(values, "blk", back)
    return len(order), send_on, send_back


def ring_gather(values):
    length, send_on, send_back = ring_steps()
    half = values.shape[0] // 2
    behind = ahead = values
    pairs = []
    for _ in range(length // 2 - 1):
        behind, ahead = send_on(behind), send_back(ahead)
        pairs.append((behind, ahead))
    behind, ahead = behind[:half], ahead[half:]
    return pairs, (send_on(behind), send_back(ahead))


class RingSum:
    def __init__(self, own, pairs, opposite, label, axis=0):
        _, self.send_on, self.send_back = ring_steps()
        self.own, self.pairs, self.label = own, list(reversed(pairs)), label
        self.onward, self.back = opposite
        self.axis = axis
        self.hop = 0

    def send(self, *hold):
        if self.hop > 0:
            behind, ahead = self.pairs[self.hop - 1]
            self.onward, self.back = self.onward + ahead, self.back + behind
        if hold:
            self.onward, self.back = after((self.onward, self.back), hold)
        self.onward, self.back = self.send_on(self.onward), self.send_back(self.back)
        return self

    def land(self, *filler):
        if filler:
            self.onward, self.back = after((self.onward, self.back), filler)
        if self.hop == 0:
            lengths = self.onward.shape[self.axis], self.back.shape[self.axis]
            spread = [(0, 0), (0, 0)]
            spread[self.axis] = (0, lengths[1])
            self.onward = jnp.pad(self.onward, spread)
            spread[self.axis] = (lengths[0], 0)
            self.back = jnp.pad(self.back, spread)
        self.hop += 1
        return self

    def total(self):
        while self.hop <= len(self.pairs):
            self.send().land()
        wide = self.own.astype(jnp.float32)
        return wide + self.onward.astype(jnp.float32) + self.back.astype(jnp.float32)


def head_share(values):
    heads, rows = lax.axis_size("head"), values.shape[0] // lax.axis_size("head")
    head = lax.axis_index("head")
    start = (0,) * (values.ndim - 1)
    share = lambda turn: lax.dynamic_slice(
        values, ((head + turn) % heads * rows, *start), (rows, *values.shape[1:])
    )
    result = share(0).astype(jnp.float32)
    for turn in range(1, heads):
        moved = [(k, (k + turn) % heads) for k in range(heads)]
        other = lax.ppermute(share(turn), "head", moved)
        result = result + other.astype(jnp.float32)
    return result


class DenseSum:
    def __init__(self, values, label, heads_first=False):
        self.heads = lax.axis_size("head")
        self.chips = lax.axis_size("blk") // 2
        self.rows = values.shape[0] // (2 * self.heads * self.chips)
        self.label, self.heads_first = label, heads_first
        self.index = lax.axis_index("blk")
        self.mine = self.core_sum(values)

    def core_sum(self, values):
        grid = values.reshape(self.heads, self.chips, 2, self.rows, values.shape[1])
        even = self.index % 2 == 0
        swapped = partner(jnp.where(even, grid[:, :, 1], grid[:, :, 0]))
        return jnp.where(even, grid[:, :, 0], grid[:, :, 1]) + swapped

    def append(self, values):
        self.mine = jnp.concatenate([self.mine, self.core_sum(values)], axis=3)

    def block(self, offset):
        chip, turns = self.index // 2, self.chips // 2
        place = jnp.where(chip % 2 == 0, chip // 2, self.chips - 1 - chip // 2)
        target = (place + offset) % self.chips
        chip = jnp.where(target < turns, 2 * target, 2 * (self.chips - 1 - target) + 1)
        heads, columns = self.mine.shape[0], self.mine.shape[3]
        piece = lax.dynamic_slice(self.mine, (0, chip, 0, 0), (heads, 1, self.rows, columns))
        return piece.reshape(heads * self.rows, columns)

    def ring(self):
        if self.heads_first:
            self.mine = head_share(self.mine).astype(jnp.bfloat16)
        pairs = [(self.block(-k), self.block(k)) for k in range(1, self.chips // 2)]
        opposite = self.block(self.chips // 2)
        axis = 1 if self.heads_first else 0
        half = opposite.shape[1] // 256 * 128 if axis else opposite.shape[0] // 2
        opposite = jnp.split(opposite, [half], axis=axis)
        return RingSum(self.block(0), pairs, opposite, self.label, axis)

    def finish(self, total):
        return total if self.heads_first else head_share(total.astype(jnp.bfloat16))

    def total(self):
        return self.finish(self.ring().total())


def project_kernel(shard, groups, rows_ref, weight_ref, cosine_ref, sine_ref, out_ref):
    values = jnp.dot(rows_ref[...], weight_ref[...], preferred_element_type=jnp.float32)
    width = values.shape[1]
    lane = lax.broadcasted_iota(jnp.int32, (shard, width), 1)
    first = lane % HDIM < HDIM // 2
    span = width // groups
    for s in range(values.shape[0] // shard):
        part = values[s * shard : (s + 1) * shard]
        turned = jnp.where(
            first, pltpu.roll(part, width - HDIM // 2, 1), pltpu.roll(part, HDIM // 2, 1)
        )
        part = (part * cosine_ref[...] + turned * sine_ref[...]).astype(jnp.bfloat16)
        for k in range(groups):
            out_ref[s, k] = part[:, k * span : (k + 1) * span]


def project(normed, weights, positions, groups, group):
    rows, width = normed.shape
    shard = positions.shape[0]
    span = (group + 2) * HDIM
    cosine, sine = rope_tables(positions, HDIM // 2)
    cosine = jnp.concatenate([cosine, cosine], axis=1)
    sine = jnp.concatenate([-sine, sine], axis=1)
    plain = (jnp.ones((shard, HDIM), jnp.float32), jnp.zeros((shard, HDIM), jnp.float32))
    cosine = jnp.concatenate(([cosine] * (group + 1) + [plain[0]]) * 2, axis=1)
    sine = jnp.concatenate(([sine] * (group + 1) + [plain[1]]) * 2, axis=1)
    table = pl.BlockSpec((shard, 2 * span), lambda j: (0, 0))
    return pl.pallas_call(
        functools.partial(project_kernel, shard, 2),
        grid=(groups // 2,),
        in_specs=[
            pl.BlockSpec((rows, width), lambda j: (0, 0)),
            pl.BlockSpec((width, 2 * span), lambda j: (0, j)),
            table,
            table,
        ],
        out_specs=pl.BlockSpec((rows // shard, 2, shard, span), lambda j: (0, j, 0, 0)),
        out_shape=jax.ShapeDtypeStruct((rows // shard, groups, shard, span), jnp.bfloat16),
        compiler_params=pltpu.CompilerParams(dimension_semantics=("arbitrary",)),
        cost_estimate=pl.CostEstimate(
            flops=2 * rows * width * groups * span,
            bytes_accessed=2 * width * groups * span,
            transcendentals=0,
        ),
        name="project",
    )(normed, weights, cosine, sine)


def with_lanes(values, extra):
    rows = values.shape[0]
    spare = jnp.zeros((rows, LANES - extra.shape[1]), values.dtype)
    return jnp.concatenate([values, extra.astype(values.dtype), spare], axis=1)


def add_lanes(padded, extra):
    _, columns = padded.shape
    spread = ((0, 0), (columns - LANES, LANES - extra.shape[1]))
    return padded + jnp.pad(extra, spread)


def layer(
    tokens,
    gain_attn,
    w_query,
    w_key,
    w_value,
    w_out,
    gain_moe,
    w_router,
    w_gate,
    w_up,
    w_down,
    routes,
    grad_out,
):
    seq_local, shard, width = tokens.shape
    token_rows = seq_local * shard
    blk_index = lax.axis_index("blk")
    blk_count = lax.axis_size("blk")
    seq_total = blk_count * shard
    part_rows = w_query.shape[0]
    groups = w_key.shape[1] // HDIM
    group = w_query.shape[1] // w_key.shape[1]
    lanes = group * HDIM
    span = lanes + 2 * HDIM
    pairs = seq_local * groups
    copies = blk_count // pairs
    experts = w_router.shape[1]
    units = w_gate.shape[2]

    mixed_weights = jnp.concatenate(
        [
            w_query.reshape(part_rows, groups, lanes),
            w_key.reshape(part_rows, groups, HDIM),
            w_value.reshape(part_rows, groups, HDIM),
        ],
        axis=2,
    ).reshape(part_rows, groups * span)
    full_mixed = gather_dense(with_lanes(mixed_weights, gain_attn[:, None]))
    full_out = gather_dense(
        with_lanes(w_out, jnp.concatenate([w_router, gain_moe[:, None]], axis=1))
    )
    router = full_out[:, width:]
    full_router = router[:, :experts]
    router = jnp.where(jnp.arange(LANES)[None, :] < experts, router, jnp.bfloat16(0.0))
    gain_first = full_mixed[:, groups * span].astype(jnp.float32)
    gain_second = full_out[:, width + experts].astype(jnp.float32)

    expert_ids = jnp.arange(experts, dtype=jnp.int32)
    routes_tok = routes.reshape(token_rows, TOP)
    chosen = jnp.any(routes_tok[:, :, None] == expert_ids[None, None, :], axis=1)
    d_out = grad_out.reshape(token_rows, width)
    grads_own = with_lanes(d_out.astype(jnp.bfloat16), chosen)
    grads_pairs, grads_opposite = ring_gather(grads_own)
    full_mixed = after(full_mixed, grads_pairs[:2])
    w_lin = jnp.concatenate([w_gate, w_up], axis=2)
    both_lin = jnp.concatenate([w_lin, partner(w_lin)], axis=0)
    both_down = jnp.concatenate([w_down, partner(w_down)], axis=0)

    residual = tokens.astype(jnp.float32).reshape(token_rows, width)
    inverse_one = rms_scale(residual)
    normed = (residual * inverse_one * gain_first).astype(jnp.bfloat16)
    positions = blk_index * shard + jnp.arange(shard, dtype=jnp.int32)
    packed = project(normed, full_mixed, positions, groups, group)

    def to_pairs(values, columns):
        values = values.reshape(pairs, 1, shard, columns)
        values = jnp.broadcast_to(values, (pairs, copies, shard, columns))
        return exchange(values.reshape(blk_count, shard, columns)).reshape(seq_total, columns)

    def to_tokens(values, columns):
        values = exchange(values.reshape(blk_count, shard, columns))
        values = values.reshape(pairs, copies, shard, columns)[:, 0]
        values = values.reshape(seq_local, groups, shard, columns).transpose(0, 2, 1, 3)
        return values.reshape(token_rows, groups * columns)

    pair_qkv = to_pairs(packed, span)
    pair_attended, flat, log_total = attend_forward(pair_qkv, group)
    attended = to_tokens(pair_attended, lanes)
    middle = residual + matmul(attended, full_out)[:, :width]
    inverse_two = rms_scale(middle)
    normed_two = (middle * inverse_two * gain_second).astype(jnp.bfloat16)
    logits = matmul(normed_two, full_router)
    gates = jax.nn.softmax(jnp.where(chosen, logits, -jnp.inf), axis=-1)

    blocks_pairs, blocks_opposite = ring_gather(normed_two)
    total = blk_count // 2 * token_rows
    ids = jnp.stack([blk_index, blk_index ^ 1]).astype(jnp.int32)

    def apply_experts(blocks, grads, slot, buffers):
        return expert_rows(
            ids, experts, blocks, grads, router, both_lin, both_down, slot, total, buffers
        )

    ring_pairs = len(blocks_pairs)
    mixed_own, back_own, buffers = apply_experts(
        [normed_two], [grads_own], 2 * ring_pairs, None
    )
    mixed_pairs, back_pairs = [], []
    for k in range(ring_pairs):
        mixed, back, buffers = apply_experts(blocks_pairs[k], grads_pairs[k], k, buffers)
        mixed_pairs.append(mixed)
        back_pairs.append(back)
    mixed_opposite, back_opposite, buffers = apply_experts(
        blocks_opposite, grads_opposite, 2 * ring_pairs + 1, buffers
    )
    rows_all, grads_all, d_lin_all, hidden_all = buffers
    back_ring = RingSum(back_own[0], back_pairs, back_opposite, "back")
    others = [
        matmul_tn(rows_all, d_lin_all[:, 2 * units :]).astype(jnp.bfloat16),
        matmul_tn(hidden_all[:, units:], grads_all).astype(jnp.bfloat16),
    ]
    others = [partner(part) for part in others]
    mine = [
        matmul_tn(rows_all, d_lin_all[:, : 2 * units]) + others[0].astype(jnp.float32),
        matmul_tn(hidden_all[:, :units], grads_all) + others[1].astype(jnp.float32),
    ]
    mine = [part.astype(jnp.bfloat16) for part in mine]
    back_sum = back_ring.total()
    theirs = [from_heads(part) for part in mine]
    mixed_ring = RingSum(mixed_own[0], mixed_pairs, mixed_opposite, "mixed")
    (mixed_ring.onward, mixed_ring.back), back_sum = lax.optimization_barrier(
        ((mixed_ring.onward, mixed_ring.back), back_sum)
    )
    mixed_ring.send()

    d_gates = back_sum[:, width : width + experts] + back_sum[:, width + experts : width + 2 * experts]
    d_logits = gates * (d_gates - jnp.sum(gates * d_gates, axis=-1, keepdims=True))
    grad_router = jnp.dot(normed_two.astype(jnp.float32).T, d_logits, precision=highest)
    d_normed_two = back_sum[:, :width] + jnp.dot(
        d_logits, full_router.astype(jnp.float32).T, precision=highest
    )
    d_mid_norm, grad_gain_second = norm_back(middle, inverse_two, gain_second, d_normed_two)
    d_mid = d_out + d_mid_norm
    d_branch = jnp.pad(d_mid.astype(jnp.bfloat16), ((0, 0), (0, LANES)))
    d_attended = matmul_nt(d_branch, full_out).astype(jnp.bfloat16)
    early = add_lanes(
        matmul_tn(attended, d_branch),
        jnp.concatenate([grad_router, grad_gain_second[:, None]], axis=1),
    ).astype(jnp.bfloat16)
    mixed_ring.land()
    d_attended, early, mixed_ring.onward, mixed_ring.back = lax.optimization_barrier(
        (d_attended, early, mixed_ring.onward, mixed_ring.back)
    )
    pair_grad = to_pairs(
        d_attended.reshape(seq_local, shard, groups, lanes).transpose(0, 2, 1, 3), lanes
    )
    pair_grad, mixed_ring.onward, mixed_ring.back = lax.optimization_barrier(
        (pair_grad, mixed_ring.onward, mixed_ring.back)
    )
    mixed_ring.send()
    pair_cosine, pair_sine = rope_tables(jnp.arange(seq_total, dtype=jnp.int32), HDIM // 2)
    pair_d = attend_backward(
        pair_qkv, pair_grad, flat, log_total, pair_cosine.T, pair_sine.T, group
    )
    early = DenseSum(early, "early", True).total()
    mixed_ring.land()
    pair_d, mixed_ring.onward, mixed_ring.back = lax.optimization_barrier(
        (pair_d, mixed_ring.onward, mixed_ring.back)
    )
    mixed_ring.send()
    d_linear = to_tokens(pair_d, span)
    mixed_ring.land()
    d_linear, early = lax.optimization_barrier((d_linear, early))
    grad_mixed = matmul_tn(normed, d_linear).astype(jnp.bfloat16)
    late = DenseSum(grad_mixed, "late", True)
    d_normed = matmul_nt(jnp.pad(d_linear, ((0, 0), (0, LANES))), full_mixed)
    d_tok_norm, grad_gain_first = norm_back(residual, inverse_one, gain_first, d_normed)
    grad_tokens = (d_mid + d_tok_norm).reshape(seq_local, shard, width)
    late.append(jnp.pad(grad_gain_first[:, None].astype(jnp.bfloat16), ((0, 0), (0, LANES - 1))))
    late_ring = late.ring()
    sums = [
        functools.reduce(jnp.add, [v.astype(jnp.float32) for v in others], part.astype(jnp.float32))
        for part, others in zip(mine, theirs)
    ]
    grad_gate_sum, grad_up_sum = sums[0][:, :units], sums[0][:, units:]
    grad_down_sum = sums[1]
    out = (middle + mixed_ring.total()).reshape(seq_local, shard, width)
    late = late.finish(late_ring.total())
    late_mixed = late[:, : groups * span].reshape(part_rows, groups, span)
    return (
        out,
        grad_tokens,
        late[:, groups * span],
        late_mixed[:, :, :lanes].reshape(part_rows, -1),
        late_mixed[:, :, lanes : lanes + HDIM].reshape(part_rows, -1),
        late_mixed[:, :, lanes + HDIM :].reshape(part_rows, -1),
        early[:, :width],
        early[:, width + experts],
        early[:, width : width + experts],
        grad_gate_sum[None],
        grad_up_sum[None],
        grad_down_sum[None],
    )


def solution(mesh):
    placed = (
        P("head", "blk", None),
        P(("head", "blk")),
        P(("head", "blk"), None),
        P(("head", "blk"), None),
        P(("head", "blk"), None),
        P(("head", "blk"), None),
        P(("head", "blk")),
        P(("head", "blk"), None),
        P("blk", None, None),
        P("blk", None, None),
        P("blk", None, None),
        P("head", "blk", None),
        P("head", "blk", None),
    )
    return jax.shard_map(
        layer,
        mesh=mesh,
        in_specs=placed,
        out_specs=(
            P("head", "blk", None),
            P("head", "blk", None),
            P(("head", "blk")),
            P(("head", "blk"), None),
            P(("head", "blk"), None),
            P(("head", "blk"), None),
            P(("head", "blk"), None),
            P(("head", "blk")),
            P(("head", "blk"), None),
            P("blk", None, None),
            P("blk", None, None),
            P("blk", None, None),
        ),
        check_vma=False,
    )
```

```python
import functools

import jax
import jax.numpy as jnp
from jax import lax
from jax.experimental import pallas as pl
from jax.experimental.pallas import tpu as pltpu
from jax.sharding import PartitionSpec as P


HDIM = 64
TOP = 8
BLOCK = 256
LANES = 128

highest = lax.Precision.HIGHEST
theta_base = 10000.0
norm_eps = 1e-06


def rope_tables(positions, half_width):
    index_float = jnp.arange(half_width, dtype=jnp.float32)
    frequency = theta_base ** (-2.0 * index_float / (2 * half_width))
    angles = positions.astype(jnp.float32)[:, None] * frequency[None, :]
    return (jnp.cos(angles), jnp.sin(angles))


def rms_scale(values):
    return lax.rsqrt(jnp.mean(values * values, axis=-1, keepdims=True) + norm_eps)


def norm_back(values, inverse, gain, d_normed):
    unit_values = values * inverse
    scaled = d_normed * gain
    d_gain = jnp.sum(d_normed * unit_values, axis=0)
    d_values = inverse * (
        scaled - unit_values * jnp.mean(scaled * unit_values, axis=-1, keepdims=True)
    )
    return (d_values, d_gain)


def matmul(left, right):
    return jnp.dot(left, right, preferred_element_type=jnp.float32)


def matmul_nt(left, right):
    return lax.dot_general(left, right, (((1,), (1,)), ((), ())), preferred_element_type=jnp.float32)


def matmul_tn(left, right):
    return lax.dot_general(left, right, (((0,), (0,)), ((), ())), preferred_element_type=jnp.float32)


def wide(block, group):
    flipped = block.T
    return jnp.concatenate([flipped[h*HDIM:(h+1)*HDIM] for h in range(group)], axis=1)


def tall(block, group):
    return jnp.concatenate([block[:, h*HDIM:(h+1)*HDIM] for h in range(group)], axis=0)


def narrow(values, group, rows):
    return jnp.concatenate([values[:, h*rows:(h+1)*rows] for h in range(group)], axis=0).T


def forward_kernel(group, qkv_ref, att_ref, flat_ref, lse_ref, key_sc, val_sc, acc_sc):
    i = pl.program_id(0)
    lanes = group*HDIM

    @pl.when(i == 0)
    def _():
        key_sc[...] = qkv_ref[:, lanes:lanes+HDIM]
        val_sc[...] = qkv_ref[:, lanes+HDIM:lanes+2*HDIM].T

    rows = pl.ds(pl.multiple_of(i*BLOCK, BLOCK), BLOCK)
    query = wide(qkv_ref[rows, :lanes], group) * jnp.bfloat16(HDIM**-0.5)
    acc_sc[...] = jnp.zeros_like(acc_sc)

    def step(j, carry):
        top, total = carry
        here = pl.ds(pl.multiple_of(j*BLOCK, BLOCK), BLOCK)
        scores = jnp.dot(key_sc[here, :], query, preferred_element_type=jnp.float32)
        new_top = jnp.maximum(top, jnp.max(scores, axis=0, keepdims=True))
        probs = jnp.exp(scores - new_top)
        fade = jnp.exp(top - new_top)
        acc_sc[...] = acc_sc[...]*fade + jnp.dot(val_sc[:, here], probs.astype(jnp.bfloat16), preferred_element_type=jnp.float32)
        return new_top, total*fade + jnp.sum(probs, axis=0, keepdims=True)

    width = group*BLOCK
    top, total = lax.fori_loop(0, i+1, step, (jnp.full((1,width), -1e30, jnp.float32), jnp.zeros((1,width), jnp.float32)))
    result = acc_sc[...] / total
    flat_ref[0] = result
    att_ref[...] = narrow(result.astype(jnp.bfloat16), group, BLOCK)
    lse_ref[0] = top + jnp.log(total)


def attend_forward(qkv, group):
    total = qkv.shape[0]; steps = total//BLOCK; lanes = group*HDIM; width = group*BLOCK
    return pl.pallas_call(
        functools.partial(forward_kernel, group),
        grid=(steps,),
        in_specs=[pl.BlockSpec((total, lanes+2*HDIM), lambda i: (0,0))],
        out_specs=[pl.BlockSpec((BLOCK, lanes), lambda i: (i,0)),
                   pl.BlockSpec((1, HDIM, width), lambda i: (i,0,0)),
                   pl.BlockSpec((1,1,width), lambda i: (i,0,0))],
        out_shape=[jax.ShapeDtypeStruct((total, lanes), jnp.bfloat16),
                   jax.ShapeDtypeStruct((steps,HDIM,width), jnp.float32),
                   jax.ShapeDtypeStruct((steps,1,width), jnp.float32)],
        scratch_shapes=[pltpu.VMEM((total,HDIM), jnp.bfloat16), pltpu.VMEM((HDIM,total), jnp.bfloat16), pltpu.VMEM((HDIM,width), jnp.float32)],
        compiler_params=pltpu.CompilerParams(dimension_semantics=("arbitrary",)),
        name="attend_forward",
    )(qkv)


def unrotate(values, cosine, sine):
    a, b = values[:HDIM//2], values[HDIM//2:]
    return jnp.concatenate([a*cosine + b*sine, b*cosine - a*sine], axis=0)


def backward_kernel(group, steps, qkv_ref, grad_ref, flat_ref, lse_ref, cos_ref, sin_ref, out_ref, key_sc, keyt_sc, val_sc, dq_sc, dk_sc, dv_sc):
    i = pl.program_id(0)
    lanes = group*HDIM
    scale = HDIM**-0.5

    @pl.when(i == 0)
    def _():
        key = qkv_ref[:, lanes:lanes+HDIM]
        key_sc[...] = key
        keyt_sc[...] = key.T
        val_sc[...] = qkv_ref[:, lanes+HDIM:lanes+2*HDIM]
        dk_sc[...] = jnp.zeros_like(dk_sc)
        dv_sc[...] = jnp.zeros_like(dv_sc)

    rows = pl.ds(pl.multiple_of(i*BLOCK, BLOCK), BLOCK)
    block = qkv_ref[rows, :lanes] * jnp.bfloat16(scale)
    query_w, query_t = wide(block, group), tall(block, group)
    grad = grad_ref[...]
    grad_w, grad_t = wide(grad, group), tall(grad, group)
    lse = lse_ref[0]
    delta = jnp.sum(grad_w.astype(jnp.float32)*flat_ref[0], axis=0, keepdims=True)
    dq_sc[...] = jnp.zeros_like(dq_sc)

    def step(j, carry):
        here = pl.ds(pl.multiple_of(j*BLOCK, BLOCK), BLOCK)
        scores = jnp.dot(key_sc[here,:], query_w, preferred_element_type=jnp.float32)
        probs = jnp.exp(scores - lse)
        dprobs = jnp.dot(val_sc[here,:], grad_w, preferred_element_type=jnp.float32)
        dv_sc[here,:] += jnp.dot(probs.astype(jnp.bfloat16), grad_t, preferred_element_type=jnp.float32)
        dscores = (probs*(dprobs-delta)).astype(jnp.bfloat16)
        dk_sc[here,:] += jnp.dot(dscores, query_t, preferred_element_type=jnp.float32)
        dq_sc[...] += jnp.dot(keyt_sc[:,here], dscores, preferred_element_type=jnp.float32)
        return carry

    lax.fori_loop(0, i+1, step, 0)
    cosine, sine = cos_ref[:, rows], sin_ref[:, rows]
    pieces = [unrotate(dq_sc[:, h*BLOCK:(h+1)*BLOCK]*scale, cosine, sine).astype(jnp.bfloat16) for h in range(group)]
    out_ref[rows, :lanes] = jnp.concatenate(pieces, axis=0).T

    @pl.when(i == steps-1)
    def _():
        def finish(j, carry):
            here = pl.ds(pl.multiple_of(j*BLOCK, BLOCK), BLOCK)
            turned = unrotate(dk_sc[here,:].T, cos_ref[:,here], sin_ref[:,here]).astype(jnp.bfloat16)
            both = jnp.concatenate([turned, dv_sc[here,:].astype(jnp.bfloat16).T], axis=0).T
            out_ref[here, lanes:lanes+2*HDIM] = both
            return carry

        lax.fori_loop(0, steps, finish, 0)


def attend_backward(qkv, grad, flat, lse, cosine, sine, group):
    total = qkv.shape[0]; steps = total//BLOCK; lanes = group*HDIM; width = group*BLOCK
    return pl.pallas_call(
        functools.partial(backward_kernel, group, steps),
        grid=(steps,),
        in_specs=[pl.BlockSpec((total, lanes+2*HDIM), lambda i: (0,0)),
                  pl.BlockSpec((BLOCK, lanes), lambda i: (i,0)),
                  pl.BlockSpec((1, HDIM, width), lambda i: (i,0,0)),
                  pl.BlockSpec((1,1,width), lambda i: (i,0,0)),
                  pl.BlockSpec((HDIM//2, total), lambda i: (0,0)),
                  pl.BlockSpec((HDIM//2, total), lambda i: (0,0))],
        out_specs=pl.BlockSpec((total, lanes+2*HDIM), lambda i: (0,0)),
        out_shape=jax.ShapeDtypeStruct((total, lanes+2*HDIM), jnp.bfloat16),
        scratch_shapes=[pltpu.VMEM((total,HDIM), jnp.bfloat16), pltpu.VMEM((HDIM,total), jnp.bfloat16), pltpu.VMEM((total,HDIM), jnp.bfloat16),
                        pltpu.VMEM((HDIM,width), jnp.float32), pltpu.VMEM((total,HDIM), jnp.float32), pltpu.VMEM((total,HDIM), jnp.float32)],
        compiler_params=pltpu.CompilerParams(dimension_semantics=("arbitrary",)),
        name="attend_backward",
    )(qkv, grad, flat, lse, cosine, sine)


def expert_kernel(
    parts, rows, width, experts, steps, chained, index_ref, *refs
):
    blocks = refs[:parts]
    grads = refs[parts : 2 * parts]
    router_ref, lin_ref, down_ref = refs[2 * parts : 2 * parts + 3]
    refs = refs[2 * parts + 3 + (4 if chained else 0) :]
    mixed_refs, back_refs, refs = refs[:parts], refs[parts : 2 * parts], refs[2 * parts :]
    rows_ref, grads_ref, d_lin_ref, hidden_ref = refs[:4]
    gates_sc, d_gates_sc, mixed_sc, back_sc = refs[4:]
    part = rows // parts
    units = down_ref.shape[1]
    step = pl.program_id(0)
    lane = lax.broadcasted_iota(jnp.int32, (rows, LANES), 1)

    @pl.when(step == 0)
    def _():
        for k in range(parts):
            here = pl.ds(k * part, part)
            rows_ref[here, :] = blocks[k][...]
            grads_ref[here, :] = grads[k][:, :width]
            logits = jnp.dot(blocks[k][...], router_ref[...], preferred_element_type=jnp.float32)
            logits = jnp.where(grads[k][:, width:].astype(jnp.float32) > 0.5, logits, -1e30)
            weight = jnp.exp(logits - jnp.max(logits, axis=1, keepdims=True))
            gates_sc[here, :] = weight / jnp.sum(weight, axis=1, keepdims=True)
        d_gates_sc[...] = jnp.zeros_like(d_gates_sc)

    expert = index_ref[step]
    own = lane == expert
    gate = jnp.sum(jnp.where(own, gates_sc[...], 0.0), axis=1, keepdims=True)
    block = rows_ref[...]
    lin = jnp.dot(block, lin_ref[0], preferred_element_type=jnp.float32)
    gate_lin, up_lin = lin[:, :units], lin[:, units:]
    d_hidden = matmul_nt(grads_ref[...], down_ref[0])
    sigma = 1.0 / (1.0 + jnp.exp(-gate_lin))
    active = gate_lin * sigma
    hidden = active * up_lin
    d_gates_sc[...] += jnp.where(own, jnp.sum(hidden * d_hidden, axis=1, keepdims=True), 0.0)
    hidden = (gate * hidden).astype(jnp.bfloat16)
    d_hidden = gate * d_hidden
    slope = sigma + active - active * sigma
    d_gate = (d_hidden * up_lin * slope).astype(jnp.bfloat16)
    d_up = (d_hidden * active).astype(jnp.bfloat16)
    hidden_ref[...] = hidden
    d_lin = jnp.concatenate([d_gate, d_up], axis=1)
    d_lin_ref[...] = d_lin
    mixed = jnp.dot(hidden, down_ref[0], preferred_element_type=jnp.float32)
    back = matmul_nt(d_lin, lin_ref[0])

    @pl.when(step == 0)
    def _():
        mixed_sc[...] = mixed
        back_sc[...] = back

    @pl.when(step > 0)
    def _():
        mixed_sc[...] += mixed
        back_sc[...] += back

    @pl.when(step == steps - 1)
    def _():
        d_gates = d_gates_sc[...]
        high = d_gates.astype(jnp.bfloat16).astype(jnp.float32)
        low = pltpu.roll(d_gates - high, experts, 1)
        d_gates = jnp.where(lane < experts, high, low).astype(jnp.bfloat16)
        for k in range(parts):
            here = slice(k * part, (k + 1) * part)
            mixed_refs[k][...] = mixed_sc[here, :].astype(jnp.bfloat16)
            back_refs[k][:, :width] = back_sc[here, :].astype(jnp.bfloat16)
            back_refs[k][:, width:] = d_gates[here]


def expert_rows(index, experts, blocks, grads, router, lin, down, slot, total, buffers):
    parts = len(blocks)
    part, width = blocks[0].shape
    rows = parts * part
    units = down.shape[1]
    steps = 2
    whole = lambda *shape: pl.BlockSpec(shape, lambda i, ids: (0,) * len(shape))
    columns = lambda count: pl.BlockSpec((rows, count), lambda i, ids: (slot, i))
    kept = pl.BlockSpec((rows, width), lambda i, ids: (slot, 0))
    chained = buffers is not None
    shapes = [
        *[jax.ShapeDtypeStruct((part, width), jnp.bfloat16)] * parts,
        *[jax.ShapeDtypeStruct((part, width + LANES), jnp.bfloat16)] * parts,
        jax.ShapeDtypeStruct((total, width), jnp.bfloat16),
        jax.ShapeDtypeStruct((total, width), jnp.bfloat16),
        jax.ShapeDtypeStruct((total, 4 * units), jnp.bfloat16),
        jax.ShapeDtypeStruct((total, 2 * units), jnp.bfloat16),
    ]
    inputs = [index, *blocks, *grads, router, lin, down] + (list(buffers) if chained else [])
    first = 1 + 2 * parts + 3
    results = pl.pallas_call(
        functools.partial(expert_kernel, parts, rows, width, experts, steps, chained),
        grid_spec=pltpu.PrefetchScalarGridSpec(
            num_scalar_prefetch=1,
            grid=(steps,),
            in_specs=[whole(part, width)] * parts
            + [whole(part, width + LANES)] * parts
            + [
                whole(width, LANES),
                pl.BlockSpec((1, width, 2 * units), lambda i, ids: (i, 0, 0)),
                pl.BlockSpec((1, units, width), lambda i, ids: (i, 0, 0)),
            ]
            + ([pl.BlockSpec(memory_space=pl.ANY)] * 4 if chained else []),
            out_specs=[
                *[whole(part, width)] * parts,
                *[whole(part, width + LANES)] * parts,
                kept,
                kept,
                columns(2 * units),
                columns(units),
            ],
            scratch_shapes=[
                pltpu.VMEM((rows, LANES), jnp.float32),
                pltpu.VMEM((rows, LANES), jnp.float32),
                pltpu.VMEM((rows, width), jnp.float32),
                pltpu.VMEM((rows, width), jnp.float32),
            ],
        ),
        out_shape=shapes,
        input_output_aliases={first + k: 2 * parts + k for k in range(4)} if chained else {},
        compiler_params=pltpu.CompilerParams(dimension_semantics=("arbitrary",)),
        cost_estimate=pl.CostEstimate(
            flops=rows * width * units * 24,
            bytes_accessed=12 * width * units + 20 * rows * width,
            transcendentals=rows * units * 2,
        ),
        name="expert_rows",
    )(*inputs)
    return results[:parts], results[parts : 2 * parts], results[2 * parts :]


def exchange(values):
    return lax.all_to_all(values, "blk", split_axis=0, concat_axis=0, tiled=True)


def from_heads(values):
    heads = lax.axis_size("head")
    return [
        lax.ppermute(values, "head", [(k, (k + turn) % heads) for k in range(heads)])
        for turn in range(1, heads)
    ]


def partner(values):
    count = lax.axis_size("blk")
    return lax.ppermute(values, "blk", [(k, k ^ 1) for k in range(count)])


def after(values, *earlier):
    return lax.optimization_barrier((values, earlier))[0]


def ring_order():
    half = lax.axis_size("blk") // 4
    return [2 * k for k in range(half)] + [2 * k + 1 for k in reversed(range(half))]


def ring_steps():
    order = ring_order()
    onward, back = [], []
    for place, chip in enumerate(order):
        following = order[(place + 1) % len(order)]
        for core in range(2):
            onward.append((2 * chip + core, 2 * following + core))
            back.append((2 * following + core, 2 * chip + core))
    send_on = lambda values: lax.ppermute(values, "blk", onward)
    send_back = lambda values: lax.ppermute(values, "blk", back)
    return len(order), send_on, send_back


def ring_gather(values, axis=0):
    length, send_on, send_back = ring_steps()
    half = values.shape[axis] // 256 * 128
    behind = ahead = values
    pairs = []
    for _ in range(length // 2 - 1):
        behind, ahead = send_on(behind), send_back(ahead)
        pairs.append((behind, ahead))
    behind = lax.slice_in_dim(behind, 0, half, axis=axis)
    ahead = lax.slice_in_dim(ahead, half, ahead.shape[axis], axis=axis)
    return pairs, (send_on(behind), send_back(ahead))


class RingSum:
    def __init__(self, own, pairs, opposite, label, axis=0):
        _, self.send_on, self.send_back = ring_steps()
        self.own, self.pairs, self.label = own, list(reversed(pairs)), label
        self.onward, self.back = opposite
        self.axis = axis
        self.hop = 0

    def send(self, *hold):
        if self.hop > 0:
            behind, ahead = self.pairs[self.hop - 1]
            self.onward, self.back = self.onward + ahead, self.back + behind
        if hold:
            self.onward, self.back = after((self.onward, self.back), hold)
        self.onward, self.back = self.send_on(self.onward), self.send_back(self.back)
        return self

    def land(self, *filler):
        if filler:
            self.onward, self.back = after((self.onward, self.back), filler)
        if self.hop == 0:
            lengths = self.onward.shape[self.axis], self.back.shape[self.axis]
            spread = [(0, 0), (0, 0)]
            spread[self.axis] = (0, lengths[1])
            self.onward = jnp.pad(self.onward, spread)
            spread[self.axis] = (lengths[0], 0)
            self.back = jnp.pad(self.back, spread)
        self.hop += 1
        return self

    def total(self):
        while self.hop <= len(self.pairs):
            self.send().land()
        wide = self.own.astype(jnp.float32)
        return wide + self.onward.astype(jnp.float32) + self.back.astype(jnp.float32)


def ring_chip(offset):
    chips = lax.axis_size("blk") // 2
    chip = lax.axis_index("blk") // 2
    place = jnp.where(chip % 2 == 0, chip // 2, chips - 1 - chip // 2)
    target = (place + offset) % chips
    return jnp.where(target < chips // 2, 2 * target, 2 * (chips - 1 - target) + 1)


def all_heads(values):
    heads = lax.axis_size("head")
    head = lax.axis_index("head")
    place = lambda found, at: lax.dynamic_update_index_in_dim(result, found, at, 0)
    result = jnp.zeros((heads, *values.shape), values.dtype)
    result = place(values, head)
    for turn in range(1, heads):
        other = lax.ppermute(
            values, "head", [(k, (k + turn) % heads) for k in range(heads)]
        )
        result = place(other, (head - turn) % heads)
    return result


def ring_pieces(block, axis):
    pairs, opposite = ring_gather(block, axis)
    found = [(0, block)]
    for k, (behind, ahead) in enumerate(pairs):
        found += [(-k - 1, behind), (k + 1, ahead)]
    return found + [(len(pairs) + 1, jnp.concatenate(opposite, axis=axis))]


def dense_gather(shard):
    chips = lax.axis_size("blk") // 2
    heads = lax.axis_size("head")
    core = lax.axis_index("blk") % 2
    rows, columns = shard.shape
    block = all_heads(shard).reshape(heads * rows, columns)
    full = jnp.zeros((heads, chips, 2, rows, columns), shard.dtype)
    for offset, piece in ring_pieces(block, 1):
        for side, part in ((core, piece), (1 - core, partner(piece))):
            full = lax.dynamic_update_slice(
                full, part.reshape(heads, 1, 1, rows, columns), (0, ring_chip(offset), side, 0, 0)
            )
    return full.reshape(-1, columns)


def dense_gather_late(shard):
    chips = lax.axis_size("blk") // 2
    rows, columns = shard.shape
    found = jnp.zeros((chips, rows, columns), shard.dtype)
    for offset, piece in ring_pieces(shard, 1):
        found = lax.dynamic_update_slice(found, piece[None], (ring_chip(offset), 0, 0))
    found = all_heads(found)
    other = partner(found)
    even = lax.axis_index("blk") % 2 == 0
    pair = [jnp.where(even, found, other), jnp.where(even, other, found)]
    return jnp.stack(pair, axis=2).reshape(-1, columns)


def head_share(values):
    heads, rows = lax.axis_size("head"), values.shape[0] // lax.axis_size("head")
    head = lax.axis_index("head")
    start = (0,) * (values.ndim - 1)
    share = lambda turn: lax.dynamic_slice(
        values, ((head + turn) % heads * rows, *start), (rows, *values.shape[1:])
    )
    result = share(0).astype(jnp.float32)
    for turn in range(1, heads):
        moved = [(k, (k + turn) % heads) for k in range(heads)]
        other = lax.ppermute(share(turn), "head", moved)
        result = result + other.astype(jnp.float32)
    return result


class DenseSum:
    def __init__(self, values, label, heads_first=False):
        self.heads = lax.axis_size("head")
        self.chips = lax.axis_size("blk") // 2
        self.rows = values.shape[0] // (2 * self.heads * self.chips)
        self.label, self.heads_first = label, heads_first
        self.index = lax.axis_index("blk")
        self.mine = self.core_sum(values)

    def core_sum(self, values):
        grid = values.reshape(self.heads, self.chips, 2, self.rows, values.shape[1])
        even = self.index % 2 == 0
        swapped = partner(jnp.where(even, grid[:, :, 1], grid[:, :, 0]))
        return jnp.where(even, grid[:, :, 0], grid[:, :, 1]) + swapped

    def append(self, values):
        self.mine = jnp.concatenate([self.mine, self.core_sum(values)], axis=3)

    def block(self, offset):
        chip = ring_chip(offset)
        heads, columns = self.mine.shape[0], self.mine.shape[3]
        piece = lax.dynamic_slice(self.mine, (0, chip, 0, 0), (heads, 1, self.rows, columns))
        return piece.reshape(heads * self.rows, columns)

    def ring(self):
        if self.heads_first:
            self.mine = head_share(self.mine).astype(jnp.bfloat16)
        pairs = [(self.block(-k), self.block(k)) for k in range(1, self.chips // 2)]
        opposite = self.block(self.chips // 2)
        axis = 1 if self.heads_first else 0
        half = opposite.shape[1] // 256 * 128 if axis else opposite.shape[0] // 2
        opposite = jnp.split(opposite, [half], axis=axis)
        return RingSum(self.block(0), pairs, opposite, self.label, axis)

    def finish(self, total):
        return total if self.heads_first else head_share(total.astype(jnp.bfloat16))

    def total(self):
        return self.finish(self.ring().total())


def project_kernel(shard, groups, rows_ref, weight_ref, cosine_ref, sine_ref, out_ref):
    values = jnp.dot(rows_ref[...], weight_ref[...], preferred_element_type=jnp.float32)
    width = values.shape[1]
    lane = lax.broadcasted_iota(jnp.int32, (shard, width), 1)
    first = lane % HDIM < HDIM // 2
    span = width // groups
    for s in range(values.shape[0] // shard):
        part = values[s * shard : (s + 1) * shard]
        turned = jnp.where(
            first, pltpu.roll(part, width - HDIM // 2, 1), pltpu.roll(part, HDIM // 2, 1)
        )
        part = (part * cosine_ref[...] + turned * sine_ref[...]).astype(jnp.bfloat16)
        for k in range(groups):
            out_ref[s, k] = part[:, k * span : (k + 1) * span]


def project(normed, weights, positions, groups, group):
    rows, width = normed.shape
    shard = positions.shape[0]
    span = (group + 2) * HDIM
    cosine, sine = rope_tables(positions, HDIM // 2)
    cosine = jnp.concatenate([cosine, cosine], axis=1)
    sine = jnp.concatenate([-sine, sine], axis=1)
    plain = (jnp.ones((shard, HDIM), jnp.float32), jnp.zeros((shard, HDIM), jnp.float32))
    cosine = jnp.concatenate(([cosine] * (group + 1) + [plain[0]]) * 2, axis=1)
    sine = jnp.concatenate(([sine] * (group + 1) + [plain[1]]) * 2, axis=1)
    table = pl.BlockSpec((shard, 2 * span), lambda j: (0, 0))
    return pl.pallas_call(
        functools.partial(project_kernel, shard, 2),
        grid=(groups // 2,),
        in_specs=[
            pl.BlockSpec((rows, width), lambda j: (0, 0)),
            pl.BlockSpec((width, 2 * span), lambda j: (0, j)),
            table,
            table,
        ],
        out_specs=pl.BlockSpec((rows // shard, 2, shard, span), lambda j: (0, j, 0, 0)),
        out_shape=jax.ShapeDtypeStruct((rows // shard, groups, shard, span), jnp.bfloat16),
        compiler_params=pltpu.CompilerParams(dimension_semantics=("arbitrary",)),
        cost_estimate=pl.CostEstimate(
            flops=2 * rows * width * groups * span,
            bytes_accessed=2 * width * groups * span,
            transcendentals=0,
        ),
        name="project",
    )(normed, weights, cosine, sine)


def with_lanes(values, extra):
    rows = values.shape[0]
    spare = jnp.zeros((rows, LANES - extra.shape[1]), values.dtype)
    return jnp.concatenate([values, extra.astype(values.dtype), spare], axis=1)


def add_lanes(padded, extra):
    _, columns = padded.shape
    spread = ((0, 0), (columns - LANES, LANES - extra.shape[1]))
    return padded + jnp.pad(extra, spread)


def layer(
    tokens,
    gain_attn,
    w_query,
    w_key,
    w_value,
    w_out,
    gain_moe,
    w_router,
    w_gate,
    w_up,
    w_down,
    routes,
    grad_out,
):
    seq_local, shard, width = tokens.shape
    token_rows = seq_local * shard
    blk_index = lax.axis_index("blk")
    blk_count = lax.axis_size("blk")
    seq_total = blk_count * shard
    part_rows = w_query.shape[0]
    groups = w_key.shape[1] // HDIM
    group = w_query.shape[1] // w_key.shape[1]
    lanes = group * HDIM
    span = lanes + 2 * HDIM
    pairs = seq_local * groups
    copies = blk_count // pairs
    experts = w_router.shape[1]
    units = w_gate.shape[2]

    mixed_weights = jnp.concatenate(
        [
            w_query.reshape(part_rows, groups, lanes),
            w_key.reshape(part_rows, groups, HDIM),
            w_value.reshape(part_rows, groups, HDIM),
        ],
        axis=2,
    ).reshape(part_rows, groups * span)
    full_mixed = dense_gather(with_lanes(mixed_weights, gain_attn[:, None]))
    full_out = dense_gather_late(
        with_lanes(w_out, jnp.concatenate([w_router, gain_moe[:, None]], axis=1))
    )
    router = full_out[:, width:]
    full_router = router[:, :experts]
    router = jnp.where(jnp.arange(LANES)[None, :] < experts, router, jnp.bfloat16(0.0))
    gain_first = full_mixed[:, groups * span].astype(jnp.float32)
    gain_second = full_out[:, width + experts].astype(jnp.float32)

    expert_ids = jnp.arange(experts, dtype=jnp.int32)
    routes_tok = routes.reshape(token_rows, TOP)
    chosen = jnp.any(routes_tok[:, :, None] == expert_ids[None, None, :], axis=1)
    d_out = grad_out.reshape(token_rows, width)
    grads_own = with_lanes(d_out.astype(jnp.bfloat16), chosen)
    grads_pairs, grads_opposite = ring_gather(grads_own)
    w_lin = jnp.concatenate([w_gate, w_up], axis=2)
    other_lin, other_down = partner(w_lin), partner(w_down)
    both_lin = jnp.concatenate([w_lin, other_lin], axis=0)
    both_down = jnp.concatenate([w_down, other_down], axis=0)

    residual = tokens.astype(jnp.float32).reshape(token_rows, width)
    inverse_one = rms_scale(residual)
    normed = (residual * inverse_one * gain_first).astype(jnp.bfloat16)
    positions = blk_index * shard + jnp.arange(shard, dtype=jnp.int32)
    packed = project(normed, full_mixed, positions, groups, group)

    def to_pairs(values, columns):
        values = values.reshape(pairs, 1, shard, columns)
        values = jnp.broadcast_to(values, (pairs, copies, shard, columns))
        return exchange(values.reshape(blk_count, shard, columns)).reshape(seq_total, columns)

    def to_tokens(values, columns):
        values = exchange(values.reshape(blk_count, shard, columns))
        values = values.reshape(pairs, copies, shard, columns)[:, 0]
        values = values.reshape(seq_local, groups, shard, columns).transpose(0, 2, 1, 3)
        return values.reshape(token_rows, groups * columns)

    pair_qkv = to_pairs(packed, span)
    pair_attended, flat, log_total = attend_forward(pair_qkv, group)
    attended = to_tokens(pair_attended, lanes)
    branch = matmul(attended, full_out)[:, :width]
    middle = residual + branch
    inverse_two = rms_scale(middle)
    normed_two = (middle * inverse_two * gain_second).astype(jnp.bfloat16)
    logits = matmul(normed_two, full_router)
    gates = jax.nn.softmax(jnp.where(chosen, logits, -jnp.inf), axis=-1)

    blocks_pairs, blocks_opposite = ring_gather(normed_two)
    total = blk_count // 2 * token_rows
    ids = jnp.stack([blk_index, blk_index ^ 1]).astype(jnp.int32)

    def apply_experts(blocks, grads, slot, buffers):
        return expert_rows(
            ids, experts, blocks, grads, router, both_lin, both_down, slot, total, buffers
        )

    ring_pairs = len(blocks_pairs)
    mixed_own, back_own, buffers = apply_experts(
        [normed_two], [grads_own], 2 * ring_pairs, None
    )
    mixed_pairs, back_pairs = [], []
    for k in range(ring_pairs):
        mixed, back, buffers = apply_experts(blocks_pairs[k], grads_pairs[k], k, buffers)
        mixed_pairs.append(mixed)
        back_pairs.append(back)
    mixed_opposite, back_opposite, buffers = apply_experts(
        blocks_opposite, grads_opposite, 2 * ring_pairs + 1, buffers
    )
    rows_all, grads_all, d_lin_all, hidden_all = buffers
    back_ring = RingSum(back_own[0], back_pairs, back_opposite, "back")
    others = [
        matmul_tn(rows_all, d_lin_all[:, 2 * units :]).astype(jnp.bfloat16),
        matmul_tn(hidden_all[:, units:], grads_all).astype(jnp.bfloat16),
    ]
    others = [partner(part) for part in others]
    mine = [
        matmul_tn(rows_all, d_lin_all[:, : 2 * units]) + others[0].astype(jnp.float32),
        matmul_tn(hidden_all[:, :units], grads_all) + others[1].astype(jnp.float32),
    ]
    mine = [part.astype(jnp.bfloat16) for part in mine]
    back_sum = back_ring.total()
    theirs = [from_heads(part) for part in mine]
    mixed_ring = RingSum(mixed_own[0], mixed_pairs, mixed_opposite, "mixed")
    (mixed_ring.onward, mixed_ring.back), back_sum = lax.optimization_barrier(
        ((mixed_ring.onward, mixed_ring.back), back_sum)
    )
    mixed_ring.send()

    d_gates = back_sum[:, width : width + experts] + back_sum[:, width + experts : width + 2 * experts]
    d_logits = gates * (d_gates - jnp.sum(gates * d_gates, axis=-1, keepdims=True))
    grad_router = jnp.dot(normed_two.astype(jnp.float32).T, d_logits, precision=highest)
    d_normed_two = back_sum[:, :width] + jnp.dot(
        d_logits, full_router.astype(jnp.float32).T, precision=highest
    )
    d_mid_norm, grad_gain_second = norm_back(middle, inverse_two, gain_second, d_normed_two)
    d_mid = d_out + d_mid_norm
    d_branch = jnp.pad(d_mid.astype(jnp.bfloat16), ((0, 0), (0, LANES)))
    d_attended = matmul_nt(d_branch, full_out).astype(jnp.bfloat16)
    early = add_lanes(
        matmul_tn(attended, d_branch),
        jnp.concatenate([grad_router, grad_gain_second[:, None]], axis=1),
    ).astype(jnp.bfloat16)
    mixed_ring.land()
    d_attended, early, mixed_ring.onward, mixed_ring.back = lax.optimization_barrier(
        (d_attended, early, mixed_ring.onward, mixed_ring.back)
    )
    pair_grad = to_pairs(
        d_attended.reshape(seq_local, shard, groups, lanes).transpose(0, 2, 1, 3), lanes
    )
    pair_grad, mixed_ring.onward, mixed_ring.back = lax.optimization_barrier(
        (pair_grad, mixed_ring.onward, mixed_ring.back)
    )
    mixed_ring.send()
    pair_cosine, pair_sine = rope_tables(jnp.arange(seq_total, dtype=jnp.int32), HDIM // 2)
    pair_d = attend_backward(
        pair_qkv, pair_grad, flat, log_total, pair_cosine.T, pair_sine.T, group
    )
    early = DenseSum(early, "early", True).total()
    mixed_ring.land()
    pair_d, mixed_ring.onward, mixed_ring.back = lax.optimization_barrier(
        (pair_d, mixed_ring.onward, mixed_ring.back)
    )
    mixed_ring.send()
    d_linear = to_tokens(pair_d, span)
    mixed_ring.land()
    d_linear, early = lax.optimization_barrier((d_linear, early))
    grad_mixed = matmul_tn(normed, d_linear).astype(jnp.bfloat16)
    late = DenseSum(grad_mixed, "late", True)
    d_normed = matmul_nt(jnp.pad(d_linear, ((0, 0), (0, LANES))), full_mixed)
    d_tok_norm, grad_gain_first = norm_back(residual, inverse_one, gain_first, d_normed)
    grad_tokens = (d_mid + d_tok_norm).reshape(seq_local, shard, width)
    late.append(jnp.pad(grad_gain_first[:, None].astype(jnp.bfloat16), ((0, 0), (0, LANES - 1))))
    late_ring = late.ring()
    sums = [
        functools.reduce(jnp.add, [v.astype(jnp.float32) for v in others], part.astype(jnp.float32))
        for part, others in zip(mine, theirs)
    ]
    grad_gate_sum, grad_up_sum = sums[0][:, :units], sums[0][:, units:]
    grad_down_sum = sums[1]
    out = (middle + mixed_ring.total()).reshape(seq_local, shard, width)
    late = late.finish(late_ring.total())
    late_mixed = late[:, : groups * span].reshape(part_rows, groups, span)
    return (
        out,
        grad_tokens,
        late[:, groups * span],
        late_mixed[:, :, :lanes].reshape(part_rows, -1),
        late_mixed[:, :, lanes : lanes + HDIM].reshape(part_rows, -1),
        late_mixed[:, :, lanes + HDIM :].reshape(part_rows, -1),
        early[:, :width],
        early[:, width + experts],
        early[:, width : width + experts],
        grad_gate_sum[None],
        grad_up_sum[None],
        grad_down_sum[None],
    )


def solution(mesh):
    placed = (
        P("head", "blk", None),
        P(("head", "blk")),
        P(("head", "blk"), None),
        P(("head", "blk"), None),
        P(("head", "blk"), None),
        P(("head", "blk"), None),
        P(("head", "blk")),
        P(("head", "blk"), None),
        P("blk", None, None),
        P("blk", None, None),
        P("blk", None, None),
        P("head", "blk", None),
        P("head", "blk", None),
    )
    return jax.shard_map(
        layer,
        mesh=mesh,
        in_specs=placed,
        out_specs=(
            P("head", "blk", None),
            P("head", "blk", None),
            P(("head", "blk")),
            P(("head", "blk"), None),
            P(("head", "blk"), None),
            P(("head", "blk"), None),
            P(("head", "blk"), None),
            P(("head", "blk")),
            P(("head", "blk"), None),
            P("blk", None, None),
            P("blk", None, None),
            P("blk", None, None),
        ),
        check_vma=False,
    )
```

```python
import functools

import jax
import jax.numpy as jnp
from jax import lax
from jax.experimental import pallas as pl
from jax.experimental.pallas import tpu as pltpu
from jax.sharding import PartitionSpec as P


HDIM = 64
TOP = 8
BLOCK = 256
LANES = 128

highest = lax.Precision.HIGHEST
theta_base = 10000.0
norm_eps = 1e-06


def rope_tables(positions, half_width):
    index_float = jnp.arange(half_width, dtype=jnp.float32)
    frequency = theta_base ** (-2.0 * index_float / (2 * half_width))
    angles = positions.astype(jnp.float32)[:, None] * frequency[None, :]
    return (jnp.cos(angles), jnp.sin(angles))


def rms_scale(values):
    return lax.rsqrt(jnp.mean(values * values, axis=-1, keepdims=True) + norm_eps)


def norm_back(values, inverse, gain, d_normed):
    unit_values = values * inverse
    scaled = d_normed * gain
    d_gain = jnp.sum(d_normed * unit_values, axis=0)
    d_values = inverse * (
        scaled - unit_values * jnp.mean(scaled * unit_values, axis=-1, keepdims=True)
    )
    return (d_values, d_gain)


def matmul(left, right):
    return jnp.dot(left, right, preferred_element_type=jnp.float32)


def matmul_nt(left, right):
    return lax.dot_general(left, right, (((1,), (1,)), ((), ())), preferred_element_type=jnp.float32)


def matmul_tn(left, right):
    return lax.dot_general(left, right, (((0,), (0,)), ((), ())), preferred_element_type=jnp.float32)


def wide(ref, i, group):
    blocks = [ref[2 * i], ref[2 * i + 1]] if i is not None else [ref[0], ref[1]]
    pieces = [b[h * HDIM : (h + 1) * HDIM] for h in range(group) for b in blocks]
    return jnp.concatenate(pieces, axis=1)


def narrow(values, group, k):
    starts = [h * BLOCK + k * LANES for h in range(group)]
    return jnp.concatenate([values[:, s : s + LANES] for s in starts], axis=0)


def spread(qkv_ref, start, row_ref, column_ref):
    def step(b, carry):
        here = pl.ds(pl.multiple_of(b * LANES, LANES), LANES)
        piece = qkv_ref[b, start : start + HDIM]
        if row_ref is not None:
            row_ref[here, :] = piece.T
        if column_ref is not None:
            column_ref[:, here] = piece
        return carry

    lax.fori_loop(0, qkv_ref.shape[0], step, 0)


def forward_kernel(group, qkv_ref, att_ref, flat_ref, lse_ref, key_sc, val_sc, acc_sc):
    i = pl.program_id(0)
    lanes = group*HDIM

    @pl.when(i == 0)
    def _():
        spread(qkv_ref, lanes, key_sc, None)
        spread(qkv_ref, lanes + HDIM, None, val_sc)

    query = wide(qkv_ref, i, group) * jnp.bfloat16(HDIM**-0.5)
    acc_sc[...] = jnp.zeros_like(acc_sc)

    def step(j, carry):
        top, total = carry
        here = pl.ds(pl.multiple_of(j*BLOCK, BLOCK), BLOCK)
        scores = jnp.dot(key_sc[here, :], query, preferred_element_type=jnp.float32)
        new_top = jnp.maximum(top, jnp.max(scores, axis=0, keepdims=True))
        probs = jnp.exp(scores - new_top)
        fade = jnp.exp(top - new_top)
        acc_sc[...] = acc_sc[...]*fade + jnp.dot(val_sc[:, here], probs.astype(jnp.bfloat16), preferred_element_type=jnp.float32)
        return new_top, total*fade + jnp.sum(probs, axis=0, keepdims=True)

    width = group*BLOCK
    top, total = lax.fori_loop(0, i+1, step, (jnp.full((1,width), -1e30, jnp.float32), jnp.zeros((1,width), jnp.float32)))
    result = acc_sc[...] / total
    flat_ref[0] = result
    for k in range(2):
        att_ref[k] = narrow(result, group, k).astype(jnp.bfloat16)
    lse_ref[0] = top + jnp.log(total)


def attend_forward(qkv, group):
    count = qkv.shape[0]; total = count*LANES; steps = total//BLOCK; lanes = group*HDIM; width = group*BLOCK
    return pl.pallas_call(
        functools.partial(forward_kernel, group),
        grid=(steps,),
        in_specs=[pl.BlockSpec((count, lanes+2*HDIM, LANES), lambda i: (0,0,0))],
        out_specs=[pl.BlockSpec((2, lanes, LANES), lambda i: (i,0,0)),
                   pl.BlockSpec((1, HDIM, width), lambda i: (i,0,0)),
                   pl.BlockSpec((1,1,width), lambda i: (i,0,0))],
        out_shape=[jax.ShapeDtypeStruct((count, lanes, LANES), jnp.bfloat16),
                   jax.ShapeDtypeStruct((steps,HDIM,width), jnp.float32),
                   jax.ShapeDtypeStruct((steps,1,width), jnp.float32)],
        scratch_shapes=[pltpu.VMEM((total,HDIM), jnp.bfloat16), pltpu.VMEM((HDIM,total), jnp.bfloat16), pltpu.VMEM((HDIM,width), jnp.float32)],
        compiler_params=pltpu.CompilerParams(dimension_semantics=("arbitrary",)),
        name="attend_forward",
    )(qkv)


def unrotate(values, cosine, sine):
    a, b = values[:HDIM//2], values[HDIM//2:]
    return jnp.concatenate([a*cosine + b*sine, b*cosine - a*sine], axis=0)


def backward_kernel(group, steps, qkv_ref, grad_ref, flat_ref, lse_ref, cos_ref, sin_ref, out_ref, key_sc, keyt_sc, val_sc, dq_sc, dk_sc, dv_sc):
    i = pl.program_id(0)
    lanes = group*HDIM
    scale = HDIM**-0.5

    @pl.when(i == 0)
    def _():
        spread(qkv_ref, lanes, key_sc, keyt_sc)
        spread(qkv_ref, lanes + HDIM, val_sc, None)
        dk_sc[...] = jnp.zeros_like(dk_sc)
        dv_sc[...] = jnp.zeros_like(dv_sc)

    rows = pl.ds(pl.multiple_of(i*BLOCK, BLOCK), BLOCK)
    query_w = wide(qkv_ref, i, group) * jnp.bfloat16(scale)
    grad_w = wide(grad_ref, None, group)
    query_t, grad_t = query_w.T, grad_w.T
    lse = lse_ref[0]
    delta = jnp.sum(grad_w.astype(jnp.float32)*flat_ref[0], axis=0, keepdims=True)
    dq_sc[...] = jnp.zeros_like(dq_sc)

    def step(j, carry):
        here = pl.ds(pl.multiple_of(j*BLOCK, BLOCK), BLOCK)
        scores = jnp.dot(key_sc[here,:], query_w, preferred_element_type=jnp.float32)
        probs = jnp.exp(scores - lse)
        dprobs = jnp.dot(val_sc[here,:], grad_w, preferred_element_type=jnp.float32)
        dv_sc[here,:] += jnp.dot(probs.astype(jnp.bfloat16), grad_t, preferred_element_type=jnp.float32)
        dscores = (probs*(dprobs-delta)).astype(jnp.bfloat16)
        dk_sc[here,:] += jnp.dot(dscores, query_t, preferred_element_type=jnp.float32)
        dq_sc[...] += jnp.dot(keyt_sc[:,here], dscores, preferred_element_type=jnp.float32)
        return carry

    lax.fori_loop(0, i+1, step, 0)
    cosine, sine = cos_ref[:, rows], sin_ref[:, rows]
    pieces = [unrotate(dq_sc[:, h*BLOCK:(h+1)*BLOCK]*scale, cosine, sine).astype(jnp.bfloat16) for h in range(group)]
    for k in range(2):
        columns = slice(k * LANES, (k + 1) * LANES)
        out_ref[2 * i + k, :lanes] = jnp.concatenate([p[:, columns] for p in pieces], axis=0)

    @pl.when(i == steps-1)
    def _():
        def finish(j, carry):
            here = pl.ds(pl.multiple_of(j*BLOCK, BLOCK), BLOCK)
            turned = unrotate(dk_sc[here,:].T, cos_ref[:,here], sin_ref[:,here]).astype(jnp.bfloat16)
            both = jnp.concatenate([turned, dv_sc[here,:].astype(jnp.bfloat16).T], axis=0)
            for k in range(2):
                out_ref[2 * j + k, lanes:] = both[:, k * LANES : (k + 1) * LANES]
            return carry

        lax.fori_loop(0, steps, finish, 0)


def attend_backward(qkv, grad, flat, lse, cosine, sine, group):
    count = qkv.shape[0]; total = count*LANES; steps = total//BLOCK; lanes = group*HDIM; width = group*BLOCK
    return pl.pallas_call(
        functools.partial(backward_kernel, group, steps),
        grid=(steps,),
        in_specs=[pl.BlockSpec((count, lanes+2*HDIM, LANES), lambda i: (0,0,0)),
                  pl.BlockSpec((2, lanes, LANES), lambda i: (i,0,0)),
                  pl.BlockSpec((1, HDIM, width), lambda i: (i,0,0)),
                  pl.BlockSpec((1,1,width), lambda i: (i,0,0)),
                  pl.BlockSpec((HDIM//2, total), lambda i: (0,0)),
                  pl.BlockSpec((HDIM//2, total), lambda i: (0,0))],
        out_specs=pl.BlockSpec((count, lanes+2*HDIM, LANES), lambda i: (0,0,0)),
        out_shape=jax.ShapeDtypeStruct((count, lanes+2*HDIM, LANES), jnp.bfloat16),
        scratch_shapes=[pltpu.VMEM((total,HDIM), jnp.bfloat16), pltpu.VMEM((HDIM,total), jnp.bfloat16), pltpu.VMEM((total,HDIM), jnp.bfloat16),
                        pltpu.VMEM((HDIM,width), jnp.float32), pltpu.VMEM((total,HDIM), jnp.float32), pltpu.VMEM((total,HDIM), jnp.float32)],
        compiler_params=pltpu.CompilerParams(dimension_semantics=("arbitrary",)),
        name="attend_backward",
    )(qkv, grad, flat, lse, cosine, sine)


def expert_kernel(
    parts, rows, width, experts, steps, chained, index_ref, *refs
):
    blocks = refs[:parts]
    grads = refs[parts : 2 * parts]
    router_ref, lin_ref, down_ref = refs[2 * parts : 2 * parts + 3]
    refs = refs[2 * parts + 3 + (4 if chained else 0) :]
    mixed_refs, back_refs, refs = refs[:parts], refs[parts : 2 * parts], refs[2 * parts :]
    rows_ref, grads_ref, d_lin_ref, hidden_ref = refs[:4]
    gates_sc, d_gates_sc, mixed_sc, back_sc = refs[4:]
    part = rows // parts
    units = down_ref.shape[1]
    step = pl.program_id(0)
    lane = lax.broadcasted_iota(jnp.int32, (rows, LANES), 1)

    @pl.when(step == 0)
    def _():
        for k in range(parts):
            here = pl.ds(k * part, part)
            rows_ref[here, :] = blocks[k][...]
            grads_ref[here, :] = grads[k][:, :width]
            logits = jnp.dot(blocks[k][...], router_ref[...], preferred_element_type=jnp.float32)
            logits = jnp.where(grads[k][:, width:].astype(jnp.float32) > 0.5, logits, -1e30)
            weight = jnp.exp(logits - jnp.max(logits, axis=1, keepdims=True))
            gates_sc[here, :] = weight / jnp.sum(weight, axis=1, keepdims=True)
        d_gates_sc[...] = jnp.zeros_like(d_gates_sc)

    expert = index_ref[step]
    own = lane == expert
    gate = jnp.sum(jnp.where(own, gates_sc[...], 0.0), axis=1, keepdims=True)
    block = rows_ref[...]
    lin = jnp.dot(block, lin_ref[0], preferred_element_type=jnp.float32)
    gate_lin, up_lin = lin[:, :units], lin[:, units:]
    d_hidden = matmul_nt(grads_ref[...], down_ref[0])
    sigma = 1.0 / (1.0 + jnp.exp(-gate_lin))
    active = gate_lin * sigma
    hidden = active * up_lin
    d_gates_sc[...] += jnp.where(own, jnp.sum(hidden * d_hidden, axis=1, keepdims=True), 0.0)
    hidden = (gate * hidden).astype(jnp.bfloat16)
    d_hidden = gate * d_hidden
    slope = sigma + active - active * sigma
    d_gate = (d_hidden * up_lin * slope).astype(jnp.bfloat16)
    d_up = (d_hidden * active).astype(jnp.bfloat16)
    hidden_ref[...] = hidden
    d_lin = jnp.concatenate([d_gate, d_up], axis=1)
    d_lin_ref[...] = d_lin
    mixed = jnp.dot(hidden, down_ref[0], preferred_element_type=jnp.float32)
    back = matmul_nt(d_lin, lin_ref[0])

    @pl.when(step == 0)
    def _():
        mixed_sc[...] = mixed
        back_sc[...] = back

    @pl.when(step > 0)
    def _():
        mixed_sc[...] += mixed
        back_sc[...] += back

    @pl.when(step == steps - 1)
    def _():
        d_gates = d_gates_sc[...]
        high = d_gates.astype(jnp.bfloat16).astype(jnp.float32)
        low = pltpu.roll(d_gates - high, experts, 1)
        d_gates = jnp.where(lane < experts, high, low).astype(jnp.bfloat16)
        for k in range(parts):
            here = slice(k * part, (k + 1) * part)
            mixed_refs[k][...] = mixed_sc[here, :].astype(jnp.bfloat16)
            back_refs[k][:, :width] = back_sc[here, :].astype(jnp.bfloat16)
            back_refs[k][:, width:] = d_gates[here]


def expert_rows(index, experts, blocks, grads, router, lin, down, slot, total, buffers):
    parts = len(blocks)
    part, width = blocks[0].shape
    rows = parts * part
    units = down.shape[1]
    steps = 2
    whole = lambda *shape: pl.BlockSpec(shape, lambda i, ids: (0,) * len(shape))
    columns = lambda count: pl.BlockSpec((rows, count), lambda i, ids: (slot, i))
    kept = pl.BlockSpec((rows, width), lambda i, ids: (slot, 0))
    chained = buffers is not None
    shapes = [
        *[jax.ShapeDtypeStruct((part, width), jnp.bfloat16)] * parts,
        *[jax.ShapeDtypeStruct((part, width + LANES), jnp.bfloat16)] * parts,
        jax.ShapeDtypeStruct((total, width), jnp.bfloat16),
        jax.ShapeDtypeStruct((total, width), jnp.bfloat16),
        jax.ShapeDtypeStruct((total, 4 * units), jnp.bfloat16),
        jax.ShapeDtypeStruct((total, 2 * units), jnp.bfloat16),
    ]
    inputs = [index, *blocks, *grads, router, lin, down] + (list(buffers) if chained else [])
    first = 1 + 2 * parts + 3
    results = pl.pallas_call(
        functools.partial(expert_kernel, parts, rows, width, experts, steps, chained),
        grid_spec=pltpu.PrefetchScalarGridSpec(
            num_scalar_prefetch=1,
            grid=(steps,),
            in_specs=[whole(part, width)] * parts
            + [whole(part, width + LANES)] * parts
            + [
                whole(width, LANES),
                pl.BlockSpec((1, width, 2 * units), lambda i, ids: (i, 0, 0)),
                pl.BlockSpec((1, units, width), lambda i, ids: (i, 0, 0)),
            ]
            + ([pl.BlockSpec(memory_space=pl.ANY)] * 4 if chained else []),
            out_specs=[
                *[whole(part, width)] * parts,
                *[whole(part, width + LANES)] * parts,
                kept,
                kept,
                columns(2 * units),
                columns(units),
            ],
            scratch_shapes=[
                pltpu.VMEM((rows, LANES), jnp.float32),
                pltpu.VMEM((rows, LANES), jnp.float32),
                pltpu.VMEM((rows, width), jnp.float32),
                pltpu.VMEM((rows, width), jnp.float32),
            ],
        ),
        out_shape=shapes,
        input_output_aliases={first + k: 2 * parts + k for k in range(4)} if chained else {},
        compiler_params=pltpu.CompilerParams(dimension_semantics=("arbitrary",)),
        cost_estimate=pl.CostEstimate(
            flops=rows * width * units * 24,
            bytes_accessed=12 * width * units + 20 * rows * width,
            transcendentals=rows * units * 2,
        ),
        name="expert_rows",
    )(*inputs)
    return results[:parts], results[parts : 2 * parts], results[2 * parts :]


def contract(equation, left, right):
    return jnp.einsum(equation, left, right, preferred_element_type=jnp.float32)


def exchange(values):
    return lax.all_to_all(values, "blk", split_axis=0, concat_axis=0, tiled=True)


def from_heads(values):
    heads = lax.axis_size("head")
    return [
        lax.ppermute(values, "head", [(k, (k + turn) % heads) for k in range(heads)])
        for turn in range(1, heads)
    ]


def partner(values):
    count = lax.axis_size("blk")
    return lax.ppermute(values, "blk", [(k, k ^ 1) for k in range(count)])


def after(values, *earlier):
    return lax.optimization_barrier((values, earlier))[0]


def ring_order():
    half = lax.axis_size("blk") // 4
    return [2 * k for k in range(half)] + [2 * k + 1 for k in reversed(range(half))]


def ring_steps():
    order = ring_order()
    onward, back = [], []
    for place, chip in enumerate(order):
        following = order[(place + 1) % len(order)]
        for core in range(2):
            onward.append((2 * chip + core, 2 * following + core))
            back.append((2 * following + core, 2 * chip + core))
    send_on = lambda values: lax.ppermute(values, "blk", onward)
    send_back = lambda values: lax.ppermute(values, "blk", back)
    return len(order), send_on, send_back


def ring_gather(values, axis=0):
    length, send_on, send_back = ring_steps()
    half = values.shape[axis] // 256 * 128
    behind = ahead = values
    pairs = []
    for _ in range(length // 2 - 1):
        behind, ahead = send_on(behind), send_back(ahead)
        pairs.append((behind, ahead))
    behind = lax.slice_in_dim(behind, 0, half, axis=axis)
    ahead = lax.slice_in_dim(ahead, half, ahead.shape[axis], axis=axis)
    return pairs, (send_on(behind), send_back(ahead))


class RingSum:
    def __init__(self, own, pairs, opposite, label, axis=0):
        _, self.send_on, self.send_back = ring_steps()
        self.own, self.pairs, self.label = own, list(reversed(pairs)), label
        self.onward, self.back = opposite
        self.axis = axis
        self.hop = 0

    def send(self, *hold):
        if self.hop > 0:
            behind, ahead = self.pairs[self.hop - 1]
            self.onward, self.back = self.onward + ahead, self.back + behind
        if hold:
            self.onward, self.back = after((self.onward, self.back), hold)
        self.onward, self.back = self.send_on(self.onward), self.send_back(self.back)
        return self

    def land(self, *filler):
        if filler:
            self.onward, self.back = after((self.onward, self.back), filler)
        if self.hop == 0:
            lengths = self.onward.shape[self.axis], self.back.shape[self.axis]
            spread = [(0, 0), (0, 0)]
            spread[self.axis] = (0, lengths[1])
            self.onward = jnp.pad(self.onward, spread)
            spread[self.axis] = (lengths[0], 0)
            self.back = jnp.pad(self.back, spread)
        self.hop += 1
        return self

    def total(self):
        while self.hop <= len(self.pairs):
            self.send().land()
        wide = self.own.astype(jnp.float32)
        return wide + self.onward.astype(jnp.float32) + self.back.astype(jnp.float32)


def ring_chip(offset):
    chips = lax.axis_size("blk") // 2
    chip = lax.axis_index("blk") // 2
    place = jnp.where(chip % 2 == 0, chip // 2, chips - 1 - chip // 2)
    target = (place + offset) % chips
    return jnp.where(target < chips // 2, 2 * target, 2 * (chips - 1 - target) + 1)


def all_heads(values):
    heads = lax.axis_size("head")
    head = lax.axis_index("head")
    place = lambda found, at: lax.dynamic_update_index_in_dim(result, found, at, 0)
    result = jnp.zeros((heads, *values.shape), values.dtype)
    result = place(values, head)
    for turn in range(1, heads):
        other = lax.ppermute(
            values, "head", [(k, (k + turn) % heads) for k in range(heads)]
        )
        result = place(other, (head - turn) % heads)
    return result


def ring_pieces(block, axis):
    pairs, opposite = ring_gather(block, axis)
    found = [(0, block)]
    for k, (behind, ahead) in enumerate(pairs):
        found += [(-k - 1, behind), (k + 1, ahead)]
    return found + [(len(pairs) + 1, jnp.concatenate(opposite, axis=axis))]


def dense_gather(shard):
    chips = lax.axis_size("blk") // 2
    heads = lax.axis_size("head")
    core = lax.axis_index("blk") % 2
    rows, columns = shard.shape
    block = all_heads(shard).reshape(heads * rows, columns)
    full = jnp.zeros((heads, chips, 2, rows, columns), shard.dtype)
    for offset, piece in ring_pieces(block, 1):
        for side, part in ((core, piece), (1 - core, partner(piece))):
            full = lax.dynamic_update_slice(
                full, part.reshape(heads, 1, 1, rows, columns), (0, ring_chip(offset), side, 0, 0)
            )
    return full.reshape(-1, columns)


def dense_gather_late(shard):
    chips = lax.axis_size("blk") // 2
    rows, columns = shard.shape
    found = jnp.zeros((chips, rows, columns), shard.dtype)
    for offset, piece in ring_pieces(shard, 1):
        found = lax.dynamic_update_slice(found, piece[None], (ring_chip(offset), 0, 0))
    found = all_heads(found)
    other = partner(found)
    even = lax.axis_index("blk") % 2 == 0
    pair = [jnp.where(even, found, other), jnp.where(even, other, found)]
    return jnp.stack(pair, axis=2).reshape(-1, columns)


def head_share(values):
    heads, rows = lax.axis_size("head"), values.shape[0] // lax.axis_size("head")
    head = lax.axis_index("head")
    start = (0,) * (values.ndim - 1)
    share = lambda turn: lax.dynamic_slice(
        values, ((head + turn) % heads * rows, *start), (rows, *values.shape[1:])
    )
    result = share(0).astype(jnp.float32)
    for turn in range(1, heads):
        moved = [(k, (k + turn) % heads) for k in range(heads)]
        other = lax.ppermute(share(turn), "head", moved)
        result = result + other.astype(jnp.float32)
    return result


class DenseSum:
    def __init__(self, values, label, heads_first=False, staged=False):
        self.staged = staged
        self.heads = lax.axis_size("head")
        self.chips = lax.axis_size("blk") // 2
        self.rows = values.shape[0] // (2 * self.heads * self.chips)
        self.label, self.heads_first = label, heads_first
        self.index = lax.axis_index("blk")
        self.mine = self.core_sum(values)

    def core_sum(self, values):
        grid = values.reshape(self.heads, self.chips, 2, self.rows, values.shape[1])
        even = self.index % 2 == 0
        swapped = partner(jnp.where(even, grid[:, :, 1], grid[:, :, 0]))
        return jnp.where(even, grid[:, :, 0], grid[:, :, 1]) + swapped

    def append(self, values):
        self.mine = jnp.concatenate([self.mine, self.core_sum(values)], axis=3)

    def block(self, offset):
        chip = ring_chip(offset)
        heads, columns = self.mine.shape[0], self.mine.shape[3]
        piece = lax.dynamic_slice(self.mine, (0, chip, 0, 0), (heads, 1, self.rows, columns))
        return piece.reshape(heads * self.rows, columns)

    def blocks(self, offsets):
        if not self.heads_first:
            return [self.block(offset) for offset in offsets]
        columns = self.mine.shape[3]
        taken = [
            lax.dynamic_slice(
                self.mine, (0, ring_chip(offset), 0, 0), (self.heads, 1, self.rows, columns)
            )
            for offset in offsets
        ]
        total = head_share(jnp.concatenate(taken, axis=1))
        return [total[0, k].astype(jnp.bfloat16) for k in range(len(offsets))]

    def ring(self):
        far = self.chips // 2
        if self.staged:
            stages = [[far, 1 - far, far - 1]]
            stages += [[-k, k] for k in reversed(range(1, far - 1))] + [[0]]
        else:
            stages = [list(range(1 - far, far + 1))]
        found = {}
        for offsets in stages:
            found.update(zip(offsets, self.blocks(offsets)))
        pairs = [(found[-k], found[k]) for k in range(1, far)]
        opposite = found[far]
        axis = 1 if self.heads_first else 0
        half = opposite.shape[1] // 256 * 128 if axis else opposite.shape[0] // 2
        opposite = jnp.split(opposite, [half], axis=axis)
        return RingSum(found[0], pairs, opposite, self.label, axis)

    def finish(self, total):
        return total if self.heads_first else head_share(total.astype(jnp.bfloat16))

    def total(self):
        return self.finish(self.ring().total())


def project_kernel(shard, groups, rows_ref, weight_ref, cosine_ref, sine_ref, out_ref):
    values = jnp.dot(rows_ref[...], weight_ref[...], preferred_element_type=jnp.float32)
    width = values.shape[1]
    lane = lax.broadcasted_iota(jnp.int32, (shard, width), 1)
    first = lane % HDIM < HDIM // 2
    span = width // groups
    for s in range(values.shape[0] // shard):
        part = values[s * shard : (s + 1) * shard]
        turned = jnp.where(
            first, pltpu.roll(part, width - HDIM // 2, 1), pltpu.roll(part, HDIM // 2, 1)
        )
        part = (part * cosine_ref[...] + turned * sine_ref[...]).astype(jnp.bfloat16)
        for k in range(groups):
            out_ref[s, k] = part[:, k * span : (k + 1) * span].T


def project(normed, weights, positions, groups, group):
    rows, width = normed.shape
    shard = positions.shape[0]
    span = (group + 2) * HDIM
    cosine, sine = rope_tables(positions, HDIM // 2)
    cosine = jnp.concatenate([cosine, cosine], axis=1)
    sine = jnp.concatenate([-sine, sine], axis=1)
    plain = (jnp.ones((shard, HDIM), jnp.float32), jnp.zeros((shard, HDIM), jnp.float32))
    cosine = jnp.concatenate(([cosine] * (group + 1) + [plain[0]]) * 2, axis=1)
    sine = jnp.concatenate(([sine] * (group + 1) + [plain[1]]) * 2, axis=1)
    table = pl.BlockSpec((shard, 2 * span), lambda j: (0, 0))
    return pl.pallas_call(
        functools.partial(project_kernel, shard, 2),
        grid=(groups // 2,),
        in_specs=[
            pl.BlockSpec((rows, width), lambda j: (0, 0)),
            pl.BlockSpec((width, 2 * span), lambda j: (0, j)),
            table,
            table,
        ],
        out_specs=pl.BlockSpec((rows // shard, 2, span, shard), lambda j: (0, j, 0, 0)),
        out_shape=jax.ShapeDtypeStruct((rows // shard, groups, span, shard), jnp.bfloat16),
        compiler_params=pltpu.CompilerParams(dimension_semantics=("arbitrary",)),
        cost_estimate=pl.CostEstimate(
            flops=2 * rows * width * groups * span,
            bytes_accessed=2 * width * groups * span,
            transcendentals=0,
        ),
        name="project",
    )(normed, weights, cosine, sine)


def with_lanes(values, extra):
    rows = values.shape[0]
    spare = jnp.zeros((rows, LANES - extra.shape[1]), values.dtype)
    return jnp.concatenate([values, extra.astype(values.dtype), spare], axis=1)


def add_lanes(padded, extra):
    _, columns = padded.shape
    spread = ((0, 0), (columns - LANES, LANES - extra.shape[1]))
    return padded + jnp.pad(extra, spread)


def layer(
    tokens,
    gain_attn,
    w_query,
    w_key,
    w_value,
    w_out,
    gain_moe,
    w_router,
    w_gate,
    w_up,
    w_down,
    routes,
    grad_out,
):
    seq_local, shard, width = tokens.shape
    token_rows = seq_local * shard
    blk_index = lax.axis_index("blk")
    blk_count = lax.axis_size("blk")
    seq_total = blk_count * shard
    part_rows = w_query.shape[0]
    groups = w_key.shape[1] // HDIM
    group = w_query.shape[1] // w_key.shape[1]
    lanes = group * HDIM
    span = lanes + 2 * HDIM
    pairs = seq_local * groups
    copies = blk_count // pairs
    experts = w_router.shape[1]
    units = w_gate.shape[2]

    mixed_weights = jnp.concatenate(
        [
            w_query.reshape(part_rows, groups, lanes),
            w_key.reshape(part_rows, groups, HDIM),
            w_value.reshape(part_rows, groups, HDIM),
        ],
        axis=2,
    ).reshape(part_rows, groups * span)
    full_mixed = dense_gather(with_lanes(mixed_weights, gain_attn[:, None]))
    full_out = dense_gather_late(
        with_lanes(w_out, jnp.concatenate([w_router, gain_moe[:, None]], axis=1))
    )
    router = full_out[:, width:]
    full_router = router[:, :experts]
    router = jnp.where(jnp.arange(LANES)[None, :] < experts, router, jnp.bfloat16(0.0))
    gain_first = full_mixed[:, groups * span].astype(jnp.float32)
    gain_second = full_out[:, width + experts].astype(jnp.float32)

    expert_ids = jnp.arange(experts, dtype=jnp.int32)
    routes_tok = routes.reshape(token_rows, TOP)
    chosen = jnp.any(routes_tok[:, :, None] == expert_ids[None, None, :], axis=1)
    d_out = grad_out.reshape(token_rows, width)
    grads_own = with_lanes(d_out.astype(jnp.bfloat16), chosen)
    grads_pairs, grads_opposite = ring_gather(grads_own)
    w_lin = jnp.concatenate([w_gate, w_up], axis=2)
    other_lin, other_down = partner(w_lin), partner(w_down)
    both_lin = jnp.concatenate([w_lin, other_lin], axis=0)
    both_down = jnp.concatenate([w_down, other_down], axis=0)

    residual = tokens.astype(jnp.float32).reshape(token_rows, width)
    inverse_one = rms_scale(residual)
    normed = (residual * inverse_one * gain_first).astype(jnp.bfloat16)
    positions = blk_index * shard + jnp.arange(shard, dtype=jnp.int32)
    packed = project(normed, full_mixed, positions, groups, group)

    def to_pairs(values, columns):
        values = values.reshape(pairs, 1, columns, shard)
        values = jnp.broadcast_to(values, (pairs, copies, columns, shard))
        return exchange(values.reshape(blk_count, columns, shard))

    def to_tokens(values, columns):
        values = exchange(values).reshape(pairs, copies, columns, shard)[:, 0]
        return values.reshape(seq_local, groups * columns, shard)

    pair_qkv = to_pairs(packed, span)
    pair_attended, flat, log_total = attend_forward(pair_qkv, group)
    attended = to_tokens(pair_attended, lanes)
    branch = contract("sqt,qd->std", attended, full_out)
    branch = branch.reshape(token_rows, -1)[:, :width]
    middle = residual + branch
    inverse_two = rms_scale(middle)
    normed_two = (middle * inverse_two * gain_second).astype(jnp.bfloat16)
    logits = matmul(normed_two, full_router)
    gates = jax.nn.softmax(jnp.where(chosen, logits, -jnp.inf), axis=-1)

    blocks_pairs, blocks_opposite = ring_gather(normed_two)
    total = blk_count // 2 * token_rows
    ids = jnp.stack([blk_index, blk_index ^ 1]).astype(jnp.int32)

    def apply_experts(blocks, grads, slot, buffers):
        return expert_rows(
            ids, experts, blocks, grads, router, both_lin, both_down, slot, total, buffers
        )

    ring_pairs = len(blocks_pairs)
    mixed_own, back_own, buffers = apply_experts(
        [normed_two], [grads_own], 2 * ring_pairs, None
    )
    mixed_pairs, back_pairs = [], []
    for k in range(ring_pairs):
        mixed, back, buffers = apply_experts(blocks_pairs[k], grads_pairs[k], k, buffers)
        mixed_pairs.append(mixed)
        back_pairs.append(back)
    mixed_opposite, back_opposite, buffers = apply_experts(
        blocks_opposite, grads_opposite, 2 * ring_pairs + 1, buffers
    )
    rows_all, grads_all, d_lin_all, hidden_all = buffers
    back_ring = RingSum(back_own[0], back_pairs, back_opposite, "back")
    lefts = [lambda half: rows_all, lambda half: hidden_all[:, half * units :][:, :units]]
    rights = [lambda half: d_lin_all[:, 2 * half * units :][:, : 2 * units], lambda half: grads_all]
    others, mine = [], []
    for left, right in zip(lefts, rights):
        others.append(partner(matmul_tn(left(1), right(1)).astype(jnp.bfloat16)))
    for k, (left, right) in enumerate(zip(lefts, rights)):
        total = matmul_tn(left(0), right(0)) + others[k].astype(jnp.float32)
        mine.append(total.astype(jnp.bfloat16))
    back_sum = back_ring.total()
    theirs = []
    for part in mine:
        theirs.append(from_heads(part))
    mixed_ring = RingSum(mixed_own[0], mixed_pairs, mixed_opposite, "mixed")
    (mixed_ring.onward, mixed_ring.back), back_sum = lax.optimization_barrier(
        ((mixed_ring.onward, mixed_ring.back), back_sum)
    )
    mixed_ring.send()

    d_gates = back_sum[:, width : width + experts] + back_sum[:, width + experts : width + 2 * experts]
    d_logits = gates * (d_gates - jnp.sum(gates * d_gates, axis=-1, keepdims=True))
    grad_router = jnp.dot(normed_two.astype(jnp.float32).T, d_logits, precision=highest)
    d_normed_two = back_sum[:, :width] + jnp.dot(
        d_logits, full_router.astype(jnp.float32).T, precision=highest
    )
    d_mid_norm, grad_gain_second = norm_back(middle, inverse_two, gain_second, d_normed_two)
    d_mid = d_out + d_mid_norm
    d_branch = jnp.pad(d_mid.astype(jnp.bfloat16), ((0, 0), (0, LANES)))
    d_branch = d_branch.reshape(seq_local, shard, -1)
    d_attended = contract("qd,std->sqt", full_out, d_branch).astype(jnp.bfloat16)
    early = add_lanes(
        contract("sqt,std->qd", attended, d_branch),
        jnp.concatenate([grad_router, grad_gain_second[:, None]], axis=1),
    ).astype(jnp.bfloat16)
    mixed_ring.land()
    d_attended, early, mixed_ring.onward, mixed_ring.back = lax.optimization_barrier(
        (d_attended, early, mixed_ring.onward, mixed_ring.back)
    )
    pair_grad = to_pairs(d_attended, lanes)
    pair_grad, mixed_ring.onward, mixed_ring.back = lax.optimization_barrier(
        (pair_grad, mixed_ring.onward, mixed_ring.back)
    )
    mixed_ring.send()
    pair_cosine, pair_sine = rope_tables(jnp.arange(seq_total, dtype=jnp.int32), HDIM // 2)
    pair_d = attend_backward(
        pair_qkv, pair_grad, flat, log_total, pair_cosine.T, pair_sine.T, group
    )
    early = DenseSum(early, "early", True).total()
    mixed_ring.land()
    d_linear = to_tokens(pair_d, span)
    d_linear, early = lax.optimization_barrier((d_linear, early))
    grad_mixed = contract(
        "stf,sct->fc", normed.reshape(seq_local, shard, width), d_linear
    ).astype(jnp.bfloat16)
    late = DenseSum(grad_mixed, "late", True, True)
    d_normed = contract(
        "sct,fc->stf", jnp.pad(d_linear, ((0, 0), (0, LANES), (0, 0))), full_mixed
    ).reshape(token_rows, width)
    d_tok_norm, grad_gain_first = norm_back(residual, inverse_one, gain_first, d_normed)
    grad_tokens = (d_mid + d_tok_norm).reshape(seq_local, shard, width)
    grad_gain_first, mixed_ring.onward, mixed_ring.back = lax.optimization_barrier(
        (grad_gain_first, mixed_ring.onward, mixed_ring.back)
    )
    mixed_ring.send().land()
    late.append(jnp.pad(grad_gain_first[:, None].astype(jnp.bfloat16), ((0, 0), (0, LANES - 1))))
    late_ring = late.ring()
    sums = [
        functools.reduce(jnp.add, [v.astype(jnp.float32) for v in others], part.astype(jnp.float32))
        for part, others in zip(mine, theirs)
    ]
    grad_gate_sum, grad_up_sum = sums[0][None, :, :units], sums[0][None, :, units:]
    grad_down_sum = sums[1][None]
    out = (middle + mixed_ring.total()).reshape(seq_local, shard, width)
    late = late.finish(late_ring.total())
    late_mixed = late[:, : groups * span].reshape(part_rows, groups, span)
    return (
        out,
        grad_tokens,
        late[:, groups * span],
        late_mixed[:, :, :lanes].reshape(part_rows, -1),
        late_mixed[:, :, lanes : lanes + HDIM].reshape(part_rows, -1),
        late_mixed[:, :, lanes + HDIM :].reshape(part_rows, -1),
        early[:, :width],
        early[:, width + experts],
        early[:, width : width + experts],
        grad_gate_sum,
        grad_up_sum,
        grad_down_sum,
    )


def solution(mesh):
    placed = (
        P("head", "blk", None),
        P(("head", "blk")),
        P(("head", "blk"), None),
        P(("head", "blk"), None),
        P(("head", "blk"), None),
        P(("head", "blk"), None),
        P(("head", "blk")),
        P(("head", "blk"), None),
        P("blk", None, None),
        P("blk", None, None),
        P("blk", None, None),
        P("head", "blk", None),
        P("head", "blk", None),
    )
    return jax.shard_map(
        layer,
        mesh=mesh,
        in_specs=placed,
        out_specs=(
            P("head", "blk", None),
            P("head", "blk", None),
            P(("head", "blk")),
            P(("head", "blk"), None),
            P(("head", "blk"), None),
            P(("head", "blk"), None),
            P(("head", "blk"), None),
            P(("head", "blk")),
            P(("head", "blk"), None),
            P("blk", None, None),
            P("blk", None, None),
            P("blk", None, None),
        ),
        check_vma=False,
    )
```

```python
import functools

import jax
import jax.numpy as jnp
from jax import lax
from jax.experimental import pallas as pl
from jax.experimental.pallas import tpu as pltpu
from jax.sharding import PartitionSpec as P


HDIM = 64
TOP = 8
BLOCK = 256
LANES = 128
HEAD = "head"
BLK = "blk"
ORDERED = ("arbitrary",)

highest = lax.Precision.HIGHEST
theta_base = 10000.0
norm_eps = 1e-06


def rope_tables(positions, half_width):
    index_float = jnp.arange(half_width, dtype=jnp.float32)
    frequency = theta_base ** (-2.0 * index_float / (2 * half_width))
    angles = positions.astype(jnp.float32)[:, None] * frequency[None, :]
    return (jnp.cos(angles), jnp.sin(angles))


def rms_scale(values):
    return lax.rsqrt(jnp.mean(values * values, axis=-1, keepdims=True) + norm_eps)


def norm_back(values, inverse, gain, d_normed):
    unit_values = values * inverse
    scaled = d_normed * gain
    d_gain = jnp.sum(d_normed * unit_values, axis=0)
    d_values = inverse * (
        scaled - unit_values * jnp.mean(scaled * unit_values, axis=-1, keepdims=True)
    )
    return (d_values, d_gain)


def matmul(left, right):
    return jnp.dot(left, right, preferred_element_type=jnp.float32)


def matmul_nt(left, right):
    return lax.dot_general(left, right, (((1,), (1,)), ((), ())), preferred_element_type=jnp.float32)


def matmul_tn(left, right):
    return lax.dot_general(left, right, (((0,), (0,)), ((), ())), preferred_element_type=jnp.float32)


def wide(ref, i, group):
    blocks = [ref[2 * i], ref[2 * i + 1]] if i is not None else [ref[0], ref[1]]
    pieces = [b[h * HDIM : (h + 1) * HDIM] for h in range(group) for b in blocks]
    return jnp.concatenate(pieces, axis=1)


def narrow(values, group, k):
    starts = [h * BLOCK + k * LANES for h in range(group)]
    return jnp.concatenate([values[:, s : s + LANES] for s in starts], axis=0)


def spread(qkv_ref, start, row_ref, column_ref):
    def step(b, carry):
        here = pl.ds(pl.multiple_of(b * LANES, LANES), LANES)
        piece = qkv_ref[b, start : start + HDIM]
        if row_ref is not None:
            row_ref[here, :] = piece.T
        if column_ref is not None:
            column_ref[:, here] = piece
        return carry

    lax.fori_loop(0, qkv_ref.shape[0], step, 0)


def forward_kernel(group, qkv_ref, att_ref, flat_ref, lse_ref, key_sc, val_sc, acc_sc):
    i = pl.program_id(0)
    lanes = group*HDIM

    @pl.when(i == 0)
    def _():
        spread(qkv_ref, lanes, key_sc, None)
        spread(qkv_ref, lanes + HDIM, None, val_sc)

    query = wide(qkv_ref, i, group) * jnp.bfloat16(HDIM**-0.5)
    acc_sc[...] = jnp.zeros_like(acc_sc)

    def step(j, carry):
        top, total = carry
        here = pl.ds(pl.multiple_of(j*BLOCK, BLOCK), BLOCK)
        scores = jnp.dot(key_sc[here, :], query, preferred_element_type=jnp.float32)
        new_top = jnp.maximum(top, jnp.max(scores, axis=0, keepdims=True))
        probs = jnp.exp(scores - new_top)
        fade = jnp.exp(top - new_top)
        acc_sc[...] = acc_sc[...]*fade + jnp.dot(val_sc[:, here], probs.astype(jnp.bfloat16), preferred_element_type=jnp.float32)
        return new_top, total*fade + jnp.sum(probs, axis=0, keepdims=True)

    width = group*BLOCK
    top, total = lax.fori_loop(0, i+1, step, (jnp.full((1,width), -1e30, jnp.float32), jnp.zeros((1,width), jnp.float32)))
    result = acc_sc[...] / total
    flat_ref[0] = result
    for k in range(2):
        att_ref[k] = narrow(result, group, k).astype(jnp.bfloat16)
    lse_ref[0] = top + jnp.log(total)


def attend_forward(qkv, group):
    count = qkv.shape[0]; total = count*LANES; steps = total//BLOCK; lanes = group*HDIM; width = group*BLOCK
    return pl.pallas_call(
        functools.partial(forward_kernel, group),
        grid=(steps,),
        in_specs=[pl.BlockSpec((count, lanes+2*HDIM, LANES), lambda i: (0,0,0))],
        out_specs=[pl.BlockSpec((2, lanes, LANES), lambda i: (i,0,0)),
                   pl.BlockSpec((1, HDIM, width), lambda i: (i,0,0)),
                   pl.BlockSpec((1,1,width), lambda i: (i,0,0))],
        out_shape=[jax.ShapeDtypeStruct((count, lanes, LANES), jnp.bfloat16),
                   jax.ShapeDtypeStruct((steps,HDIM,width), jnp.float32),
                   jax.ShapeDtypeStruct((steps,1,width), jnp.float32)],
        scratch_shapes=[pltpu.VMEM((total,HDIM), jnp.bfloat16), pltpu.VMEM((HDIM,total), jnp.bfloat16), pltpu.VMEM((HDIM,width), jnp.float32)],
        compiler_params=pltpu.CompilerParams(dimension_semantics=ORDERED),
        name="forward",
    )(qkv)


def unrotate(values, cosine, sine):
    a, b = values[:HDIM//2], values[HDIM//2:]
    return jnp.concatenate([a*cosine + b*sine, b*cosine - a*sine], axis=0)


def backward_kernel(group, steps, qkv_ref, grad_ref, flat_ref, lse_ref, cos_ref, sin_ref, out_ref, key_sc, keyt_sc, val_sc, dq_sc, dk_sc, dv_sc):
    i = pl.program_id(0)
    lanes = group*HDIM
    scale = HDIM**-0.5

    @pl.when(i == 0)
    def _():
        spread(qkv_ref, lanes, key_sc, keyt_sc)
        spread(qkv_ref, lanes + HDIM, val_sc, None)
        dk_sc[...] = jnp.zeros_like(dk_sc)
        dv_sc[...] = jnp.zeros_like(dv_sc)

    rows = pl.ds(pl.multiple_of(i*BLOCK, BLOCK), BLOCK)
    query_w = wide(qkv_ref, i, group) * jnp.bfloat16(scale)
    grad_w = wide(grad_ref, None, group)
    query_t, grad_t = query_w.T, grad_w.T
    lse = lse_ref[0]
    delta = jnp.sum(grad_w.astype(jnp.float32)*flat_ref[0], axis=0, keepdims=True)
    dq_sc[...] = jnp.zeros_like(dq_sc)

    def step(j, carry):
        here = pl.ds(pl.multiple_of(j*BLOCK, BLOCK), BLOCK)
        scores = jnp.dot(key_sc[here,:], query_w, preferred_element_type=jnp.float32)
        probs = jnp.exp(scores - lse)
        dprobs = jnp.dot(val_sc[here,:], grad_w, preferred_element_type=jnp.float32)
        dv_sc[here,:] += jnp.dot(probs.astype(jnp.bfloat16), grad_t, preferred_element_type=jnp.float32)
        dscores = (probs*(dprobs-delta)).astype(jnp.bfloat16)
        dk_sc[here,:] += jnp.dot(dscores, query_t, preferred_element_type=jnp.float32)
        dq_sc[...] += jnp.dot(keyt_sc[:,here], dscores, preferred_element_type=jnp.float32)
        return carry

    lax.fori_loop(0, i+1, step, 0)
    cosine, sine = cos_ref[:, rows], sin_ref[:, rows]
    pieces = [unrotate(dq_sc[:, h*BLOCK:(h+1)*BLOCK]*scale, cosine, sine).astype(jnp.bfloat16) for h in range(group)]
    for k in range(2):
        columns = slice(k * LANES, (k + 1) * LANES)
        out_ref[2 * i + k, :lanes] = jnp.concatenate([p[:, columns] for p in pieces], axis=0)

    @pl.when(i == steps-1)
    def _():
        def finish(j, carry):
            here = pl.ds(pl.multiple_of(j*BLOCK, BLOCK), BLOCK)
            turned = unrotate(dk_sc[here,:].T, cos_ref[:,here], sin_ref[:,here]).astype(jnp.bfloat16)
            both = jnp.concatenate([turned, dv_sc[here,:].astype(jnp.bfloat16).T], axis=0)
            for k in range(2):
                out_ref[2 * j + k, lanes:] = both[:, k * LANES : (k + 1) * LANES]
            return carry

        lax.fori_loop(0, steps, finish, 0)


def attend_backward(qkv, grad, flat, lse, cosine, sine, group):
    count = qkv.shape[0]; total = count*LANES; steps = total//BLOCK; lanes = group*HDIM; width = group*BLOCK
    return pl.pallas_call(
        functools.partial(backward_kernel, group, steps),
        grid=(steps,),
        in_specs=[pl.BlockSpec((count, lanes+2*HDIM, LANES), lambda i: (0,0,0)),
                  pl.BlockSpec((2, lanes, LANES), lambda i: (i,0,0)),
                  pl.BlockSpec((1, HDIM, width), lambda i: (i,0,0)),
                  pl.BlockSpec((1,1,width), lambda i: (i,0,0)),
                  pl.BlockSpec((HDIM//2, total), lambda i: (0,0)),
                  pl.BlockSpec((HDIM//2, total), lambda i: (0,0))],
        out_specs=pl.BlockSpec((count, lanes+2*HDIM, LANES), lambda i: (0,0,0)),
        out_shape=jax.ShapeDtypeStruct((count, lanes+2*HDIM, LANES), jnp.bfloat16),
        scratch_shapes=[pltpu.VMEM((total,HDIM), jnp.bfloat16), pltpu.VMEM((HDIM,total), jnp.bfloat16), pltpu.VMEM((total,HDIM), jnp.bfloat16),
                        pltpu.VMEM((HDIM,width), jnp.float32), pltpu.VMEM((total,HDIM), jnp.float32), pltpu.VMEM((total,HDIM), jnp.float32)],
        compiler_params=pltpu.CompilerParams(dimension_semantics=ORDERED),
        name="backward",
    )(qkv, grad, flat, lse, cosine, sine)


def expert_kernel(
    parts, rows, width, experts, steps, chained, index_ref, *refs
):
    blocks = refs[:parts]
    grads = refs[parts : 2 * parts]
    router_ref, lin_ref, down_ref = refs[2 * parts : 2 * parts + 3]
    refs = refs[2 * parts + 3 + (4 if chained else 0) :]
    mixed_refs, back_refs, refs = refs[:parts], refs[parts : 2 * parts], refs[2 * parts :]
    rows_ref, grads_ref, d_lin_ref, hidden_ref = refs[:4]
    gates_sc, d_gates_sc, mixed_sc, back_sc = refs[4:]
    part = rows // parts
    units = down_ref.shape[1]
    step = pl.program_id(0)
    lane = lax.broadcasted_iota(jnp.int32, (rows, LANES), 1)

    @pl.when(step == 0)
    def _():
        for k in range(parts):
            here = pl.ds(k * part, part)
            rows_ref[here, :] = blocks[k][...]
            grads_ref[here, :] = grads[k][:, :width]
            logits = jnp.dot(blocks[k][...], router_ref[...], preferred_element_type=jnp.float32)
            logits = jnp.where(grads[k][:, width:].astype(jnp.float32) > 0.5, logits, -1e30)
            weight = jnp.exp(logits - jnp.max(logits, axis=1, keepdims=True))
            gates_sc[here, :] = weight / jnp.sum(weight, axis=1, keepdims=True)
        d_gates_sc[...] = jnp.zeros_like(d_gates_sc)

    expert = index_ref[step]
    own = lane == expert
    gate = jnp.sum(jnp.where(own, gates_sc[...], 0.0), axis=1, keepdims=True)
    block = rows_ref[...]
    lin = jnp.dot(block, lin_ref[0], preferred_element_type=jnp.float32)
    gate_lin, up_lin = lin[:, :units], lin[:, units:]
    d_hidden = matmul_nt(grads_ref[...], down_ref[0])
    sigma = 1.0 / (1.0 + jnp.exp(-gate_lin))
    active = gate_lin * sigma
    hidden = active * up_lin
    d_gates_sc[...] += jnp.where(own, jnp.sum(hidden * d_hidden, axis=1, keepdims=True), 0.0)
    hidden = (gate * hidden).astype(jnp.bfloat16)
    d_hidden = gate * d_hidden
    slope = sigma + active - active * sigma
    d_gate = (d_hidden * up_lin * slope).astype(jnp.bfloat16)
    d_up = (d_hidden * active).astype(jnp.bfloat16)
    hidden_ref[...] = hidden
    d_lin = jnp.concatenate([d_gate, d_up], axis=1)
    d_lin_ref[...] = d_lin
    mixed = jnp.dot(hidden, down_ref[0], preferred_element_type=jnp.float32)
    back = matmul_nt(d_lin, lin_ref[0])

    @pl.when(step == 0)
    def _():
        mixed_sc[...] = mixed
        back_sc[...] = back

    @pl.when(step > 0)
    def _():
        mixed_sc[...] += mixed
        back_sc[...] += back

    @pl.when(step == steps - 1)
    def _():
        d_gates = d_gates_sc[...]
        high = d_gates.astype(jnp.bfloat16).astype(jnp.float32)
        low = pltpu.roll(d_gates - high, experts, 1)
        d_gates = jnp.where(lane < experts, high, low).astype(jnp.bfloat16)
        for k in range(parts):
            here = slice(k * part, (k + 1) * part)
            mixed_refs[k][...] = mixed_sc[here, :].astype(jnp.bfloat16)
            back_refs[k][:, :width] = back_sc[here, :].astype(jnp.bfloat16)
            back_refs[k][:, width:] = d_gates[here]


def expert_rows(index, experts, blocks, grads, router, lin, down, slot, total, buffers):
    parts = len(blocks)
    part, width = blocks[0].shape
    rows = parts * part
    units = down.shape[1]
    steps = 2
    whole = lambda *shape: pl.BlockSpec(shape, lambda i, ids: (0,) * len(shape))
    columns = lambda count: pl.BlockSpec((rows, count), lambda i, ids: (slot, i))
    kept = pl.BlockSpec((rows, width), lambda i, ids: (slot, 0))
    chained = buffers is not None
    shapes = [
        *[jax.ShapeDtypeStruct((part, width), jnp.bfloat16)] * parts,
        *[jax.ShapeDtypeStruct((part, width + LANES), jnp.bfloat16)] * parts,
        jax.ShapeDtypeStruct((total, width), jnp.bfloat16),
        jax.ShapeDtypeStruct((total, width), jnp.bfloat16),
        jax.ShapeDtypeStruct((total, 4 * units), jnp.bfloat16),
        jax.ShapeDtypeStruct((total, 2 * units), jnp.bfloat16),
    ]
    inputs = [index, *blocks, *grads, router, lin, down] + (list(buffers) if chained else [])
    first = 1 + 2 * parts + 3
    results = pl.pallas_call(
        functools.partial(expert_kernel, parts, rows, width, experts, steps, chained),
        grid_spec=pltpu.PrefetchScalarGridSpec(
            num_scalar_prefetch=1,
            grid=(steps,),
            in_specs=[whole(part, width)] * parts
            + [whole(part, width + LANES)] * parts
            + [
                whole(width, LANES),
                pl.BlockSpec((1, width, 2 * units), lambda i, ids: (i, 0, 0)),
                pl.BlockSpec((1, units, width), lambda i, ids: (i, 0, 0)),
            ]
            + ([pl.BlockSpec(memory_space=pl.ANY)] * 4 if chained else []),
            out_specs=[
                *[whole(part, width)] * parts,
                *[whole(part, width + LANES)] * parts,
                kept,
                kept,
                columns(2 * units),
                columns(units),
            ],
            scratch_shapes=[
                pltpu.VMEM((rows, LANES), jnp.float32),
                pltpu.VMEM((rows, LANES), jnp.float32),
                pltpu.VMEM((rows, width), jnp.float32),
                pltpu.VMEM((rows, width), jnp.float32),
            ],
        ),
        out_shape=shapes,
        input_output_aliases={first + k: 2 * parts + k for k in range(4)} if chained else {},
        compiler_params=pltpu.CompilerParams(dimension_semantics=ORDERED),
        cost_estimate=pl.CostEstimate(
            flops=rows * width * units * 24,
            bytes_accessed=12 * width * units + 20 * rows * width,
            transcendentals=rows * units * 2,
        ),
        name="expert_rows",
    )(*inputs)
    return results[:parts], results[parts : 2 * parts], results[2 * parts :]


def contract(equation, left, right):
    return jnp.einsum(equation, left, right, preferred_element_type=jnp.float32)


def exchange(values):
    return lax.all_to_all(values, BLK, split_axis=0, concat_axis=0, tiled=True)


def from_heads(values):
    heads = lax.axis_size(HEAD)
    return [
        lax.ppermute(values, HEAD, [(k, (k + turn) % heads) for k in range(heads)])
        for turn in range(1, heads)
    ]


def partner(values):
    count = lax.axis_size(BLK)
    return lax.ppermute(values, BLK, [(k, k ^ 1) for k in range(count)])


def after(values, *earlier):
    return lax.optimization_barrier((values, earlier))[0]


def ring_order():
    half = lax.axis_size(BLK) // 4
    return [2 * k for k in range(half)] + [2 * k + 1 for k in reversed(range(half))]


def ring_steps():
    order = ring_order()
    onward, back = [], []
    for place, chip in enumerate(order):
        following = order[(place + 1) % len(order)]
        for core in range(2):
            onward.append((2 * chip + core, 2 * following + core))
            back.append((2 * following + core, 2 * chip + core))
    send_on = lambda values: lax.ppermute(values, BLK, onward)
    send_back = lambda values: lax.ppermute(values, BLK, back)
    return len(order), send_on, send_back


def ring_gather(values, axis=0):
    length, send_on, send_back = ring_steps()
    half = values.shape[axis] // 256 * 128
    behind = ahead = values
    pairs = []
    for _ in range(length // 2 - 1):
        behind, ahead = send_on(behind), send_back(ahead)
        pairs.append((behind, ahead))
    behind = lax.slice_in_dim(behind, 0, half, axis=axis)
    ahead = lax.slice_in_dim(ahead, half, ahead.shape[axis], axis=axis)
    return pairs, (send_on(behind), send_back(ahead))


class RingSum:
    def __init__(self, own, pairs, opposite, label, axis=0):
        _, self.send_on, self.send_back = ring_steps()
        self.own, self.pairs, self.label = own, list(reversed(pairs)), label
        self.onward, self.back = opposite
        self.axis = axis
        self.hop = 0

    def send(self, *hold):
        if self.hop > 0:
            behind, ahead = self.pairs[self.hop - 1]
            self.onward, self.back = self.onward + ahead, self.back + behind
        if hold:
            self.onward, self.back = after((self.onward, self.back), hold)
        self.onward, self.back = self.send_on(self.onward), self.send_back(self.back)
        return self

    def land(self, *filler):
        if filler:
            self.onward, self.back = after((self.onward, self.back), filler)
        if self.hop == 0:
            lengths = self.onward.shape[self.axis], self.back.shape[self.axis]
            spread = [(0, 0), (0, 0)]
            spread[self.axis] = (0, lengths[1])
            self.onward = jnp.pad(self.onward, spread)
            spread[self.axis] = (lengths[0], 0)
            self.back = jnp.pad(self.back, spread)
        self.hop += 1
        return self

    def total(self):
        while self.hop <= len(self.pairs):
            self.send().land()
        wide = self.own.astype(jnp.float32)
        return wide + self.onward.astype(jnp.float32) + self.back.astype(jnp.float32)


def ring_chip(offset):
    chips = lax.axis_size(BLK) // 2
    chip = lax.axis_index(BLK) // 2
    place = jnp.where(chip % 2 == 0, chip // 2, chips - 1 - chip // 2)
    target = (place + offset) % chips
    return jnp.where(target < chips // 2, 2 * target, 2 * (chips - 1 - target) + 1)


def all_heads(values):
    heads = lax.axis_size(HEAD)
    head = lax.axis_index(HEAD)
    place = lambda found, at: lax.dynamic_update_index_in_dim(result, found, at, 0)
    result = jnp.zeros((heads, *values.shape), values.dtype)
    result = place(values, head)
    for turn in range(1, heads):
        other = lax.ppermute(
            values, HEAD, [(k, (k + turn) % heads) for k in range(heads)]
        )
        result = place(other, (head - turn) % heads)
    return result


def ring_pieces(block, axis):
    pairs, opposite = ring_gather(block, axis)
    found = [(0, block)]
    for k, (behind, ahead) in enumerate(pairs):
        found += [(-k - 1, behind), (k + 1, ahead)]
    return found + [(len(pairs) + 1, jnp.concatenate(opposite, axis=axis))]


def dense_gather(shard):
    chips = lax.axis_size(BLK) // 2
    heads = lax.axis_size(HEAD)
    core = lax.axis_index(BLK) % 2
    rows, columns = shard.shape
    block = all_heads(shard).reshape(heads * rows, columns)
    full = jnp.zeros((heads, chips, 2, rows, columns), shard.dtype)
    for offset, piece in ring_pieces(block, 1):
        for side, part in ((core, piece), (1 - core, partner(piece))):
            full = lax.dynamic_update_slice(
                full, part.reshape(heads, 1, 1, rows, columns), (0, ring_chip(offset), side, 0, 0)
            )
    return full.reshape(-1, columns)


def dense_gather_late(shard):
    chips = lax.axis_size(BLK) // 2
    rows, columns = shard.shape
    found = jnp.zeros((chips, rows, columns), shard.dtype)
    for offset, piece in ring_pieces(shard, 1):
        found = lax.dynamic_update_slice(found, piece[None], (ring_chip(offset), 0, 0))
    found = all_heads(found)
    other = partner(found)
    even = lax.axis_index(BLK) % 2 == 0
    pair = [jnp.where(even, found, other), jnp.where(even, other, found)]
    return jnp.stack(pair, axis=2).reshape(-1, columns)


def head_share(values):
    heads, rows = lax.axis_size(HEAD), values.shape[0] // lax.axis_size(HEAD)
    head = lax.axis_index(HEAD)
    start = (0,) * (values.ndim - 1)
    share = lambda turn: lax.dynamic_slice(
        values, ((head + turn) % heads * rows, *start), (rows, *values.shape[1:])
    )
    result = share(0).astype(jnp.float32)
    for turn in range(1, heads):
        moved = [(k, (k + turn) % heads) for k in range(heads)]
        other = lax.ppermute(share(turn), HEAD, moved)
        result = result + other.astype(jnp.float32)
    return result


class DenseSum:
    def __init__(self, values, label, heads_first=False, staged=False):
        self.staged = staged
        self.heads = lax.axis_size(HEAD)
        self.chips = lax.axis_size(BLK) // 2
        self.rows = values.shape[0] // (2 * self.heads * self.chips)
        self.label, self.heads_first = label, heads_first
        self.index = lax.axis_index(BLK)
        self.mine = self.core_sum(values)

    def core_sum(self, values):
        grid = values.reshape(self.heads, self.chips, 2, self.rows, values.shape[1])
        even = self.index % 2 == 0
        swapped = partner(jnp.where(even, grid[:, :, 1], grid[:, :, 0]))
        return jnp.where(even, grid[:, :, 0], grid[:, :, 1]) + swapped

    def append(self, values):
        self.mine = jnp.concatenate([self.mine, self.core_sum(values)], axis=3)

    def block(self, offset):
        chip = ring_chip(offset)
        heads, columns = self.mine.shape[0], self.mine.shape[3]
        piece = lax.dynamic_slice(self.mine, (0, chip, 0, 0), (heads, 1, self.rows, columns))
        return piece.reshape(heads * self.rows, columns)

    def blocks(self, offsets):
        if not self.heads_first:
            return [self.block(offset) for offset in offsets]
        columns = self.mine.shape[3]
        taken = [
            lax.dynamic_slice(
                self.mine, (0, ring_chip(offset), 0, 0), (self.heads, 1, self.rows, columns)
            )
            for offset in offsets
        ]
        total = head_share(jnp.concatenate(taken, axis=1))
        return [total[0, k].astype(jnp.bfloat16) for k in range(len(offsets))]

    def ring(self):
        far = self.chips // 2
        if self.staged:
            stages = [[far, 1 - far, far - 1]]
            stages += [[-k, k] for k in reversed(range(1, far - 1))] + [[0]]
        else:
            stages = [list(range(1 - far, far + 1))]
        found = {}
        for offsets in stages:
            found.update(zip(offsets, self.blocks(offsets)))
        pairs = [(found[-k], found[k]) for k in range(1, far)]
        opposite = found[far]
        axis = 1 if self.heads_first else 0
        half = opposite.shape[1] // 256 * 128 if axis else opposite.shape[0] // 2
        opposite = jnp.split(opposite, [half], axis=axis)
        return RingSum(found[0], pairs, opposite, self.label, axis)

    def finish(self, total):
        return total if self.heads_first else head_share(total.astype(jnp.bfloat16))

    def total(self):
        return self.finish(self.ring().total())


def project_kernel(shard, groups, rows_ref, weight_ref, cosine_ref, sine_ref, out_ref):
    values = jnp.dot(rows_ref[...], weight_ref[...], preferred_element_type=jnp.float32)
    width = values.shape[1]
    lane = lax.broadcasted_iota(jnp.int32, (shard, width), 1)
    first = lane % HDIM < HDIM // 2
    span = width // groups
    for s in range(values.shape[0] // shard):
        part = values[s * shard : (s + 1) * shard]
        turned = jnp.where(
            first, pltpu.roll(part, width - HDIM // 2, 1), pltpu.roll(part, HDIM // 2, 1)
        )
        part = (part * cosine_ref[...] + turned * sine_ref[...]).astype(jnp.bfloat16)
        for k in range(groups):
            out_ref[s, k] = part[:, k * span : (k + 1) * span].T


def project(normed, weights, positions, groups, group):
    rows, width = normed.shape
    shard = positions.shape[0]
    span = (group + 2) * HDIM
    cosine, sine = rope_tables(positions, HDIM // 2)
    cosine = jnp.concatenate([cosine, cosine], axis=1)
    sine = jnp.concatenate([-sine, sine], axis=1)
    plain = (jnp.ones((shard, HDIM), jnp.float32), jnp.zeros((shard, HDIM), jnp.float32))
    cosine = jnp.concatenate(([cosine] * (group + 1) + [plain[0]]) * 2, axis=1)
    sine = jnp.concatenate(([sine] * (group + 1) + [plain[1]]) * 2, axis=1)
    table = pl.BlockSpec((shard, 2 * span), lambda j: (0, 0))
    return pl.pallas_call(
        functools.partial(project_kernel, shard, 2),
        grid=(groups // 2,),
        in_specs=[
            pl.BlockSpec((rows, width), lambda j: (0, 0)),
            pl.BlockSpec((width, 2 * span), lambda j: (0, j)),
            table,
            table,
        ],
        out_specs=pl.BlockSpec((rows // shard, 2, span, shard), lambda j: (0, j, 0, 0)),
        out_shape=jax.ShapeDtypeStruct((rows // shard, groups, span, shard), jnp.bfloat16),
        compiler_params=pltpu.CompilerParams(dimension_semantics=ORDERED),
        cost_estimate=pl.CostEstimate(
            flops=2 * rows * width * groups * span,
            bytes_accessed=2 * width * groups * span,
            transcendentals=0,
        ),
        name="project",
    )(normed, weights, cosine, sine)


def with_lanes(values, extra):
    rows = values.shape[0]
    spare = jnp.zeros((rows, LANES - extra.shape[1]), values.dtype)
    return jnp.concatenate([values, extra.astype(values.dtype), spare], axis=1)


def add_lanes(padded, extra):
    _, columns = padded.shape
    spread = ((0, 0), (columns - LANES, LANES - extra.shape[1]))
    return padded + jnp.pad(extra, spread)


def layer(
    tokens,
    gain_attn,
    w_query,
    w_key,
    w_value,
    w_out,
    gain_moe,
    w_router,
    w_gate,
    w_up,
    w_down,
    routes,
    grad_out,
):
    seq_local, shard, width = tokens.shape
    token_rows = seq_local * shard
    blk_index = lax.axis_index(BLK)
    blk_count = lax.axis_size(BLK)
    seq_total = blk_count * shard
    part_rows = w_query.shape[0]
    groups = w_key.shape[1] // HDIM
    group = w_query.shape[1] // w_key.shape[1]
    lanes = group * HDIM
    span = lanes + 2 * HDIM
    pairs = seq_local * groups
    copies = blk_count // pairs
    experts = w_router.shape[1]
    units = w_gate.shape[2]

    mixed_weights = jnp.concatenate(
        [
            w_query.reshape(part_rows, groups, lanes),
            w_key.reshape(part_rows, groups, HDIM),
            w_value.reshape(part_rows, groups, HDIM),
        ],
        axis=2,
    ).reshape(part_rows, groups * span)
    full_mixed = dense_gather(with_lanes(mixed_weights, gain_attn[:, None]))
    full_out = dense_gather_late(
        with_lanes(w_out, jnp.concatenate([w_router, gain_moe[:, None]], axis=1))
    )
    router = full_out[:, width:]
    full_router = router[:, :experts]
    router = jnp.where(jnp.arange(LANES)[None, :] < experts, router, jnp.bfloat16(0.0))
    gain_first = full_mixed[:, groups * span].astype(jnp.float32)
    gain_second = full_out[:, width + experts].astype(jnp.float32)

    expert_ids = jnp.arange(experts, dtype=jnp.int32)
    routes_tok = routes.reshape(token_rows, TOP)
    chosen = jnp.any(routes_tok[:, :, None] == expert_ids[None, None, :], axis=1)
    d_out = grad_out.reshape(token_rows, width)
    grads_own = with_lanes(d_out.astype(jnp.bfloat16), chosen)
    grads_pairs, grads_opposite = ring_gather(grads_own)
    w_lin = jnp.concatenate([w_gate, w_up], axis=2)
    other_lin, other_down = partner(w_lin), partner(w_down)
    both_lin = jnp.concatenate([w_lin, other_lin], axis=0)
    both_down = jnp.concatenate([w_down, other_down], axis=0)

    residual = tokens.astype(jnp.float32).reshape(token_rows, width)
    inverse_one = rms_scale(residual)
    normed = (residual * inverse_one * gain_first).astype(jnp.bfloat16)
    positions = blk_index * shard + jnp.arange(shard, dtype=jnp.int32)
    packed = project(normed, full_mixed, positions, groups, group)

    def to_pairs(values, columns):
        values = values.reshape(pairs, 1, columns, shard)
        values = jnp.broadcast_to(values, (pairs, copies, columns, shard))
        return exchange(values.reshape(blk_count, columns, shard))

    def to_tokens(values, columns):
        values = exchange(values).reshape(pairs, copies, columns, shard)[:, 0]
        return values.reshape(seq_local, groups * columns, shard)

    pair_qkv = to_pairs(packed, span)
    pair_attended, flat, log_total = attend_forward(pair_qkv, group)
    attended = to_tokens(pair_attended, lanes)
    branch = contract("sqt,qd->std", attended, full_out)
    branch = branch.reshape(token_rows, -1)[:, :width]
    middle = residual + branch
    inverse_two = rms_scale(middle)
    normed_two = (middle * inverse_two * gain_second).astype(jnp.bfloat16)
    logits = matmul(normed_two, full_router)
    gates = jax.nn.softmax(jnp.where(chosen, logits, -jnp.inf), axis=-1)

    blocks_pairs, blocks_opposite = ring_gather(normed_two)
    total = blk_count // 2 * token_rows
    ids = jnp.stack([blk_index, blk_index ^ 1]).astype(jnp.int32)

    def apply_experts(blocks, grads, slot, buffers):
        return expert_rows(
            ids, experts, blocks, grads, router, both_lin, both_down, slot, total, buffers
        )

    ring_pairs = len(blocks_pairs)
    mixed_own, back_own, buffers = apply_experts(
        [normed_two], [grads_own], 2 * ring_pairs, None
    )
    mixed_pairs, back_pairs = [], []
    for k in range(ring_pairs):
        mixed, back, buffers = apply_experts(blocks_pairs[k], grads_pairs[k], k, buffers)
        mixed_pairs.append(mixed)
        back_pairs.append(back)
    mixed_opposite, back_opposite, buffers = apply_experts(
        blocks_opposite, grads_opposite, 2 * ring_pairs + 1, buffers
    )
    rows_all, grads_all, d_lin_all, hidden_all = buffers
    back_ring = RingSum(back_own[0], back_pairs, back_opposite, "back")
    lefts = [lambda half: rows_all, lambda half: hidden_all[:, half * units :][:, :units]]
    rights = [lambda half: d_lin_all[:, 2 * half * units :][:, : 2 * units], lambda half: grads_all]
    others, mine = [], []
    for left, right in zip(lefts, rights):
        others.append(partner(matmul_tn(left(1), right(1)).astype(jnp.bfloat16)))
    for k, (left, right) in enumerate(zip(lefts, rights)):
        total = matmul_tn(left(0), right(0)) + others[k].astype(jnp.float32)
        mine.append(total.astype(jnp.bfloat16))
    back_sum = back_ring.total()
    theirs = []
    for part in mine:
        theirs.append(from_heads(part))
    mixed_ring = RingSum(mixed_own[0], mixed_pairs, mixed_opposite, "mixed")
    (mixed_ring.onward, mixed_ring.back), back_sum = lax.optimization_barrier(
        ((mixed_ring.onward, mixed_ring.back), back_sum)
    )
    mixed_ring.send()

    d_gates = back_sum[:, width : width + experts] + back_sum[:, width + experts : width + 2 * experts]
    d_logits = gates * (d_gates - jnp.sum(gates * d_gates, axis=-1, keepdims=True))
    grad_router = jnp.dot(normed_two.astype(jnp.float32).T, d_logits, precision=highest)
    d_normed_two = back_sum[:, :width] + jnp.dot(
        d_logits, full_router.astype(jnp.float32).T, precision=highest
    )
    d_mid_norm, grad_gain_second = norm_back(middle, inverse_two, gain_second, d_normed_two)
    d_mid = d_out + d_mid_norm
    d_branch = jnp.pad(d_mid.astype(jnp.bfloat16), ((0, 0), (0, LANES)))
    d_branch = d_branch.reshape(seq_local, shard, -1)
    d_attended = contract("qd,std->sqt", full_out, d_branch).astype(jnp.bfloat16)
    early = add_lanes(
        contract("sqt,std->qd", attended, d_branch),
        jnp.concatenate([grad_router, grad_gain_second[:, None]], axis=1),
    ).astype(jnp.bfloat16)
    mixed_ring.land()
    d_attended, early, mixed_ring.onward, mixed_ring.back = lax.optimization_barrier(
        (d_attended, early, mixed_ring.onward, mixed_ring.back)
    )
    pair_grad = to_pairs(d_attended, lanes)
    pair_grad, mixed_ring.onward, mixed_ring.back = lax.optimization_barrier(
        (pair_grad, mixed_ring.onward, mixed_ring.back)
    )
    mixed_ring.send()
    pair_cosine, pair_sine = rope_tables(jnp.arange(seq_total, dtype=jnp.int32), HDIM // 2)
    pair_d = attend_backward(
        pair_qkv, pair_grad, flat, log_total, pair_cosine.T, pair_sine.T, group
    )
    early = DenseSum(early, "early", True).total()
    mixed_ring.land()
    d_linear = to_tokens(pair_d, span)
    d_linear, early = lax.optimization_barrier((d_linear, early))
    grad_mixed = contract(
        "stf,sct->fc", normed.reshape(seq_local, shard, width), d_linear
    ).astype(jnp.bfloat16)
    late = DenseSum(grad_mixed, "late", True, True)
    d_normed = contract(
        "sct,fc->stf", jnp.pad(d_linear, ((0, 0), (0, LANES), (0, 0))), full_mixed
    ).reshape(token_rows, width)
    d_tok_norm, grad_gain_first = norm_back(residual, inverse_one, gain_first, d_normed)
    grad_tokens = (d_mid + d_tok_norm).reshape(seq_local, shard, width)
    grad_gain_first, mixed_ring.onward, mixed_ring.back = lax.optimization_barrier(
        (grad_gain_first, mixed_ring.onward, mixed_ring.back)
    )
    mixed_ring.send().land()
    late.append(jnp.pad(grad_gain_first[:, None].astype(jnp.bfloat16), ((0, 0), (0, LANES - 1))))
    late_ring = late.ring()
    sums = [
        functools.reduce(jnp.add, [v.astype(jnp.float32) for v in others], part.astype(jnp.float32))
        for part, others in zip(mine, theirs)
    ]
    grad_gate_sum, grad_up_sum = sums[0][None, :, :units], sums[0][None, :, units:]
    grad_down_sum = sums[1][None]
    out = (middle + mixed_ring.total()).reshape(seq_local, shard, width)
    late = late.finish(late_ring.total())
    late_mixed = late[:, : groups * span].reshape(part_rows, groups, span)
    return (
        out,
        grad_tokens,
        late[:, groups * span],
        late_mixed[:, :, :lanes].reshape(part_rows, -1),
        late_mixed[:, :, lanes : lanes + HDIM].reshape(part_rows, -1),
        late_mixed[:, :, lanes + HDIM :].reshape(part_rows, -1),
        early[:, :width],
        early[:, width + experts],
        early[:, width : width + experts],
        grad_gate_sum,
        grad_up_sum,
        grad_down_sum,
    )


def solution(mesh):
    placed = (
        P(HEAD, BLK, None),
        P((HEAD, BLK)),
        P((HEAD, BLK), None),
        P((HEAD, BLK), None),
        P((HEAD, BLK), None),
        P((HEAD, BLK), None),
        P((HEAD, BLK)),
        P((HEAD, BLK), None),
        P(BLK, None, None),
        P(BLK, None, None),
        P(BLK, None, None),
        P(HEAD, BLK, None),
        P(HEAD, BLK, None),
    )
    return jax.shard_map(
        layer,
        mesh=mesh,
        in_specs=placed,
        out_specs=(
            P(HEAD, BLK, None),
            P(HEAD, BLK, None),
            P((HEAD, BLK)),
            P((HEAD, BLK), None),
            P((HEAD, BLK), None),
            P((HEAD, BLK), None),
            P((HEAD, BLK), None),
            P((HEAD, BLK)),
            P((HEAD, BLK), None),
            P(BLK, None, None),
            P(BLK, None, None),
            P(BLK, None, None),
        ),
        check_vma=False,
    )
```

```python
import functools

import jax
import jax.numpy as jnp
from jax import lax
from jax.experimental import pallas as pl
from jax.experimental.pallas import tpu as pltpu
from jax.sharding import PartitionSpec as P


HDIM = 64
TOP = 8
BLOCK = 256
LANES = 128
HEAD = "head"
BLK = "blk"
ORDERED = ("arbitrary",)

highest = lax.Precision.HIGHEST
theta_base = 10000.0
norm_eps = 1e-06


def rope_tables(positions, half_width):
    index_float = jnp.arange(half_width, dtype=jnp.float32)
    frequency = theta_base ** (-2.0 * index_float / (2 * half_width))
    angles = positions.astype(jnp.float32)[:, None] * frequency[None, :]
    return (jnp.cos(angles), jnp.sin(angles))


def rms_scale(values):
    return lax.rsqrt(jnp.mean(values * values, axis=-1, keepdims=True) + norm_eps)


def norm_back(values, inverse, gain, d_normed):
    unit_values = values * inverse
    scaled = d_normed * gain
    d_gain = jnp.sum(d_normed * unit_values, axis=0)
    d_values = inverse * (
        scaled - unit_values * jnp.mean(scaled * unit_values, axis=-1, keepdims=True)
    )
    return (d_values, d_gain)


def matmul(left, right):
    return jnp.dot(left, right, preferred_element_type=jnp.float32)


def matmul_nt(left, right):
    return lax.dot_general(left, right, (((1,), (1,)), ((), ())), preferred_element_type=jnp.float32)


def matmul_tn(left, right):
    return lax.dot_general(left, right, (((0,), (0,)), ((), ())), preferred_element_type=jnp.float32)


def wide(ref, i, group):
    blocks = [ref[2 * i], ref[2 * i + 1]] if i is not None else [ref[0], ref[1]]
    pieces = [b[h * HDIM : (h + 1) * HDIM] for h in range(group) for b in blocks]
    return jnp.concatenate(pieces, axis=1)


def narrow(values, group, k):
    starts = [h * BLOCK + k * LANES for h in range(group)]
    return jnp.concatenate([values[:, s : s + LANES] for s in starts], axis=0)


def spread(qkv_ref, start, row_ref, column_ref):
    def step(b, carry):
        here = pl.ds(pl.multiple_of(b * LANES, LANES), LANES)
        piece = qkv_ref[b, start : start + HDIM]
        if row_ref is not None:
            row_ref[here, :] = piece.T
        if column_ref is not None:
            column_ref[:, here] = piece
        return carry

    lax.fori_loop(0, qkv_ref.shape[0], step, 0)


def forward_kernel(group, qkv_ref, att_ref, flat_ref, lse_ref, key_sc, val_sc, acc_sc):
    i = pl.program_id(0)
    lanes = group*HDIM

    @pl.when(i == 0)
    def _():
        spread(qkv_ref, lanes, key_sc, None)
        spread(qkv_ref, lanes + HDIM, None, val_sc)

    query = wide(qkv_ref, i, group) * jnp.bfloat16(HDIM**-0.5)
    acc_sc[...] = jnp.zeros_like(acc_sc)

    def step(j, carry):
        top, total = carry
        here = pl.ds(pl.multiple_of(j*BLOCK, BLOCK), BLOCK)
        scores = jnp.dot(key_sc[here, :], query, preferred_element_type=jnp.float32)
        new_top = jnp.maximum(top, jnp.max(scores, axis=0, keepdims=True))
        probs = jnp.exp(scores - new_top)
        fade = jnp.exp(top - new_top)
        acc_sc[...] = acc_sc[...]*fade + jnp.dot(val_sc[:, here], probs.astype(jnp.bfloat16), preferred_element_type=jnp.float32)
        return new_top, total*fade + jnp.sum(probs, axis=0, keepdims=True)

    width = group*BLOCK
    top, total = lax.fori_loop(0, i+1, step, (jnp.full((1,width), -1e30, jnp.float32), jnp.zeros((1,width), jnp.float32)))
    result = acc_sc[...] / total
    flat_ref[0] = result
    for k in range(2):
        att_ref[k] = narrow(result, group, k).astype(jnp.bfloat16)
    lse_ref[0] = top + jnp.log(total)


def attend_forward(qkv, group):
    count = qkv.shape[0]; total = count*LANES; steps = total//BLOCK; lanes = group*HDIM; width = group*BLOCK
    return pl.pallas_call(
        functools.partial(forward_kernel, group),
        grid=(steps,),
        in_specs=[pl.BlockSpec((count, lanes+2*HDIM, LANES), lambda i: (0,0,0))],
        out_specs=[pl.BlockSpec((2, lanes, LANES), lambda i: (i,0,0)),
                   pl.BlockSpec((1, HDIM, width), lambda i: (i,0,0)),
                   pl.BlockSpec((1,1,width), lambda i: (i,0,0))],
        out_shape=[jax.ShapeDtypeStruct((count, lanes, LANES), jnp.bfloat16),
                   jax.ShapeDtypeStruct((steps,HDIM,width), jnp.float32),
                   jax.ShapeDtypeStruct((steps,1,width), jnp.float32)],
        scratch_shapes=[pltpu.VMEM((total,HDIM), jnp.bfloat16), pltpu.VMEM((HDIM,total), jnp.bfloat16), pltpu.VMEM((HDIM,width), jnp.float32)],
        compiler_params=pltpu.CompilerParams(dimension_semantics=ORDERED),
        name="forward",
    )(qkv)


def unrotate(values, cosine, sine):
    a, b = values[:HDIM//2], values[HDIM//2:]
    return jnp.concatenate([a*cosine + b*sine, b*cosine - a*sine], axis=0)


def backward_kernel(group, steps, qkv_ref, grad_ref, flat_ref, lse_ref, cos_ref, sin_ref, out_ref, key_sc, keyt_sc, val_sc, dq_sc, dk_sc, dv_sc):
    i = pl.program_id(0)
    lanes = group*HDIM
    scale = HDIM**-0.5

    @pl.when(i == 0)
    def _():
        spread(qkv_ref, lanes, key_sc, keyt_sc)
        spread(qkv_ref, lanes + HDIM, val_sc, None)
        dk_sc[...] = jnp.zeros_like(dk_sc)
        dv_sc[...] = jnp.zeros_like(dv_sc)

    rows = pl.ds(pl.multiple_of(i*BLOCK, BLOCK), BLOCK)
    query_w = wide(qkv_ref, i, group) * jnp.bfloat16(scale)
    grad_w = wide(grad_ref, None, group)
    query_t, grad_t = query_w.T, grad_w.T
    lse = lse_ref[0]
    delta = jnp.sum(grad_w.astype(jnp.float32)*flat_ref[0], axis=0, keepdims=True)
    dq_sc[...] = jnp.zeros_like(dq_sc)

    def step(j, carry):
        here = pl.ds(pl.multiple_of(j*BLOCK, BLOCK), BLOCK)
        scores = jnp.dot(key_sc[here,:], query_w, preferred_element_type=jnp.float32)
        probs = jnp.exp(scores - lse)
        dprobs = jnp.dot(val_sc[here,:], grad_w, preferred_element_type=jnp.float32)
        dv_sc[here,:] += jnp.dot(probs.astype(jnp.bfloat16), grad_t, preferred_element_type=jnp.float32)
        dscores = (probs*(dprobs-delta)).astype(jnp.bfloat16)
        dk_sc[here,:] += jnp.dot(dscores, query_t, preferred_element_type=jnp.float32)
        dq_sc[...] += jnp.dot(keyt_sc[:,here], dscores, preferred_element_type=jnp.float32)
        return carry

    lax.fori_loop(0, i+1, step, 0)
    cosine, sine = cos_ref[:, rows], sin_ref[:, rows]
    pieces = [unrotate(dq_sc[:, h*BLOCK:(h+1)*BLOCK]*scale, cosine, sine).astype(jnp.bfloat16) for h in range(group)]
    for k in range(2):
        columns = slice(k * LANES, (k + 1) * LANES)
        out_ref[2 * i + k, :lanes] = jnp.concatenate([p[:, columns] for p in pieces], axis=0)

    @pl.when(i == steps-1)
    def _():
        def finish(j, carry):
            here = pl.ds(pl.multiple_of(j*BLOCK, BLOCK), BLOCK)
            turned = unrotate(dk_sc[here,:].T, cos_ref[:,here], sin_ref[:,here]).astype(jnp.bfloat16)
            both = jnp.concatenate([turned, dv_sc[here,:].astype(jnp.bfloat16).T], axis=0)
            for k in range(2):
                out_ref[2 * j + k, lanes:] = both[:, k * LANES : (k + 1) * LANES]
            return carry

        lax.fori_loop(0, steps, finish, 0)


def attend_backward(qkv, grad, flat, lse, cosine, sine, group):
    count = qkv.shape[0]; total = count*LANES; steps = total//BLOCK; lanes = group*HDIM; width = group*BLOCK
    return pl.pallas_call(
        functools.partial(backward_kernel, group, steps),
        grid=(steps,),
        in_specs=[pl.BlockSpec((count, lanes+2*HDIM, LANES), lambda i: (0,0,0)),
                  pl.BlockSpec((2, lanes, LANES), lambda i: (i,0,0)),
                  pl.BlockSpec((1, HDIM, width), lambda i: (i,0,0)),
                  pl.BlockSpec((1,1,width), lambda i: (i,0,0)),
                  pl.BlockSpec((HDIM//2, total), lambda i: (0,0)),
                  pl.BlockSpec((HDIM//2, total), lambda i: (0,0))],
        out_specs=pl.BlockSpec((count, lanes+2*HDIM, LANES), lambda i: (0,0,0)),
        out_shape=jax.ShapeDtypeStruct((count, lanes+2*HDIM, LANES), jnp.bfloat16),
        scratch_shapes=[pltpu.VMEM((total,HDIM), jnp.bfloat16), pltpu.VMEM((HDIM,total), jnp.bfloat16), pltpu.VMEM((total,HDIM), jnp.bfloat16),
                        pltpu.VMEM((HDIM,width), jnp.float32), pltpu.VMEM((total,HDIM), jnp.float32), pltpu.VMEM((total,HDIM), jnp.float32)],
        compiler_params=pltpu.CompilerParams(dimension_semantics=ORDERED),
        name="backward",
    )(qkv, grad, flat, lse, cosine, sine)


def expert_kernel(
    parts, rows, width, experts, steps, chained, index_ref, *refs
):
    blocks = refs[:parts]
    grads = refs[parts : 2 * parts]
    router_ref, lin_ref, down_ref = refs[2 * parts : 2 * parts + 3]
    refs = refs[2 * parts + 3 + (4 if chained else 0) :]
    mixed_refs, back_refs, refs = refs[:parts], refs[parts : 2 * parts], refs[2 * parts :]
    rows_ref, grads_ref, d_lin_ref, hidden_ref = refs[:4]
    gates_sc, d_gates_sc, mixed_sc, back_sc = refs[4:]
    part = rows // parts
    units = down_ref.shape[1]
    step = pl.program_id(0)
    lane = lax.broadcasted_iota(jnp.int32, (rows, LANES), 1)

    @pl.when(step == 0)
    def _():
        for k in range(parts):
            here = pl.ds(k * part, part)
            rows_ref[here, :] = blocks[k][...]
            grads_ref[here, :] = grads[k][:, :width]
            logits = jnp.dot(blocks[k][...], router_ref[...], preferred_element_type=jnp.float32)
            logits = jnp.where(grads[k][:, width:].astype(jnp.float32) > 0.5, logits, -1e30)
            weight = jnp.exp(logits - jnp.max(logits, axis=1, keepdims=True))
            gates_sc[here, :] = weight / jnp.sum(weight, axis=1, keepdims=True)
        d_gates_sc[...] = jnp.zeros_like(d_gates_sc)

    expert = index_ref[step]
    own = lane == expert
    gate = jnp.sum(jnp.where(own, gates_sc[...], 0.0), axis=1, keepdims=True)
    block = rows_ref[...]
    lin = jnp.dot(block, lin_ref[0], preferred_element_type=jnp.float32)
    gate_lin, up_lin = lin[:, :units], lin[:, units:]
    d_hidden = matmul_nt(grads_ref[...], down_ref[0])
    sigma = 1.0 / (1.0 + jnp.exp(-gate_lin))
    active = gate_lin * sigma
    hidden = active * up_lin
    d_gates_sc[...] += jnp.where(own, jnp.sum(hidden * d_hidden, axis=1, keepdims=True), 0.0)
    hidden = (gate * hidden).astype(jnp.bfloat16)
    d_hidden = gate * d_hidden
    slope = sigma + active - active * sigma
    d_gate = (d_hidden * up_lin * slope).astype(jnp.bfloat16)
    d_up = (d_hidden * active).astype(jnp.bfloat16)
    hidden_ref[...] = hidden
    d_lin = jnp.concatenate([d_gate, d_up], axis=1)
    d_lin_ref[...] = d_lin
    mixed = jnp.dot(hidden, down_ref[0], preferred_element_type=jnp.float32)
    back = matmul_nt(d_lin, lin_ref[0])

    @pl.when(step == 0)
    def _():
        mixed_sc[...] = mixed
        back_sc[...] = back

    @pl.when(step > 0)
    def _():
        mixed_sc[...] += mixed
        back_sc[...] += back

    @pl.when(step == steps - 1)
    def _():
        d_gates = d_gates_sc[...]
        high = d_gates.astype(jnp.bfloat16).astype(jnp.float32)
        low = pltpu.roll(d_gates - high, experts, 1)
        d_gates = jnp.where(lane < experts, high, low).astype(jnp.bfloat16)
        for k in range(parts):
            here = slice(k * part, (k + 1) * part)
            mixed_refs[k][...] = mixed_sc[here, :].astype(jnp.bfloat16)
            back_refs[k][:, :width] = back_sc[here, :].astype(jnp.bfloat16)
            back_refs[k][:, width:] = d_gates[here]


def expert_rows(index, experts, blocks, grads, router, lin, down, slot, total, buffers):
    parts = len(blocks)
    part, width = blocks[0].shape
    rows = parts * part
    units = down.shape[1]
    steps = 2
    whole = lambda *shape: pl.BlockSpec(shape, lambda i, ids: (0,) * len(shape))
    columns = lambda count: pl.BlockSpec((rows, count), lambda i, ids: (slot, i))
    kept = pl.BlockSpec((rows, width), lambda i, ids: (slot, 0))
    chained = buffers is not None
    shapes = [
        *[jax.ShapeDtypeStruct((part, width), jnp.bfloat16)] * parts,
        *[jax.ShapeDtypeStruct((part, width + LANES), jnp.bfloat16)] * parts,
        jax.ShapeDtypeStruct((total, width), jnp.bfloat16),
        jax.ShapeDtypeStruct((total, width), jnp.bfloat16),
        jax.ShapeDtypeStruct((total, 4 * units), jnp.bfloat16),
        jax.ShapeDtypeStruct((total, 2 * units), jnp.bfloat16),
    ]
    inputs = [index, *blocks, *grads, router, lin, down] + (list(buffers) if chained else [])
    first = 1 + 2 * parts + 3
    results = pl.pallas_call(
        functools.partial(expert_kernel, parts, rows, width, experts, steps, chained),
        grid_spec=pltpu.PrefetchScalarGridSpec(
            num_scalar_prefetch=1,
            grid=(steps,),
            in_specs=[whole(part, width)] * parts
            + [whole(part, width + LANES)] * parts
            + [
                whole(width, LANES),
                pl.BlockSpec((1, width, 2 * units), lambda i, ids: (i, 0, 0)),
                pl.BlockSpec((1, units, width), lambda i, ids: (i, 0, 0)),
            ]
            + ([pl.BlockSpec(memory_space=pl.ANY)] * 4 if chained else []),
            out_specs=[
                *[whole(part, width)] * parts,
                *[whole(part, width + LANES)] * parts,
                kept,
                kept,
                columns(2 * units),
                columns(units),
            ],
            scratch_shapes=[
                pltpu.VMEM((rows, LANES), jnp.float32),
                pltpu.VMEM((rows, LANES), jnp.float32),
                pltpu.VMEM((rows, width), jnp.float32),
                pltpu.VMEM((rows, width), jnp.float32),
            ],
        ),
        out_shape=shapes,
        input_output_aliases={first + k: 2 * parts + k for k in range(4)} if chained else {},
        compiler_params=pltpu.CompilerParams(dimension_semantics=ORDERED),
        cost_estimate=pl.CostEstimate(
            flops=rows * width * units * 24,
            bytes_accessed=12 * width * units + 20 * rows * width,
            transcendentals=rows * units * 2,
        ),
        name="expert_rows",
    )(*inputs)
    return results[:parts], results[parts : 2 * parts], results[2 * parts :]


def contract(equation, left, right):
    return jnp.einsum(equation, left, right, preferred_element_type=jnp.float32)


def exchange(values):
    return lax.all_to_all(values, BLK, split_axis=0, concat_axis=0, tiled=True)


def from_heads(values):
    heads = lax.axis_size(HEAD)
    return [
        lax.ppermute(values, HEAD, [(k, (k + turn) % heads) for k in range(heads)])
        for turn in range(1, heads)
    ]


def partner(values):
    count = lax.axis_size(BLK)
    return lax.ppermute(values, BLK, [(k, k ^ 1) for k in range(count)])


def after(values, *earlier):
    return lax.optimization_barrier((values, earlier))[0]


def ring_order():
    half = lax.axis_size(BLK) // 4
    return [2 * k for k in range(half)] + [2 * k + 1 for k in reversed(range(half))]


def ring_steps():
    order = ring_order()
    onward, back = [], []
    for place, chip in enumerate(order):
        following = order[(place + 1) % len(order)]
        for core in range(2):
            onward.append((2 * chip + core, 2 * following + core))
            back.append((2 * following + core, 2 * chip + core))
    send_on = lambda values: lax.ppermute(values, BLK, onward)
    send_back = lambda values: lax.ppermute(values, BLK, back)
    return len(order), send_on, send_back


def ring_gather(values, axis=0):
    length, send_on, send_back = ring_steps()
    half = values.shape[axis] // 256 * 128
    behind = ahead = values
    pairs = []
    for _ in range(length // 2 - 1):
        behind, ahead = send_on(behind), send_back(ahead)
        pairs.append((behind, ahead))
    behind = lax.slice_in_dim(behind, 0, half, axis=axis)
    ahead = lax.slice_in_dim(ahead, half, ahead.shape[axis], axis=axis)
    return pairs, (send_on(behind), send_back(ahead))


class RingSum:
    def __init__(self, own, pairs, opposite, label, axis=0):
        _, self.send_on, self.send_back = ring_steps()
        self.own, self.pairs, self.label = own, list(reversed(pairs)), label
        self.onward, self.back = opposite
        self.axis = axis
        self.hop = 0

    def send(self, *hold):
        if self.hop > 0:
            behind, ahead = self.pairs[self.hop - 1]
            self.onward, self.back = self.onward + ahead, self.back + behind
        if hold:
            self.onward, self.back = after((self.onward, self.back), hold)
        self.onward, self.back = self.send_on(self.onward), self.send_back(self.back)
        return self

    def land(self, *filler):
        if filler:
            self.onward, self.back = after((self.onward, self.back), filler)
        if self.hop == 0:
            lengths = self.onward.shape[self.axis], self.back.shape[self.axis]
            spread = [(0, 0), (0, 0)]
            spread[self.axis] = (0, lengths[1])
            self.onward = jnp.pad(self.onward, spread)
            spread[self.axis] = (lengths[0], 0)
            self.back = jnp.pad(self.back, spread)
        self.hop += 1
        return self

    def total(self):
        while self.hop <= len(self.pairs):
            self.send().land()
        wide = self.own.astype(jnp.float32)
        return wide + self.onward.astype(jnp.float32) + self.back.astype(jnp.float32)


def ring_chip(offset):
    chips = lax.axis_size(BLK) // 2
    chip = lax.axis_index(BLK) // 2
    place = jnp.where(chip % 2 == 0, chip // 2, chips - 1 - chip // 2)
    target = (place + offset) % chips
    return jnp.where(target < chips // 2, 2 * target, 2 * (chips - 1 - target) + 1)


def all_heads(values):
    heads = lax.axis_size(HEAD)
    head = lax.axis_index(HEAD)
    place = lambda found, at: lax.dynamic_update_index_in_dim(result, found, at, 0)
    result = jnp.zeros((heads, *values.shape), values.dtype)
    result = place(values, head)
    for turn in range(1, heads):
        other = lax.ppermute(
            values, HEAD, [(k, (k + turn) % heads) for k in range(heads)]
        )
        result = place(other, (head - turn) % heads)
    return result


def ring_pieces(block, axis):
    pairs, opposite = ring_gather(block, axis)
    found = [(0, block)]
    for k, (behind, ahead) in enumerate(pairs):
        found += [(-k - 1, behind), (k + 1, ahead)]
    return found + [(len(pairs) + 1, jnp.concatenate(opposite, axis=axis))]


def dense_gather(shard):
    chips = lax.axis_size(BLK) // 2
    heads = lax.axis_size(HEAD)
    core = lax.axis_index(BLK) % 2
    rows, columns = shard.shape
    block = all_heads(shard).reshape(heads * rows, columns)
    full = jnp.zeros((heads, chips, 2, rows, columns), shard.dtype)
    for offset, piece in ring_pieces(block, 1):
        for side, part in ((core, piece), (1 - core, partner(piece))):
            full = lax.dynamic_update_slice(
                full, part.reshape(heads, 1, 1, rows, columns), (0, ring_chip(offset), side, 0, 0)
            )
    return full.reshape(-1, columns)


def dense_gather_late(shard):
    chips = lax.axis_size(BLK) // 2
    rows, columns = shard.shape
    found = jnp.zeros((chips, rows, columns), shard.dtype)
    for offset, piece in ring_pieces(shard, 1):
        found = lax.dynamic_update_slice(found, piece[None], (ring_chip(offset), 0, 0))
    found = all_heads(found)
    other = partner(found)
    even = lax.axis_index(BLK) % 2 == 0
    pair = [jnp.where(even, found, other), jnp.where(even, other, found)]
    return jnp.stack(pair, axis=2).reshape(-1, columns)


def head_share(values):
    heads, rows = lax.axis_size(HEAD), values.shape[0] // lax.axis_size(HEAD)
    head = lax.axis_index(HEAD)
    start = (0,) * (values.ndim - 1)
    share = lambda turn: lax.dynamic_slice(
        values, ((head + turn) % heads * rows, *start), (rows, *values.shape[1:])
    )
    result = share(0).astype(jnp.float32)
    for turn in range(1, heads):
        moved = [(k, (k + turn) % heads) for k in range(heads)]
        other = lax.ppermute(share(turn), HEAD, moved)
        result = result + other.astype(jnp.float32)
    return result


class DenseSum:
    def __init__(self, values, label, heads_first=False, staged=False):
        self.staged = staged
        self.heads = lax.axis_size(HEAD)
        self.chips = lax.axis_size(BLK) // 2
        self.rows = values.shape[0] // (2 * self.heads * self.chips)
        self.label, self.heads_first = label, heads_first
        self.index = lax.axis_index(BLK)
        self.mine = self.core_sum(values)

    def core_sum(self, values):
        grid = values.reshape(self.heads, self.chips, 2, self.rows, values.shape[1])
        even = self.index % 2 == 0
        swapped = partner(jnp.where(even, grid[:, :, 1], grid[:, :, 0]))
        return jnp.where(even, grid[:, :, 0], grid[:, :, 1]) + swapped

    def append(self, values):
        self.mine = jnp.concatenate([self.mine, self.core_sum(values)], axis=3)

    def block(self, offset):
        chip = ring_chip(offset)
        heads, columns = self.mine.shape[0], self.mine.shape[3]
        piece = lax.dynamic_slice(self.mine, (0, chip, 0, 0), (heads, 1, self.rows, columns))
        return piece.reshape(heads * self.rows, columns)

    def blocks(self, offsets):
        if not self.heads_first:
            return [self.block(offset) for offset in offsets]
        columns = self.mine.shape[3]
        taken = [
            lax.dynamic_slice(
                self.mine, (0, ring_chip(offset), 0, 0), (self.heads, 1, self.rows, columns)
            )
            for offset in offsets
        ]
        total = head_share(jnp.concatenate(taken, axis=1))
        return [total[0, k].astype(jnp.bfloat16) for k in range(len(offsets))]

    def ring(self):
        far = self.chips // 2
        if self.staged:
            stages = [[far, 1 - far, far - 1]]
            stages += [[-k, k] for k in reversed(range(1, far - 1))] + [[0]]
        else:
            stages = [list(range(1 - far, far + 1))]
        found = {}
        for offsets in stages:
            found.update(zip(offsets, self.blocks(offsets)))
        pairs = [(found[-k], found[k]) for k in range(1, far)]
        opposite = found[far]
        axis = 1 if self.heads_first else 0
        half = opposite.shape[1] // 256 * 128 if axis else opposite.shape[0] // 2
        opposite = jnp.split(opposite, [half], axis=axis)
        return RingSum(found[0], pairs, opposite, self.label, axis)

    def finish(self, total):
        return total if self.heads_first else head_share(total.astype(jnp.bfloat16))

    def total(self):
        return self.finish(self.ring().total())


def project_kernel(shard, groups, rows_ref, weight_ref, cosine_ref, sine_ref, out_ref):
    values = jnp.dot(rows_ref[...], weight_ref[...], preferred_element_type=jnp.float32)
    width = values.shape[1]
    lane = lax.broadcasted_iota(jnp.int32, (shard, width), 1)
    first = lane % HDIM < HDIM // 2
    span = width // groups
    for s in range(values.shape[0] // shard):
        part = values[s * shard : (s + 1) * shard]
        turned = jnp.where(
            first, pltpu.roll(part, width - HDIM // 2, 1), pltpu.roll(part, HDIM // 2, 1)
        )
        part = (part * cosine_ref[...] + turned * sine_ref[...]).astype(jnp.bfloat16)
        for k in range(groups):
            out_ref[s, k] = part[:, k * span : (k + 1) * span].T


def project(normed, weights, positions, groups, group):
    rows, width = normed.shape
    shard = positions.shape[0]
    span = (group + 2) * HDIM
    cosine, sine = rope_tables(positions, HDIM // 2)
    cosine = jnp.concatenate([cosine, cosine], axis=1)
    sine = jnp.concatenate([-sine, sine], axis=1)
    plain = (jnp.ones((shard, HDIM), jnp.float32), jnp.zeros((shard, HDIM), jnp.float32))
    cosine = jnp.concatenate(([cosine] * (group + 1) + [plain[0]]) * 2, axis=1)
    sine = jnp.concatenate(([sine] * (group + 1) + [plain[1]]) * 2, axis=1)
    table = pl.BlockSpec((shard, 2 * span), lambda j: (0, 0))
    return pl.pallas_call(
        functools.partial(project_kernel, shard, 2),
        grid=(groups // 2,),
        in_specs=[
            pl.BlockSpec((rows, width), lambda j: (0, 0)),
            pl.BlockSpec((width, 2 * span), lambda j: (0, j)),
            table,
            table,
        ],
        out_specs=pl.BlockSpec((rows // shard, 2, span, shard), lambda j: (0, j, 0, 0)),
        out_shape=jax.ShapeDtypeStruct((rows // shard, groups, span, shard), jnp.bfloat16),
        compiler_params=pltpu.CompilerParams(dimension_semantics=ORDERED),
        cost_estimate=pl.CostEstimate(
            flops=2 * rows * width * groups * span,
            bytes_accessed=2 * width * groups * span,
            transcendentals=0,
        ),
        name="project",
    )(normed, weights, cosine, sine)


def with_lanes(values, extra):
    rows = values.shape[0]
    spare = jnp.zeros((rows, LANES - extra.shape[1]), values.dtype)
    return jnp.concatenate([values, extra.astype(values.dtype), spare], axis=1)


def add_lanes(padded, extra):
    _, columns = padded.shape
    spread = ((0, 0), (columns - LANES, LANES - extra.shape[1]))
    return padded + jnp.pad(extra, spread)


def layer(
    tokens,
    gain_attn,
    w_query,
    w_key,
    w_value,
    w_out,
    gain_moe,
    w_router,
    w_gate,
    w_up,
    w_down,
    routes,
    grad_out,
):
    seq_local, shard, width = tokens.shape
    token_rows = seq_local * shard
    blk_index = lax.axis_index(BLK)
    blk_count = lax.axis_size(BLK)
    seq_total = blk_count * shard
    part_rows = w_query.shape[0]
    groups = w_key.shape[1] // HDIM
    group = w_query.shape[1] // w_key.shape[1]
    lanes = group * HDIM
    span = lanes + 2 * HDIM
    pairs = seq_local * groups
    copies = blk_count // pairs
    experts = w_router.shape[1]
    units = w_gate.shape[2]

    mixed_weights = jnp.concatenate(
        [
            w_query.reshape(part_rows, groups, lanes),
            w_key.reshape(part_rows, groups, HDIM),
            w_value.reshape(part_rows, groups, HDIM),
        ],
        axis=2,
    ).reshape(part_rows, groups * span)
    full_mixed = dense_gather(with_lanes(mixed_weights, gain_attn[:, None]))
    full_out = dense_gather_late(
        with_lanes(w_out, jnp.concatenate([w_router, gain_moe[:, None]], axis=1))
    )
    router = full_out[:, width:]
    full_router = router[:, :experts]
    router = jnp.where(jnp.arange(LANES)[None, :] < experts, router, jnp.bfloat16(0.0))
    gain_first = full_mixed[:, groups * span].astype(jnp.float32)
    gain_second = full_out[:, width + experts].astype(jnp.float32)

    expert_ids = jnp.arange(experts, dtype=jnp.int32)
    routes_tok = routes.reshape(token_rows, TOP)
    chosen = jnp.any(routes_tok[:, :, None] == expert_ids[None, None, :], axis=1)
    d_out = grad_out.reshape(token_rows, width)
    grads_own = with_lanes(d_out.astype(jnp.bfloat16), chosen)
    grads_pairs, grads_opposite = ring_gather(grads_own)
    w_lin = jnp.concatenate([w_gate, w_up], axis=2)
    other_lin, other_down = partner(w_lin), partner(w_down)
    both_lin = jnp.concatenate([w_lin, other_lin], axis=0)
    both_down = jnp.concatenate([w_down, other_down], axis=0)

    residual = tokens.astype(jnp.float32).reshape(token_rows, width)
    inverse_one = rms_scale(residual)
    normed = (residual * inverse_one * gain_first).astype(jnp.bfloat16)
    positions = blk_index * shard + jnp.arange(shard, dtype=jnp.int32)
    packed = project(normed, full_mixed, positions, groups, group)

    def to_pairs(values, columns):
        values = values.reshape(pairs, 1, columns, shard)
        values = jnp.broadcast_to(values, (pairs, copies, columns, shard))
        return exchange(values.reshape(blk_count, columns, shard))

    def to_tokens(values, columns):
        values = exchange(values).reshape(pairs, copies, columns, shard)[:, 0]
        return values.reshape(seq_local, groups * columns, shard)

    pair_qkv = to_pairs(packed, span)
    pair_attended, flat, log_total = attend_forward(pair_qkv, group)
    attended = to_tokens(pair_attended, lanes)
    branch = contract("sqt,qd->std", attended, full_out)
    branch = branch.reshape(token_rows, -1)[:, :width]
    middle = residual + branch
    inverse_two = rms_scale(middle)
    normed_two = (middle * inverse_two * gain_second).astype(jnp.bfloat16)
    logits = matmul(normed_two, full_router)
    gates = jax.nn.softmax(jnp.where(chosen, logits, -jnp.inf), axis=-1)

    blocks_pairs, blocks_opposite = ring_gather(normed_two)
    total = blk_count // 2 * token_rows
    ids = jnp.stack([blk_index, blk_index ^ 1]).astype(jnp.int32)

    def apply_experts(blocks, grads, slot, buffers):
        return expert_rows(
            ids, experts, blocks, grads, router, both_lin, both_down, slot, total, buffers
        )

    ring_pairs = len(blocks_pairs)
    mixed_own, back_own, buffers = apply_experts(
        [normed_two], [grads_own], 2 * ring_pairs, None
    )
    mixed_pairs, back_pairs = [], []
    for k in range(ring_pairs):
        mixed, back, buffers = apply_experts(blocks_pairs[k], grads_pairs[k], k, buffers)
        mixed_pairs.append(mixed)
        back_pairs.append(back)
    mixed_opposite, back_opposite, buffers = apply_experts(
        blocks_opposite, grads_opposite, 2 * ring_pairs + 1, buffers
    )
    rows_all, grads_all, d_lin_all, hidden_all = buffers
    back_ring = RingSum(back_own[0], back_pairs, back_opposite, "back")
    lefts = [lambda half: rows_all, lambda half: hidden_all[:, half * units :][:, :units]]
    rights = [lambda half: d_lin_all[:, 2 * half * units :][:, : 2 * units], lambda half: grads_all]
    others, mine = [], []
    for left, right in zip(lefts, rights):
        others.append(partner(matmul_tn(left(1), right(1)).astype(jnp.bfloat16)))
    for k, (left, right) in enumerate(zip(lefts, rights)):
        total = matmul_tn(left(0), right(0)) + others[k].astype(jnp.float32)
        mine.append(total.astype(jnp.bfloat16))
    back_sum = back_ring.total()
    theirs = []
    for part in mine:
        theirs.append(from_heads(part))
    mixed_ring = RingSum(mixed_own[0], mixed_pairs, mixed_opposite, "mixed")
    (mixed_ring.onward, mixed_ring.back), back_sum = lax.optimization_barrier(
        ((mixed_ring.onward, mixed_ring.back), back_sum)
    )
    mixed_ring.send()

    d_gates = back_sum[:, width : width + experts] + back_sum[:, width + experts : width + 2 * experts]
    d_logits = gates * (d_gates - jnp.sum(gates * d_gates, axis=-1, keepdims=True))
    grad_router = jnp.dot(normed_two.astype(jnp.float32).T, d_logits, precision=highest)
    d_normed_two = back_sum[:, :width] + jnp.dot(
        d_logits, full_router.astype(jnp.float32).T, precision=highest
    )
    d_mid_norm, grad_gain_second = norm_back(middle, inverse_two, gain_second, d_normed_two)
    d_mid = d_out + d_mid_norm
    d_branch = jnp.pad(d_mid.astype(jnp.bfloat16), ((0, 0), (0, LANES)))
    d_branch = d_branch.reshape(seq_local, shard, -1)
    d_attended = contract("qd,std->sqt", full_out, d_branch).astype(jnp.bfloat16)
    early = add_lanes(
        contract("sqt,std->qd", attended, d_branch),
        jnp.concatenate([grad_router, grad_gain_second[:, None]], axis=1),
    ).astype(jnp.bfloat16)
    mixed_ring.land()
    d_attended, mixed_ring.onward, mixed_ring.back = lax.optimization_barrier(
        (d_attended, mixed_ring.onward, mixed_ring.back)
    )
    pair_grad = to_pairs(d_attended, lanes)
    pair_grad, mixed_ring.onward, mixed_ring.back = lax.optimization_barrier(
        (pair_grad, mixed_ring.onward, mixed_ring.back)
    )
    mixed_ring.send()
    pair_cosine, pair_sine = rope_tables(jnp.arange(seq_total, dtype=jnp.int32), HDIM // 2)
    pair_d = attend_backward(
        pair_qkv, pair_grad, flat, log_total, pair_cosine.T, pair_sine.T, group
    )
    early = DenseSum(early, "early", True).total()
    mixed_ring.land()
    d_linear = to_tokens(pair_d, span)
    grad_mixed = contract(
        "stf,sct->fc", normed.reshape(seq_local, shard, width), d_linear
    ).astype(jnp.bfloat16)
    late = DenseSum(grad_mixed, "late", True, True)
    d_normed = contract(
        "sct,fc->stf", jnp.pad(d_linear, ((0, 0), (0, LANES), (0, 0))), full_mixed
    ).reshape(token_rows, width)
    d_tok_norm, grad_gain_first = norm_back(residual, inverse_one, gain_first, d_normed)
    grad_tokens = (d_mid + d_tok_norm).reshape(seq_local, shard, width)
    grad_gain_first, mixed_ring.onward, mixed_ring.back = lax.optimization_barrier(
        (grad_gain_first, mixed_ring.onward, mixed_ring.back)
    )
    late.append(jnp.pad(grad_gain_first[:, None].astype(jnp.bfloat16), ((0, 0), (0, LANES - 1))))
    late.mine, mixed_ring.onward, mixed_ring.back = lax.optimization_barrier(
        (late.mine, mixed_ring.onward, mixed_ring.back)
    )
    mixed_ring.send().land()
    late_ring = late.ring()
    sums = [
        functools.reduce(jnp.add, [v.astype(jnp.float32) for v in others], part.astype(jnp.float32))
        for part, others in zip(mine, theirs)
    ]
    grad_gate_sum, grad_up_sum = sums[0][None, :, :units], sums[0][None, :, units:]
    grad_down_sum = sums[1][None]
    out = (middle + mixed_ring.total()).reshape(seq_local, shard, width)
    late = late.finish(late_ring.total())
    late_mixed = late[:, : groups * span].reshape(part_rows, groups, span)
    return (
        out,
        grad_tokens,
        late[:, groups * span],
        late_mixed[:, :, :lanes].reshape(part_rows, -1),
        late_mixed[:, :, lanes : lanes + HDIM].reshape(part_rows, -1),
        late_mixed[:, :, lanes + HDIM :].reshape(part_rows, -1),
        early[:, :width],
        early[:, width + experts],
        early[:, width : width + experts],
        grad_gate_sum,
        grad_up_sum,
        grad_down_sum,
    )


def solution(mesh):
    placed = (
        P(HEAD, BLK, None),
        P((HEAD, BLK)),
        P((HEAD, BLK), None),
        P((HEAD, BLK), None),
        P((HEAD, BLK), None),
        P((HEAD, BLK), None),
        P((HEAD, BLK)),
        P((HEAD, BLK), None),
        P(BLK, None, None),
        P(BLK, None, None),
        P(BLK, None, None),
        P(HEAD, BLK, None),
        P(HEAD, BLK, None),
    )
    return jax.shard_map(
        layer,
        mesh=mesh,
        in_specs=placed,
        out_specs=(
            P(HEAD, BLK, None),
            P(HEAD, BLK, None),
            P((HEAD, BLK)),
            P((HEAD, BLK), None),
            P((HEAD, BLK), None),
            P((HEAD, BLK), None),
            P((HEAD, BLK), None),
            P((HEAD, BLK)),
            P((HEAD, BLK), None),
            P(BLK, None, None),
            P(BLK, None, None),
            P(BLK, None, None),
        ),
        check_vma=False,
    )
```
